32 devices in a mesh: rows: 16 (over z, y, x), cols: 2 (over core).
Axes of the slice: x: 2, y: 2, z: 4, core: 2. Of those that a mesh axis runs over, the one named last changes fastest.
Arguments:
- snapshots: bfloat16 [16384, 2, 2, 128], P('rows', 'cols'), may hold values from -12 to 12
- scales: float32 [32, 2, 2], P('rows'), may hold values from 0.2 to 9
Outputs:
- coefficients: float32 [128, 2, 2, 128], P(None, 'cols')
- updated: bfloat16 [16384, 2, 2, 128], P('rows', 'cols')
The draws below stay inside these ranges and needn't reach their ends.
All inputs are finite; a program needn't handle non-finite values.
Results may differ from the reference program's by a relative error of at most 0.012.
Values may be sent and summed in bfloat16 or wider, within the bound.
No kernel may reach another device: no remote copies, remote signals or barrier semaphores. Data moves between devices by JAX's collectives and lax.ppermute only.
A program may use at most 64 MiB of HBM per device.

```python
import math
import jax
import jax.numpy as jnp
from jax import lax

PANEL = 128
ROUNDS = 2
SB = 512
M_ROWS = 16384
GROUPS = 2
SBLOCKS = 32


def draw_snapshots(key, part):
    keys = jax.random.split(jax.random.fold_in(key, 7), 4)
    shape = (M_ROWS, GROUPS, ROUNDS, PANEL)
    base = jax.random.normal(keys[0], (M_ROWS, PANEL), jnp.float32)
    own = jax.random.normal(keys[1], shape, jnp.float32)
    weights = jax.random.uniform(keys[2], (2, PANEL), jnp.float32, -0.8, 0.8)
    mixed = base + weights[0] * jnp.roll(base, 1, axis=1) + weights[1] * jnp.roll(base, PANEL // 3 + 1, axis=1)
    gains = jax.random.uniform(keys[3], (GROUPS, ROUNDS, PANEL), jnp.float32, 0.5, 1.2)
    group_ids = jnp.arange(GROUPS, dtype=jnp.int32)[:, None, None]
    round_ids = jnp.arange(ROUNDS, dtype=jnp.int32)[None, :, None]
    chan_ids = jnp.arange(PANEL, dtype=jnp.int32)[None, None, :]
    source = (chan_ids + 17 * round_ids + 5 * group_ids) % PANEL
    trailing = gains * mixed[:, source] + 0.8 * own
    first = (group_ids == 0) & (round_ids == 0)
    result = jnp.where(first[None], mixed[:, None, None, :] + 0.3 * own, trailing)
    return jnp.clip(result, -12.0, 12.0).astype(jnp.bfloat16)


def draw_scales(key, part):
    keys = jax.random.split(jax.random.fold_in(key, 13), 1)
    rise = 3.0 ** (jnp.arange(SBLOCKS, dtype=jnp.float32) / (SBLOCKS - 1))
    spread = jnp.exp(jax.random.uniform(keys[0], (SBLOCKS, GROUPS, ROUNDS), jnp.float32, math.log(0.3), math.log(3.0)))
    return rise[:, None, None] * spread


def setup_inputs(seed: int = 0) -> dict:
    key_list = jax.random.split(jax.random.key(seed), 3)
    return {
        "snapshots": draw_snapshots(jax.random.fold_in(key_list[2], 71), 0),
        "scales": draw_scales(jax.random.fold_in(key_list[2], 71), 0),
    }


HIGH = lax.Precision.HIGHEST

def reference(snapshots, scales):
    columns = GROUPS * ROUNDS * PANEL
    blocks = snapshots.reshape(SBLOCKS, SB, GROUPS, ROUNDS, PANEL)

    def block_values(block, scale):
        return (block.astype(jnp.float32) * scale[None, :, :, None]).reshape(SB, columns)

    def gram_step(carry, pair):
        block_vals = block_values(pair[0], pair[1])
        panel = block_vals[:, :PANEL]
        return (carry + jnp.dot(panel.T.astype(jnp.float32), panel.astype(jnp.float32), precision=HIGH, preferred_element_type=jnp.float32), None)
    gram, _ = lax.scan(gram_step, jnp.zeros((PANEL, PANEL), jnp.float32), (blocks, scales))
    upper = jnp.linalg.cholesky(gram).T
    inverse = lax.linalg.triangular_solve(upper, jnp.eye(PANEL, dtype=jnp.float32), left_side=True, lower=False)

    def coef_step(carry, pair):
        block_vals = block_values(pair[0], pair[1])
        basis = jnp.dot(block_vals[:, :PANEL].astype(jnp.float32), inverse.astype(jnp.float32), precision=HIGH, preferred_element_type=jnp.float32)
        return (carry + jnp.dot(basis.T.astype(jnp.float32), block_vals.astype(jnp.float32), precision=HIGH, preferred_element_type=jnp.float32), None)
    raw, _ = lax.scan(coef_step, jnp.zeros((PANEL, columns), jnp.float32), (blocks, scales))
    root = math.sqrt(M_ROWS)

    def update_block(pair):
        block_vals = block_values(pair[0], pair[1])
        basis = jnp.dot(block_vals[:, :PANEL].astype(jnp.float32), inverse.astype(jnp.float32), precision=HIGH, preferred_element_type=jnp.float32)
        remainder = block_vals - jnp.dot(basis.astype(jnp.float32), raw.astype(jnp.float32), precision=HIGH, preferred_element_type=jnp.float32)
        whole = jnp.concatenate([root * basis, remainder[:, PANEL:]], axis=1)
        return whole.astype(jnp.bfloat16)
    updated = lax.map(update_block, (blocks, scales)).reshape(M_ROWS, GROUPS, ROUNDS, PANEL)
    coefficients = (raw / root).reshape(PANEL, GROUPS, ROUNDS, PANEL)
    return (coefficients, updated)
```

```python
import functools
import math

import jax
import jax.numpy as jnp
from jax import lax
from jax.experimental import pallas as pl
from jax.experimental.pallas import tpu as pltpu
from jax.sharding import PartitionSpec as P

F32 = jnp.float32
BF16 = jnp.bfloat16
HIGH = lax.Precision.HIGHEST
VMEM = pl.BlockSpec(memory_space=pltpu.VMEM)
SMEM = pl.BlockSpec(memory_space=pltpu.SMEM)


def partner(x, axis, count, offset):
    return lax.ppermute(x, axis, [(i, i ^ offset) for i in range(count)])


def total(x, axis, count):
    if count & (count - 1):
        return lax.psum(x, axis)
    stride = 1
    while stride < count:
        radix = 4 if (count // stride) % 4 == 0 else 2
        others = [partner(x, axis, count, b * stride) for b in range(1, radix)]
        for other in others:
            x = x + other
        stride *= radix
    return x


def from_leader(x, axis, count, mine):
    if count & (count - 1):
        return lax.psum(jnp.where(mine == 0, x, jnp.zeros_like(x)), axis)
    stride = 1
    while 2 * stride < count:
        x = jnp.where((mine & stride) != 0, partner(x, axis, count, stride), x)
        stride *= 2
    return x, partner(x, axis, count, stride), stride


def lanes(x, p):
    return jnp.broadcast_to(x[:, p : p + 1], x.shape)


def sublanes(x, j):
    return jnp.broadcast_to(x[j : j + 1, :], x.shape)


def lower_inverse(rows, width):
    n = len(rows)
    rid = lax.broadcasted_iota(jnp.int32, (8, width), 0)
    cid = lax.broadcasted_iota(jnp.int32, (8, width), 1)
    done = []
    for k in range(n):
        base = 8 * k
        held = rows[k]
        columns = [lanes(held, base + j) for j in range(8)]
        inside = (cid >= base) & (cid < base + 8)
        eye = jnp.where(cid - base == rid, 1.0, 0.0).astype(F32)
        full = jnp.where(inside, eye, held)
        forward = full
        root_scale = jnp.zeros((8, width), F32)
        scale = jnp.zeros((8, width), F32)
        for j in range(8):
            pivot = sublanes(columns[j], j)
            inverse = 1.0 / pivot
            root_scale = jnp.where(rid == j, lax.rsqrt(pivot), root_scale)
            scale = jnp.where(rid == j, inverse, scale)
            ratio = columns[j] * inverse
            ratio_all = jnp.where(rid == j, 0.0, ratio)
            ratio_below = jnp.where(rid > j, ratio, 0.0)
            for m in range(j + 1, 8):
                columns[m] = columns[m] - ratio_all * sublanes(columns[m], j)
            full = full - ratio_all * sublanes(full, j)
            forward = forward - ratio_below * sublanes(forward, j)
        done.append(jnp.where(cid <= rid + base, forward * root_scale, 0.0))
        full = full * scale
        if k + 1 < n:
            spread = [sublanes(full, j) for j in range(8)]
            for i in range(k + 1, n):
                terms = [lanes(rows[i], base + j) * spread[j] for j in range(8)]
                while len(terms) > 1:
                    terms = [terms[q] + terms[q + 1] for q in range(0, len(terms), 2)]
                rows[i] = jnp.where(inside, 0.0, rows[i]) - terms[0]
    return done


def leading(z_ref, recv_ref, stride):
    mine = lax.axis_index("cols")
    return jnp.where((mine & stride) == 0, z_ref[...], recv_ref[...])


def products_kernel(rounds, nblock, stride, scale_ref, z_ref, kept_ref, recv_ref, out_ref, own, lead):
    group = lax.axis_index("cols")
    width = z_ref.shape[1]
    points = z_ref.shape[0] // rounds // nblock
    own[...] = z_ref[...].astype(F32)
    lead[...] = leading(kept_ref, recv_ref, stride).astype(F32)
    out = jnp.zeros(out_ref.shape, F32)
    for b in range(nblock):
        start = b * points * rounds
        panel = lead[pl.ds(start, points, stride=rounds), :].astype(BF16)
        parts = [panel] + [own[pl.ds(start + r, points, stride=rounds), :].astype(BF16) for r in range(rounds)]
        block = lax.dot_general(
            panel, jnp.concatenate(parts, axis=1), (((0,), (0,)), ((), ())), preferred_element_type=F32
        )
        first = scale_ref[b, 0]
        pieces = [block[:, :width] * (first * first)]
        for r in range(rounds):
            factor = first * scale_ref[b, group * rounds + r]
            pieces.append(block[:, (r + 1) * width : (r + 2) * width] * factor)
        out = out + jnp.concatenate(pieces, axis=1)
    out_ref[...] = out


def spread_kernel(rounds, stride, kept_ref, recv_ref, out_ref):
    width = kept_ref.shape[1]
    rows = lax.broadcasted_iota(jnp.int32, kept_ref.shape, 0) % rounds
    lead = leading(kept_ref, recv_ref, stride).astype(F32)
    for r in range(rounds):
        moved = lead if r == 0 else pltpu.roll(lead, r, 0)
        out_ref[:, r * width : (r + 1) * width] = jnp.where(rows == r, moved, 0.0).astype(BF16)


def factor_kernel(rounds, root, sums_ref, coef_ref, weight_ref):
    group = lax.axis_index("cols")
    width = sums_ref.shape[0]
    rows = [sums_ref[8 * i : 8 * i + 8, :width] for i in range(width // 8)]
    inverse = jnp.concatenate(lower_inverse(rows, width), axis=0)
    across = inverse.T
    for r in range(rounds):
        cross = sums_ref[:, (r + 1) * width : (r + 2) * width]
        raw = jnp.dot(inverse, cross, precision=HIGH, preferred_element_type=F32)
        coef_ref[pl.ds(r, width, stride=rounds), :] = raw * (1.0 / root)
        weight = jnp.dot(across, raw, precision=HIGH, preferred_element_type=F32)
        if r == 0:
            weight = jnp.where(group == 0, -root * across, weight)
        upper = weight.astype(BF16)
        weight_ref[r * width : (r + 1) * width, :width] = upper
        weight_ref[r * width : (r + 1) * width, width:] = (weight - upper.astype(F32)).astype(BF16)


def update_kernel(rounds, nblock, scale_ref, z_ref, lead_ref, weight_ref, out_ref):
    group = lax.axis_index("cols")
    width = z_ref.shape[1]
    span = z_ref.shape[0] // nblock
    row = lax.broadcasted_iota(jnp.int32, (span, width), 0) % rounds
    for b in range(nblock):
        at = slice(b * span, (b + 1) * span)
        acc = jnp.dot(lead_ref[at, :], weight_ref[...], preferred_element_type=F32)
        acc = (acc[:, :width] + acc[:, width:]) * scale_ref[b, 0]
        factor = jnp.zeros((span, width), F32)
        for r in range(rounds):
            own = scale_ref[b, group * rounds + r]
            if r == 0:
                own = jnp.where(group == 0, 0.0, own)
            factor = jnp.where(row == r, own, factor)
        out_ref[at, :] = (z_ref[at, :].astype(F32) * factor - acc).astype(BF16)


def shards(snapshots, scales):
    points, _, rounds, width = snapshots.shape
    nblock = scales.shape[0]
    n_rows, n_cols = lax.axis_size("rows"), lax.axis_size("cols")
    root = math.sqrt(points * n_rows)
    long = points * rounds
    z = snapshots.reshape(long, width)
    flat = scales.reshape(nblock, -1)
    kept, recv, stride = from_leader(z, "cols", n_cols, lax.axis_index("cols"))
    params = pltpu.CompilerParams(vmem_limit_bytes=48 << 20)
    partial = pl.pallas_call(
        functools.partial(products_kernel, rounds, nblock, stride),
        out_shape=jax.ShapeDtypeStruct((width, (rounds + 1) * width), F32),
        in_specs=[SMEM, VMEM, VMEM, VMEM],
        out_specs=VMEM,
        scratch_shapes=[pltpu.VMEM((long, width), F32)] * 2,
        compiler_params=params,
        name="products",
    )(flat, z, kept, recv)
    lead = pl.pallas_call(
        functools.partial(spread_kernel, rounds, stride),
        out_shape=jax.ShapeDtypeStruct((long, rounds * width), BF16),
        in_specs=[VMEM, VMEM],
        out_specs=VMEM,
        compiler_params=params,
        name="spread",
    )(kept, recv)
    sums = total(partial, "rows", n_rows)
    coef, weight = pl.pallas_call(
        functools.partial(factor_kernel, rounds, root),
        out_shape=[
            jax.ShapeDtypeStruct((width * rounds, width), F32),
            jax.ShapeDtypeStruct((rounds * width, 2 * width), BF16),
        ],
        in_specs=[VMEM],
        out_specs=[VMEM, VMEM],
        compiler_params=params,
        name="factor",
    )(sums)
    updated = pl.pallas_call(
        functools.partial(update_kernel, rounds, nblock),
        out_shape=jax.ShapeDtypeStruct((long, width), BF16),
        in_specs=[SMEM, VMEM, VMEM, VMEM],
        out_specs=VMEM,
        compiler_params=params,
        name="update",
    )(flat, z, lead, weight)
    return coef.reshape(width, 1, rounds, width), updated.reshape(snapshots.shape)


def solution(mesh):
    return jax.shard_map(
        shards,
        mesh=mesh,
        in_specs=(P("rows", "cols", None, None), P("rows", None, None)),
        out_specs=(P(None, "cols", None, None), P("rows", "cols", None, None)),
        check_vma=False,
    )
```

```python
import functools
import math

import jax
import jax.numpy as jnp
from jax import lax
from jax.experimental import pallas as pl
from jax.experimental.pallas import tpu as pltpu
from jax.sharding import PartitionSpec as P

F32 = jnp.float32
BF16 = jnp.bfloat16
HIGH = lax.Precision.HIGHEST
VMEM = pl.BlockSpec(memory_space=pltpu.VMEM)
SMEM = pl.BlockSpec(memory_space=pltpu.SMEM)


def partner(x, axis, count, offset):
    return lax.ppermute(x, axis, [(i, i ^ offset) for i in range(count)])


def radices(count):
    found = []
    stride = 1
    while stride < count:
        radix = 4 if (count // stride) % 4 == 0 else 2
        found.append((stride, radix))
        stride *= radix
    return found


def from_leader(x, count, mine):
    stride = 1
    while 2 * stride < count:
        x = jnp.where((mine & stride) != 0, partner(x, "cols", count, stride), x)
        stride *= 2
    return x, partner(x, "cols", count, stride), stride


def lanes(x, p):
    return jnp.broadcast_to(x[:, p : p + 1], x.shape)


def sublanes(x, j):
    return jnp.broadcast_to(x[j : j + 1, :], x.shape)


def lower_inverse(rows, width):
    n = len(rows)
    rid = lax.broadcasted_iota(jnp.int32, (8, width), 0)
    cid = lax.broadcasted_iota(jnp.int32, (8, width), 1)
    done = []
    for k in range(n):
        base = 8 * k
        held = rows[k]
        columns = [lanes(held, base + j) for j in range(8)]
        inside = (cid >= base) & (cid < base + 8)
        eye = jnp.where(cid - base == rid, 1.0, 0.0).astype(F32)
        full = jnp.where(inside, eye, held)
        forward = full
        root_scale = jnp.zeros((8, width), F32)
        scale = jnp.zeros((8, width), F32)
        for j in range(8):
            pivot = sublanes(columns[j], j)
            inverse = 1.0 / pivot
            root_scale = jnp.where(rid == j, lax.rsqrt(pivot), root_scale)
            scale = jnp.where(rid == j, inverse, scale)
            ratio = columns[j] * inverse
            ratio_all = jnp.where(rid == j, 0.0, ratio)
            ratio_below = jnp.where(rid > j, ratio, 0.0)
            for m in range(j + 1, 8):
                columns[m] = columns[m] - ratio_all * sublanes(columns[m], j)
            full = full - ratio_all * sublanes(full, j)
            forward = forward - ratio_below * sublanes(forward, j)
        done.append(jnp.where(cid <= rid + base, forward * root_scale, 0.0))
        full = full * scale
        if k + 1 < n:
            spread = [sublanes(full, j) for j in range(8)]
            for i in range(k + 1, n):
                terms = [lanes(rows[i], base + j) * spread[j] for j in range(8)]
                while len(terms) > 1:
                    terms = [terms[q] + terms[q + 1] for q in range(0, len(terms), 2)]
                rows[i] = jnp.where(inside, 0.0, rows[i]) - terms[0]
    return done


def pack(gram):
    width = gram.shape[0]
    half = width // 2
    row = lax.broadcasted_iota(jnp.int32, (half, width), 0)
    col = lax.broadcasted_iota(jnp.int32, (half, width), 1)
    turned = pltpu.roll(gram[half:, :], half, 1)
    both = jnp.where((col < half) & (row < col), turned, gram[:half, :])
    diagonal = jnp.sum(jnp.where(row + half == col, gram[half:, :], 0.0), axis=0, keepdims=True)
    return jnp.concatenate([both, jnp.broadcast_to(diagonal, (8, width))], axis=0)


def unpack(packed):
    width = packed.shape[1]
    half = width // 2
    row = lax.broadcasted_iota(jnp.int32, (width, width), 0)
    col = lax.broadcasted_iota(jnp.int32, (width, width), 1)
    both = packed[:half, :]
    square = jnp.concatenate([both, pltpu.roll(both, half, 1)], axis=0)
    direct = ((row < half) & ((col >= half) | (col <= row))) | ((row >= half) & (col >= half) & (col > row))
    gram = jnp.where(direct, square, square.T)
    return jnp.where((row == col) & (row >= half), jnp.broadcast_to(packed[half : half + 1, :], gram.shape), gram)


def leading(z_ref, recv_ref, stride):
    mine = lax.axis_index("cols")
    return jnp.where((mine & stride) == 0, z_ref[...], recv_ref[...])


def split_kernel(rounds, z_ref, out_ref, own):
    width = z_ref.shape[1]
    points = z_ref.shape[0] // rounds
    own[...] = z_ref[...].astype(F32)
    for r in range(rounds):
        out_ref[:, r * width : (r + 1) * width] = own[pl.ds(r, points, stride=rounds), :].astype(BF16)


def products_kernel(rounds, nblock, stride, radix, scale_ref, own_ref, kept_ref, recv_ref, *rest):
    outs, (lead, cross) = rest[:radix], rest[radix:]
    group = lax.axis_index("cols")
    digit = lax.axis_index("rows") % radix
    width = kept_ref.shape[1]
    points = own_ref.shape[0] // nblock
    part = width // radix
    lead[...] = leading(kept_ref, recv_ref, stride).astype(F32)
    out = jnp.zeros((width, (rounds + 1) * width), F32)
    for b in range(nblock):
        panel = lead[pl.ds(b * points * rounds, points, stride=rounds), :].astype(BF16)
        own = own_ref[b * points : (b + 1) * points, :]
        block = lax.dot_general(
            panel, jnp.concatenate([panel, own], axis=1), (((0,), (0,)), ((), ())), preferred_element_type=F32
        )
        first = scale_ref[b, 0, 0]
        pieces = [block[:, :width] * (first * first)]
        for r in range(rounds):
            pieces.append(block[:, (r + 1) * width : (r + 2) * width] * (first * scale_ref[b, group, r]))
        out = out + jnp.concatenate(pieces, axis=1)
    packed = pack(out[:, :width])
    height = packed.shape[0]
    for r in range(rounds):
        cross[r * width : (r + 1) * width, :] = out[:, (r + 1) * width : (r + 2) * width]
    for b in range(radix):
        outs[b][:height, :] = packed
        for r in range(rounds):
            at = pl.multiple_of(r * width + (digit ^ b) * part, part)
            outs[b][height + r * part : height + (r + 1) * part, :] = cross[pl.ds(at, part), :]


def spread_kernel(rounds, stride, kept_ref, recv_ref, out_ref):
    width = kept_ref.shape[1]
    rows = lax.broadcasted_iota(jnp.int32, kept_ref.shape, 0) % rounds
    lead = leading(kept_ref, recv_ref, stride).astype(F32)
    for r in range(rounds):
        moved = lead if r == 0 else pltpu.roll(lead, r, 0)
        out_ref[:, r * width : (r + 1) * width] = jnp.where(rows == r, moved, 0.0).astype(BF16)


def factor_kernel(packed_ref, inverse_ref):
    width = packed_ref.shape[1]
    gram = unpack(packed_ref[...])
    rows = [gram[8 * i : 8 * i + 8, :] for i in range(width // 8)]
    for i, row in enumerate(lower_inverse(rows, width)):
        inverse_ref[8 * i : 8 * i + 8, :] = row


def finish_kernel(rounds, nblock, radix, root, chunks, scale_ref, z_ref, lead_ref, inverse_ref, *rest):
    parts, (coef_ref, out_ref, cross, held, sems) = rest[:radix], rest[radix:]
    group = lax.axis_index("cols")
    digit = lax.axis_index("rows") % radix
    width = z_ref.shape[1]
    part = width // radix
    for b in range(radix):
        for r in range(rounds):
            at = pl.multiple_of((digit ^ b) * part, part)
            cross[pl.ds(at, part), r * width : (r + 1) * width] = parts[b][r * part : (r + 1) * part, :]
    inverse = inverse_ref[...]
    across = inverse.T
    raw = jnp.dot(inverse, cross[...], precision=HIGH, preferred_element_type=F32)
    weights = jnp.dot(across, raw, precision=HIGH, preferred_element_type=F32)
    stacked = []
    for r in range(rounds):
        coef_ref[pl.ds(r, width, stride=rounds), :] = raw[:, r * width : (r + 1) * width] * (1.0 / root)
        weight = weights[:, r * width : (r + 1) * width]
        if r == 0:
            weight = jnp.where(group == 0, -root * across, weight)
        upper = weight.astype(BF16)
        stacked.append(jnp.concatenate([upper, (weight - upper.astype(F32)).astype(BF16)], axis=1))
    weight = jnp.concatenate(stacked, axis=0)
    span = z_ref.shape[0] // chunks
    row = lax.broadcasted_iota(jnp.int32, (span, width), 0) % rounds
    copies = []
    for c in range(chunks):
        block = c * nblock // chunks
        at = slice(c * span, (c + 1) * span)
        acc = jnp.dot(lead_ref[at, :], weight, preferred_element_type=F32)
        acc = (acc[:, :width] + acc[:, width:]) * scale_ref[block, 0, 0]
        factor = jnp.zeros((span, width), F32)
        for r in range(rounds):
            own = scale_ref[block, group, r]
            if r == 0:
                own = jnp.where(group == 0, 0.0, own)
            factor = jnp.where(row == r, own, factor)
        held[at, :] = (z_ref[at, :].astype(F32) * factor - acc).astype(BF16)
        copies.append(pltpu.make_async_copy(held.at[at, :], out_ref.at[at, :], sems.at[c]))
        copies[-1].start()
    for copy in copies:
        copy.wait()


def shards(snapshots, scales):
    points, _, rounds, width = snapshots.shape
    nblock = scales.shape[0]
    n_rows, n_cols = lax.axis_size("rows"), lax.axis_size("cols")
    root = math.sqrt(points * n_rows)
    long = points * rounds
    z = snapshots.reshape(long, width)
    kept, recv, stride = from_leader(z, n_cols, lax.axis_index("cols"))
    phases = radices(n_rows)
    radix = phases[0][1]
    height = width // 2 + 8
    payload = height + rounds * width // radix
    params = pltpu.CompilerParams(vmem_limit_bytes=48 << 20)
    own = pl.pallas_call(
        functools.partial(split_kernel, rounds),
        out_shape=jax.ShapeDtypeStruct((points, rounds * width), BF16),
        in_specs=[VMEM],
        out_specs=VMEM,
        scratch_shapes=[pltpu.VMEM((long, width), F32)],
        compiler_params=params,
        name="split",
    )(z)
    sent = pl.pallas_call(
        functools.partial(products_kernel, rounds, nblock, stride, radix),
        out_shape=[jax.ShapeDtypeStruct((payload, width), F32)] * radix,
        in_specs=[SMEM, VMEM, VMEM, VMEM],
        out_specs=[VMEM] * radix,
        scratch_shapes=[pltpu.VMEM((long, width), F32), pltpu.VMEM((rounds * width, width), F32)],
        compiler_params=params,
        name="products",
    )(scales, own, kept, recv)
    lead = pl.pallas_call(
        functools.partial(spread_kernel, rounds, stride),
        out_shape=jax.ShapeDtypeStruct((long, rounds * width), BF16),
        in_specs=[VMEM, VMEM],
        out_specs=VMEM,
        compiler_params=params,
        name="spread",
    )(kept, recv)
    sums = sent[0]
    for step, (hop, base) in enumerate(phases):
        source = sent if step == 0 else [sums] * base
        others = [partner(source[b], "rows", n_rows, b * hop) for b in range(1, base)]
        for other in others:
            sums = sums + other
    mine = sums[height:]
    parts = [mine] + [partner(mine, "rows", n_rows, b) for b in range(1, radix)]
    inverse = pl.pallas_call(
        factor_kernel,
        out_shape=jax.ShapeDtypeStruct((width, width), F32),
        in_specs=[VMEM],
        out_specs=VMEM,
        compiler_params=params,
        cost_estimate=pl.CostEstimate(flops=1 << 30, bytes_accessed=1 << 23, transcendentals=0),
        name="factor",
    )(sums[:height])
    chunks = 2 * nblock
    coef, updated = pl.pallas_call(
        functools.partial(finish_kernel, rounds, nblock, radix, root, chunks),
        out_shape=[
            jax.ShapeDtypeStruct((width * rounds, width), F32),
            jax.ShapeDtypeStruct((long, width), BF16),
        ],
        in_specs=[SMEM] + [VMEM] * (3 + radix),
        out_specs=[VMEM, pl.BlockSpec(memory_space=pl.ANY)],
        scratch_shapes=[
            pltpu.VMEM((width, rounds * width), F32),
            pltpu.VMEM((long, width), BF16),
            pltpu.SemaphoreType.DMA((chunks,)),
        ],
        compiler_params=params,
        name="finish",
    )(scales, z, lead, inverse, *parts)
    return coef.reshape(width, 1, rounds, width), updated.reshape(snapshots.shape)


def solution(mesh):
    return jax.shard_map(
        shards,
        mesh=mesh,
        in_specs=(P("rows", "cols", None, None), P("rows", None, None)),
        out_specs=(P(None, "cols", None, None), P("rows", "cols", None, None)),
        check_vma=False,
    )
```

```python
import functools
import math

import jax
import jax.numpy as jnp
from jax import lax
from jax.experimental import pallas as pl
from jax.experimental.pallas import tpu as pltpu
from jax.sharding import PartitionSpec as P

F32 = jnp.float32
BF16 = jnp.bfloat16
HIGH = lax.Precision.HIGHEST
VMEM = pl.BlockSpec(memory_space=pltpu.VMEM)
SMEM = pl.BlockSpec(memory_space=pltpu.SMEM)


def partner(x, count, offset):
    return lax.ppermute(x, "cols", [(i, i ^ offset) for i in range(count)])


def radices(count):
    found = []
    stride = 1
    while stride < count:
        radix = 4 if (count // stride) % 4 == 0 else 2
        found.append((stride, radix))
        stride *= radix
    return found


def exchange(x, phases, step, b, n_rows, n_cols):
    pairs = []
    for row in range(n_rows):
        for col in range(n_cols):
            stride = phases[(step + turn(phases, col)) % len(phases)][0]
            pairs.append((row * n_cols + col, (row ^ (b * stride)) * n_cols + col))
    return lax.ppermute(x, ("rows", "cols"), pairs)


def turn(phases, col):
    return col % 2 if len({radix for _, radix in phases}) == 1 else 0


def row_digit(phases, n_cols):
    row, digit = lax.axis_index("rows"), None
    for col in range(min(n_cols, 2)):
        stride, radix = phases[turn(phases, col) % len(phases)]
        own = (row // stride) % radix
        digit = own if digit is None else jnp.where(lax.axis_index("cols") % 2 == 0, digit, own)
    return digit


def from_leader(x, count, mine):
    stride = 1
    while 2 * stride < count:
        x = jnp.where((mine & stride) != 0, partner(x, count, stride), x)
        stride *= 2
    return x, partner(x, count, stride), stride


def lanes(x, p):
    return jnp.broadcast_to(x[:, p : p + 1], x.shape)


def sublanes(x, j):
    return jnp.broadcast_to(x[j : j + 1, :], x.shape)


def lower_inverse(rows, width):
    n = len(rows)
    rid = lax.broadcasted_iota(jnp.int32, (8, width), 0)
    cid = lax.broadcasted_iota(jnp.int32, (8, width), 1)
    done = []
    for k in range(n):
        base = 8 * k
        held = rows[k]
        columns = [lanes(held, base + j) for j in range(8)]
        inside = (cid >= base) & (cid < base + 8)
        eye = jnp.where(cid - base == rid, 1.0, 0.0).astype(F32)
        full = jnp.where(inside, eye, held)
        forward = full
        root_scale = jnp.zeros((8, width), F32)
        scale = jnp.zeros((8, width), F32)
        for j in range(8):
            pivot = sublanes(columns[j], j)
            inverse = 1.0 / pivot
            root_scale = jnp.where(rid == j, lax.rsqrt(pivot), root_scale)
            scale = jnp.where(rid == j, inverse, scale)
            ratio = columns[j] * inverse
            ratio_all = jnp.where(rid == j, 0.0, ratio)
            ratio_below = jnp.where(rid > j, ratio, 0.0)
            for m in range(j + 1, 8):
                columns[m] = columns[m] - ratio_all * sublanes(columns[m], j)
            full = full - ratio_all * sublanes(full, j)
            forward = forward - ratio_below * sublanes(forward, j)
        done.append(jnp.where(cid <= rid + base, forward * root_scale, 0.0))
        full = full * scale
        if k + 1 < n:
            spread = [sublanes(full, j) for j in range(8)]
            for i in range(k + 1, n):
                terms = [lanes(rows[i], base + j) * spread[j] for j in range(8)]
                while len(terms) > 1:
                    terms = [terms[q] + terms[q + 1] for q in range(0, len(terms), 2)]
                rows[i] = jnp.where(inside, 0.0, rows[i]) - terms[0]
    return done


def pack(gram):
    width = gram.shape[0]
    half = width // 2
    row = lax.broadcasted_iota(jnp.int32, (half, width), 0)
    col = lax.broadcasted_iota(jnp.int32, (half, width), 1)
    turned = pltpu.roll(gram[half:, :], half, 1)
    both = jnp.where((col < half) & (row < col), turned, gram[:half, :])
    diagonal = jnp.sum(jnp.where(row + half == col, gram[half:, :], 0.0), axis=0, keepdims=True)
    return jnp.concatenate([both, jnp.broadcast_to(diagonal, (8, width))], axis=0)


def unpack(packed):
    width = packed.shape[1]
    half = width // 2
    row = lax.broadcasted_iota(jnp.int32, (width, width), 0)
    col = lax.broadcasted_iota(jnp.int32, (width, width), 1)
    both = packed[:half, :]
    square = jnp.concatenate([both, pltpu.roll(both, half, 1)], axis=0)
    direct = ((row < half) & ((col >= half) | (col <= row))) | ((row >= half) & (col >= half) & (col > row))
    gram = jnp.where(direct, square, square.T)
    return jnp.where((row == col) & (row >= half), jnp.broadcast_to(packed[half : half + 1, :], gram.shape), gram)


def leading(z_ref, recv_ref, stride):
    mine = lax.axis_index("cols")
    return jnp.where((mine & stride) == 0, z_ref[...], recv_ref[...])


def split_kernel(rounds, z_ref, out_ref, own):
    width = z_ref.shape[1]
    points = z_ref.shape[0] // rounds
    own[...] = z_ref[...].astype(F32)
    for r in range(rounds):
        out_ref[:, r * width : (r + 1) * width] = own[pl.ds(r, points, stride=rounds), :].astype(BF16)


def products_kernel(rounds, nblock, stride, phases, radix, scale_ref, own_ref, kept_ref, recv_ref, *rest):
    outs, (lead, cross) = rest[:radix], rest[radix:]
    group = lax.axis_index("cols")
    digit = row_digit(phases, lax.axis_size("cols"))
    width = kept_ref.shape[1]
    points = own_ref.shape[0] // nblock
    part = width // radix
    lead[...] = leading(kept_ref, recv_ref, stride).astype(F32)
    out = jnp.zeros((width, (rounds + 1) * width), F32)
    for b in range(nblock):
        panel = lead[pl.ds(b * points * rounds, points, stride=rounds), :].astype(BF16)
        own = own_ref[b * points : (b + 1) * points, :]
        block = lax.dot_general(
            panel, jnp.concatenate([panel, own], axis=1), (((0,), (0,)), ((), ())), preferred_element_type=F32
        )
        first = scale_ref[b, 0, 0]
        pieces = [block[:, :width] * (first * first)]
        for r in range(rounds):
            pieces.append(block[:, (r + 1) * width : (r + 2) * width] * (first * scale_ref[b, group, r]))
        out = out + jnp.concatenate(pieces, axis=1)
    packed = pack(out[:, :width])
    height = packed.shape[0]
    for r in range(rounds):
        cross[r * width : (r + 1) * width, :] = out[:, (r + 1) * width : (r + 2) * width]
    for b in range(radix):
        outs[b][:height, :] = packed
        for r in range(rounds):
            at = pl.multiple_of(r * width + (digit ^ b) * part, part)
            outs[b][height + r * part : height + (r + 1) * part, :] = cross[pl.ds(at, part), :]


def spread_kernel(rounds, stride, kept_ref, recv_ref, out_ref):
    width = kept_ref.shape[1]
    rows = lax.broadcasted_iota(jnp.int32, kept_ref.shape, 0) % rounds
    lead = leading(kept_ref, recv_ref, stride).astype(F32)
    for r in range(rounds):
        moved = lead if r == 0 else pltpu.roll(lead, r, 0)
        out_ref[:, r * width : (r + 1) * width] = jnp.where(rows == r, moved, 0.0).astype(BF16)


def factor_kernel(packed_ref, inverse_ref):
    width = packed_ref.shape[1]
    gram = unpack(packed_ref[...])
    rows = [gram[8 * i : 8 * i + 8, :] for i in range(width // 8)]
    for i, row in enumerate(lower_inverse(rows, width)):
        inverse_ref[8 * i : 8 * i + 8, :] = row


def finish_kernel(rounds, nblock, phases, radix, root, chunks, scale_ref, z_ref, lead_ref, inverse_ref, *rest):
    parts, (coef_ref, out_ref, cross, held, sems) = rest[:radix], rest[radix:]
    group = lax.axis_index("cols")
    digit = row_digit(phases, lax.axis_size("cols"))
    width = z_ref.shape[1]
    part = width // radix
    for b in range(radix):
        for r in range(rounds):
            at = pl.multiple_of((digit ^ b) * part, part)
            cross[pl.ds(at, part), r * width : (r + 1) * width] = parts[b][r * part : (r + 1) * part, :]
    inverse = inverse_ref[...]
    across = inverse.T
    raw = jnp.dot(inverse, cross[...], precision=HIGH, preferred_element_type=F32)
    weights = jnp.dot(across, raw, precision=HIGH, preferred_element_type=F32)
    stacked = []
    for r in range(rounds):
        coef_ref[pl.ds(r, width, stride=rounds), :] = raw[:, r * width : (r + 1) * width] * (1.0 / root)
        weight = weights[:, r * width : (r + 1) * width]
        if r == 0:
            weight = jnp.where(group == 0, -root * across, weight)
        upper = weight.astype(BF16)
        stacked.append(jnp.concatenate([upper, (weight - upper.astype(F32)).astype(BF16)], axis=1))
    weight = jnp.concatenate(stacked, axis=0)
    span = z_ref.shape[0] // chunks
    row = lax.broadcasted_iota(jnp.int32, (span, width), 0) % rounds
    copies = []
    for c in range(chunks):
        block = c * nblock // chunks
        at = slice(c * span, (c + 1) * span)
        acc = jnp.dot(lead_ref[at, :], weight, preferred_element_type=F32)
        acc = (acc[:, :width] + acc[:, width:]) * scale_ref[block, 0, 0]
        factor = jnp.zeros((span, width), F32)
        for r in range(rounds):
            own = scale_ref[block, group, r]
            if r == 0:
                own = jnp.where(group == 0, 0.0, own)
            factor = jnp.where(row == r, own, factor)
        held[at, :] = (z_ref[at, :].astype(F32) * factor - acc).astype(BF16)
        copies.append(pltpu.make_async_copy(held.at[at, :], out_ref.at[at, :], sems.at[c]))
        copies[-1].start()
    for copy in copies:
        copy.wait()


def shards(snapshots, scales):
    points, _, rounds, width = snapshots.shape
    nblock = scales.shape[0]
    n_rows, n_cols = lax.axis_size("rows"), lax.axis_size("cols")
    root = math.sqrt(points * n_rows)
    long = points * rounds
    z = snapshots.reshape(long, width)
    kept, recv, stride = from_leader(z, n_cols, lax.axis_index("cols"))
    phases = radices(n_rows)
    radix = phases[0][1]
    height = width // 2 + 8
    payload = height + rounds * width // radix
    params = pltpu.CompilerParams(vmem_limit_bytes=48 << 20)
    own = pl.pallas_call(
        functools.partial(split_kernel, rounds),
        out_shape=jax.ShapeDtypeStruct((points, rounds * width), BF16),
        in_specs=[VMEM],
        out_specs=VMEM,
        scratch_shapes=[pltpu.VMEM((long, width), F32)],
        compiler_params=params,
        name="split",
    )(z)
    sent = pl.pallas_call(
        functools.partial(products_kernel, rounds, nblock, stride, phases, radix),
        out_shape=[jax.ShapeDtypeStruct((payload, width), F32)] * radix,
        in_specs=[SMEM, VMEM, VMEM, VMEM],
        out_specs=[VMEM] * radix,
        scratch_shapes=[pltpu.VMEM((long, width), F32), pltpu.VMEM((rounds * width, width), F32)],
        compiler_params=params,
        name="products",
    )(scales, own, kept, recv)
    lead = pl.pallas_call(
        functools.partial(spread_kernel, rounds, stride),
        out_shape=jax.ShapeDtypeStruct((long, rounds * width), BF16),
        in_specs=[VMEM, VMEM],
        out_specs=VMEM,
        compiler_params=params,
        name="spread",
    )(kept, recv)
    sums = sent[0]
    for step, (_, base) in enumerate(phases):
        source = sent if step == 0 else [sums] * base
        others = [exchange(source[b], phases, step, b, n_rows, n_cols) for b in range(1, base)]
        for other in others:
            sums = sums + other
    mine = sums[height:]
    parts = [mine] + [exchange(mine, phases, 0, b, n_rows, n_cols) for b in range(1, radix)]
    inverse = pl.pallas_call(
        factor_kernel,
        out_shape=jax.ShapeDtypeStruct((width, width), F32),
        in_specs=[VMEM],
        out_specs=VMEM,
        compiler_params=params,
        cost_estimate=pl.CostEstimate(flops=1 << 30, bytes_accessed=1 << 23, transcendentals=0),
        name="factor",
    )(sums[:height])
    chunks = 2 * nblock
    coef, updated = pl.pallas_call(
        functools.partial(finish_kernel, rounds, nblock, phases, radix, root, chunks),
        out_shape=[
            jax.ShapeDtypeStruct((width * rounds, width), F32),
            jax.ShapeDtypeStruct((long, width), BF16),
        ],
        in_specs=[SMEM] + [VMEM] * (3 + radix),
        out_specs=[VMEM, pl.BlockSpec(memory_space=pl.ANY)],
        scratch_shapes=[
            pltpu.VMEM((width, rounds * width), F32),
            pltpu.VMEM((long, width), BF16),
            pltpu.SemaphoreType.DMA((chunks,)),
        ],
        compiler_params=params,
        name="finish",
    )(scales, z, lead, inverse, *parts)
    return coef.reshape(width, 1, rounds, width), updated.reshape(snapshots.shape)


def solution(mesh):
    return jax.shard_map(
        shards,
        mesh=mesh,
        in_specs=(P("rows", "cols", None, None), P("rows", None, None)),
        out_specs=(P(None, "cols", None, None), P("rows", "cols", None, None)),
        check_vma=False,
    )
```

```python
import functools
import math

import jax
import jax.numpy as jnp
from jax import lax
from jax.experimental import pallas as pl
from jax.experimental.pallas import tpu as pltpu
from jax.sharding import PartitionSpec as P

F32 = jnp.float32
BF16 = jnp.bfloat16
HIGH = lax.Precision.HIGHEST
VMEM = pl.BlockSpec(memory_space=pltpu.VMEM)
SMEM = pl.BlockSpec(memory_space=pltpu.SMEM)


def partner(x, axis, count, offset):
    return lax.ppermute(x, axis, [(i, i ^ offset) for i in range(count)])


def radices(count):
    found = []
    stride = 1
    while stride < count:
        radix = 4 if (count // stride) % 4 == 0 else 2
        found.append((stride, radix))
        stride *= radix
    return found


def from_leader(x, count, mine):
    stride = 1
    while 2 * stride < count:
        x = jnp.where((mine & stride) != 0, partner(x, "cols", count, stride), x)
        stride *= 2
    return x, partner(x, "cols", count, stride), stride


def lanes(x, p):
    return jnp.broadcast_to(x[:, p : p + 1], x.shape)


def sublanes(x, j):
    return jnp.broadcast_to(x[j : j + 1, :], x.shape)


def lower_inverse(rows, width):
    n = len(rows)
    rid = lax.broadcasted_iota(jnp.int32, (8, width), 0)
    cid = lax.broadcasted_iota(jnp.int32, (8, width), 1)
    done = []
    for k in range(n):
        base = 8 * k
        held = rows[k]
        columns = [lanes(held, base + j) for j in range(8)]
        inside = (cid >= base) & (cid < base + 8)
        eye = jnp.where(cid - base == rid, 1.0, 0.0).astype(F32)
        full = jnp.where(inside, eye, held)
        forward = full
        root_scale = jnp.zeros((8, width), F32)
        scale = jnp.zeros((8, width), F32)
        for j in range(8):
            pivot = sublanes(columns[j], j)
            inverse = 1.0 / pivot
            root_scale = jnp.where(rid == j, lax.rsqrt(pivot), root_scale)
            scale = jnp.where(rid == j, inverse, scale)
            ratio = columns[j] * inverse
            ratio_all = jnp.where(rid == j, 0.0, ratio)
            ratio_below = jnp.where(rid > j, ratio, 0.0)
            for m in range(j + 1, 8):
                columns[m] = columns[m] - ratio_all * sublanes(columns[m], j)
            full = full - ratio_all * sublanes(full, j)
            forward = forward - ratio_below * sublanes(forward, j)
        done.append(jnp.where(cid <= rid + base, forward * root_scale, 0.0))
        full = full * scale
        if k + 1 < n:
            spread = [sublanes(full, j) for j in range(8)]
            for i in range(k + 1, n):
                terms = [lanes(rows[i], base + j) * spread[j] for j in range(8)]
                while len(terms) > 1:
                    terms = [terms[q] + terms[q + 1] for q in range(0, len(terms), 2)]
                rows[i] = jnp.where(inside, 0.0, rows[i]) - terms[0]
    return done


def pack(gram):
    width = gram.shape[0]
    half = width // 2
    row = lax.broadcasted_iota(jnp.int32, (half, width), 0)
    col = lax.broadcasted_iota(jnp.int32, (half, width), 1)
    turned = pltpu.roll(gram[half:, :], half, 1)
    both = jnp.where((col < half) & (row < col), turned, gram[:half, :])
    diagonal = jnp.sum(jnp.where(row + half == col, gram[half:, :], 0.0), axis=0, keepdims=True)
    return jnp.concatenate([both, jnp.broadcast_to(diagonal, (8, width))], axis=0)


def unpack(packed):
    width = packed.shape[1]
    half = width // 2
    row = lax.broadcasted_iota(jnp.int32, (width, width), 0)
    col = lax.broadcasted_iota(jnp.int32, (width, width), 1)
    both = packed[:half, :]
    square = jnp.concatenate([both, pltpu.roll(both, half, 1)], axis=0)
    direct = ((row < half) & ((col >= half) | (col <= row))) | ((row >= half) & (col >= half) & (col > row))
    gram = jnp.where(direct, square, square.T)
    return jnp.where((row == col) & (row >= half), jnp.broadcast_to(packed[half : half + 1, :], gram.shape), gram)


def leading(z_ref, recv_ref, stride):
    mine = lax.axis_index("cols")
    return jnp.where((mine & stride) == 0, z_ref[...], recv_ref[...])


def split_kernel(rounds, z_ref, out_ref, own):
    width = z_ref.shape[1]
    points = z_ref.shape[0] // rounds
    own[...] = z_ref[...].astype(F32)
    for r in range(rounds):
        out_ref[:, r * width : (r + 1) * width] = own[pl.ds(r, points, stride=rounds), :].astype(BF16)


def products_kernel(rounds, nblock, stride, scale_ref, own_ref, kept_ref, recv_ref, same_ref, other_ref, lead, cross):
    group = lax.axis_index("cols")
    digit = lax.axis_index("rows") % 2
    width = kept_ref.shape[1]
    points = own_ref.shape[0] // nblock
    half = width // 2
    lead[...] = leading(kept_ref, recv_ref, stride).astype(F32)
    out = jnp.zeros((width, rounds * width), F32)
    for b in range(nblock):
        panel = lead[pl.ds(b * points * rounds, points, stride=rounds), :].astype(BF16)
        own = own_ref[b * points : (b + 1) * points, :]
        block = lax.dot_general(panel, own, (((0,), (0,)), ((), ())), preferred_element_type=F32)
        first = scale_ref[b, 0, 0]
        pieces = [block[:, r * width : (r + 1) * width] * (first * scale_ref[b, group, r]) for r in range(rounds)]
        out = out + jnp.concatenate(pieces, axis=1)
    packed = pack(out[:, :width])
    height = packed.shape[0]
    for r in range(rounds):
        cross[r * width : (r + 1) * width, :] = out[:, r * width : (r + 1) * width]
    for ref, place in ((same_ref, digit), (other_ref, 1 - digit)):
        for r in range(rounds):
            rows = cross[pl.ds(pl.multiple_of(r * width + place * half, half), half), :]
            if r == 0:
                ref[:half, :] = jnp.where(group == 0, packed[:half, :], rows)
                ref[half:height, :] = packed[half:, :]
            else:
                ref[height + (r - 1) * half : height + r * half, :] = rows


def spread_kernel(rounds, stride, kept_ref, recv_ref, out_ref):
    width = kept_ref.shape[1]
    rows = lax.broadcasted_iota(jnp.int32, kept_ref.shape, 0) % rounds
    lead = leading(kept_ref, recv_ref, stride).astype(F32)
    for r in range(rounds):
        moved = lead if r == 0 else pltpu.roll(lead, r, 0)
        out_ref[:, r * width : (r + 1) * width] = jnp.where(rows == r, moved, 0.0).astype(BF16)


def factor_kernel(stride, kept_ref, recv_ref, inverse_ref, gram_ref):
    width = kept_ref.shape[1]
    mine = lax.axis_index("cols")
    height = width // 2 + 8
    packed = jnp.where((mine & stride) == 0, kept_ref[:height, :], recv_ref[:height, :])
    gram = unpack(packed)
    gram_ref[...] = gram
    rows = [gram[8 * i : 8 * i + 8, :] for i in range(width // 8)]
    for i, row in enumerate(lower_inverse(rows, width)):
        inverse_ref[8 * i : 8 * i + 8, :] = row


def finish_kernel(rounds, nblock, root, chunks, scale_ref, z_ref, lead_ref, inverse_ref, gram_ref, same_ref, other_ref, coef_ref, out_ref, cross, held, sems):
    group = lax.axis_index("cols")
    digit = lax.axis_index("rows") % 2
    width = z_ref.shape[1]
    half = width // 2
    height = half + 8
    for ref, place in ((same_ref, digit), (other_ref, 1 - digit)):
        at = pl.ds(pl.multiple_of(place * half, half), half)
        for r in range(rounds):
            if r == 0:
                rows = jnp.where(group == 0, gram_ref[at, :], ref[:half, :])
            else:
                rows = ref[height + (r - 1) * half : height + r * half, :]
            cross[at, r * width : (r + 1) * width] = rows
    inverse = inverse_ref[...]
    across = inverse.T
    raw = jnp.dot(inverse, cross[...], precision=HIGH, preferred_element_type=F32)
    weights = jnp.dot(across, raw, precision=HIGH, preferred_element_type=F32)
    stacked = []
    for r in range(rounds):
        coef_ref[pl.ds(r, width, stride=rounds), :] = raw[:, r * width : (r + 1) * width] * (1.0 / root)
        weight = weights[:, r * width : (r + 1) * width]
        if r == 0:
            weight = jnp.where(group == 0, -root * across, weight)
        upper = weight.astype(BF16)
        stacked.append(jnp.concatenate([upper, (weight - upper.astype(F32)).astype(BF16)], axis=1))
    weight = jnp.concatenate(stacked, axis=0)
    span = z_ref.shape[0] // chunks
    row = lax.broadcasted_iota(jnp.int32, (span, width), 0) % rounds
    copies = []
    for c in range(chunks):
        block = c * nblock // chunks
        at = slice(c * span, (c + 1) * span)
        acc = jnp.dot(lead_ref[at, :], weight, preferred_element_type=F32)
        acc = (acc[:, :width] + acc[:, width:]) * scale_ref[block, 0, 0]
        factor = jnp.zeros((span, width), F32)
        for r in range(rounds):
            own = scale_ref[block, group, r]
            if r == 0:
                own = jnp.where(group == 0, 0.0, own)
            factor = jnp.where(row == r, own, factor)
        held[at, :] = (z_ref[at, :].astype(F32) * factor - acc).astype(BF16)
        copies.append(pltpu.make_async_copy(held.at[at, :], out_ref.at[at, :], sems.at[c]))
        copies[-1].start()
    for copy in copies:
        copy.wait()


def shards(snapshots, scales):
    points, _, rounds, width = snapshots.shape
    nblock = scales.shape[0]
    n_rows, n_cols = lax.axis_size("rows"), lax.axis_size("cols")
    root = math.sqrt(points * n_rows)
    long = points * rounds
    z = snapshots.reshape(long, width)
    kept, recv, stride = from_leader(z, n_cols, lax.axis_index("cols"))
    phases = radices(n_rows)
    payload = (rounds * width) // 2 + 8
    params = pltpu.CompilerParams(vmem_limit_bytes=48 << 20)
    own = pl.pallas_call(
        functools.partial(split_kernel, rounds),
        out_shape=jax.ShapeDtypeStruct((points, rounds * width), BF16),
        in_specs=[VMEM],
        out_specs=VMEM,
        scratch_shapes=[pltpu.VMEM((long, width), F32)],
        compiler_params=params,
        name="split",
    )(z)
    sent = pl.pallas_call(
        functools.partial(products_kernel, rounds, nblock, stride),
        out_shape=[jax.ShapeDtypeStruct((payload, width), F32)] * 2,
        in_specs=[SMEM, VMEM, VMEM, VMEM],
        out_specs=[VMEM] * 2,
        scratch_shapes=[pltpu.VMEM((long, width), F32), pltpu.VMEM((rounds * width, width), F32)],
        compiler_params=params,
        name="products",
    )(scales, own, kept, recv)
    lead = pl.pallas_call(
        functools.partial(spread_kernel, rounds, stride),
        out_shape=jax.ShapeDtypeStruct((long, rounds * width), BF16),
        in_specs=[VMEM, VMEM],
        out_specs=VMEM,
        compiler_params=params,
        name="spread",
    )(kept, recv)
    sums = sent[0]
    for step, (hop, base) in enumerate(phases):
        source = sent if step == 0 else [sums] * 2
        others = [partner(source[b % 2], "rows", n_rows, b * hop) for b in range(1, base)]
        for other in others:
            sums = sums + other
    first, second, bit = from_leader(sums, n_cols, lax.axis_index("cols"))
    gathered = partner(sums, "rows", n_rows, 1)
    inverse, gram = pl.pallas_call(
        functools.partial(factor_kernel, bit),
        out_shape=[jax.ShapeDtypeStruct((width, width), F32)] * 2,
        in_specs=[VMEM] * 2,
        out_specs=[VMEM] * 2,
        compiler_params=params,
        cost_estimate=pl.CostEstimate(flops=1 << 30, bytes_accessed=1 << 23, transcendentals=0),
        name="factor",
    )(first, second)
    chunks = 2 * nblock
    coef, updated = pl.pallas_call(
        functools.partial(finish_kernel, rounds, nblock, root, chunks),
        out_shape=[
            jax.ShapeDtypeStruct((width * rounds, width), F32),
            jax.ShapeDtypeStruct((long, width), BF16),
        ],
        in_specs=[SMEM] + [VMEM] * 6,
        out_specs=[VMEM, pl.BlockSpec(memory_space=pl.ANY)],
        scratch_shapes=[
            pltpu.VMEM((width, rounds * width), F32),
            pltpu.VMEM((long, width), BF16),
            pltpu.SemaphoreType.DMA((chunks,)),
        ],
        compiler_params=params,
        name="finish",
    )(scales, z, lead, inverse, gram, sums, gathered)
    return coef.reshape(width, 1, rounds, width), updated.reshape(snapshots.shape)


def solution(mesh):
    return jax.shard_map(
        shards,
        mesh=mesh,
        in_specs=(P("rows", "cols", None, None), P("rows", None, None)),
        out_specs=(P(None, "cols", None, None), P("rows", "cols", None, None)),
        check_vma=False,
    )
```

```python
import functools
import math

import jax
import jax.numpy as jnp
from jax import lax
from jax.experimental import pallas as pl
from jax.experimental.pallas import tpu as pltpu
from jax.sharding import PartitionSpec as P

F32 = jnp.float32
BF16 = jnp.bfloat16
HIGH = lax.Precision.HIGHEST
VMEM = pl.BlockSpec(memory_space=pltpu.VMEM)
SMEM = pl.BlockSpec(memory_space=pltpu.SMEM)


def partner(x, axis, count, offset):
    return lax.ppermute(x, axis, [(i, i ^ offset) for i in range(count)])


def radices(count):
    found = []
    stride = 1
    while stride < count:
        radix = 4 if (count // stride) % 4 == 0 else 2
        found.append((stride, radix))
        stride *= radix
    return found


def among_pairs(x, count, mine, root):
    stride = 2
    while stride < count:
        x = jnp.where(((mine ^ root) & stride) != 0, partner(x, "cols", count, stride), x)
        stride *= 2
    return x


def lanes(x, p):
    return jnp.broadcast_to(x[:, p : p + 1], x.shape)


def sublanes(x, j):
    return jnp.broadcast_to(x[j : j + 1, :], x.shape)


def lower_inverse(rows, width):
    n = len(rows)
    rid = lax.broadcasted_iota(jnp.int32, (8, width), 0)
    cid = lax.broadcasted_iota(jnp.int32, (8, width), 1)
    done = []
    for k in range(n):
        base = 8 * k
        held = rows[k]
        columns = [lanes(held, base + j) for j in range(8)]
        inside = (cid >= base) & (cid < base + 8)
        eye = jnp.where(cid - base == rid, 1.0, 0.0).astype(F32)
        full = jnp.where(inside, eye, held)
        forward = full
        root_scale = jnp.zeros((8, width), F32)
        scale = jnp.zeros((8, width), F32)
        for j in range(8):
            pivot = sublanes(columns[j], j)
            inverse = 1.0 / pivot
            root_scale = jnp.where(rid == j, lax.rsqrt(pivot), root_scale)
            scale = jnp.where(rid == j, inverse, scale)
            ratio = columns[j] * inverse
            ratio_all = jnp.where(rid == j, 0.0, ratio)
            ratio_below = jnp.where(rid > j, ratio, 0.0)
            for m in range(j + 1, 8):
                columns[m] = columns[m] - ratio_all * sublanes(columns[m], j)
            full = full - ratio_all * sublanes(full, j)
            forward = forward - ratio_below * sublanes(forward, j)
        done.append(jnp.where(cid <= rid + base, forward * root_scale, 0.0))
        full = full * scale
        if k + 1 < n:
            spread = [sublanes(full, j) for j in range(8)]
            for i in range(k + 1, n):
                terms = [lanes(rows[i], base + j) * spread[j] for j in range(8)]
                while len(terms) > 1:
                    terms = [terms[q] + terms[q + 1] for q in range(0, len(terms), 2)]
                rows[i] = jnp.where(inside, 0.0, rows[i]) - terms[0]
    return done


def pack(gram):
    width = gram.shape[0]
    half = width // 2
    row = lax.broadcasted_iota(jnp.int32, (half, width), 0)
    col = lax.broadcasted_iota(jnp.int32, (half, width), 1)
    turned = pltpu.roll(gram[half:, :], half, 1)
    both = jnp.where((col < half) & (row < col), turned, gram[:half, :])
    diagonal = jnp.sum(jnp.where(row + half == col, gram[half:, :], 0.0), axis=0, keepdims=True)
    return jnp.concatenate([both, jnp.broadcast_to(diagonal, (8, width))], axis=0)


def unpack(packed):
    width = packed.shape[1]
    half = width // 2
    row = lax.broadcasted_iota(jnp.int32, (width, width), 0)
    col = lax.broadcasted_iota(jnp.int32, (width, width), 1)
    both = packed[:half, :]
    square = jnp.concatenate([both, pltpu.roll(both, half, 1)], axis=0)
    direct = ((row < half) & ((col >= half) | (col <= row))) | ((row >= half) & (col >= half) & (col > row))
    gram = jnp.where(direct, square, square.T)
    return jnp.where((row == col) & (row >= half), jnp.broadcast_to(packed[half : half + 1, :], gram.shape), gram)


def leading(even_ref, odd_ref):
    return jnp.where(lax.axis_index("cols") % 2 == 0, even_ref[...], odd_ref[...])


def split_kernel(rounds, z_ref, first_ref, own_ref, wide):
    points = z_ref.shape[0] // rounds
    wide[...] = z_ref[...].astype(F32)
    first = wide[pl.ds(0, points, stride=rounds), :].astype(BF16)
    last = wide[pl.ds(1, points, stride=rounds), :].astype(BF16)
    first_ref[...] = first
    own_ref[...] = jnp.where(lax.axis_index("cols") % 2 == 1, first, last)


def products_kernel(rounds, nblock, scale_ref, first_ref, own_ref, recv_ref, *rest):
    lead_ref = rest[:-4] if len(rest) == 4 else (*rest[:2], rest[-1])
    same_ref, other_ref, wide, cross = rest if len(rest) == 4 else rest[2:-1]
    group = lax.axis_index("cols")
    odd = group % 2
    place_round = 1 - odd
    digit = lax.axis_index("rows") % 2
    width = recv_ref.shape[1]
    points = own_ref.shape[0] // nblock
    half = width // 2
    height = half + 8
    wide[...] = recv_ref[...].astype(F32)
    if lead_ref:
        lead_ref[2][...] = leading(*lead_ref[:2]).astype(F32)
    out = jnp.zeros((width, 2 * width), F32)
    for b in range(nblock):
        at = slice(b * points, (b + 1) * points)
        start = b * points * rounds
        near = wide[pl.ds(start, points, stride=rounds), :]
        far = wide[pl.ds(start + 1, points, stride=rounds), :]
        theirs = jnp.where(odd == 1, near, far).astype(BF16)
        if lead_ref:
            panel = lead_ref[2][pl.ds(start, points, stride=rounds), :].astype(BF16)
        else:
            panel = jnp.where(odd == 1, theirs, first_ref[at, :])
        block = lax.dot_general(
            panel, jnp.concatenate([theirs, own_ref[at, :]], axis=1), (((0,), (0,)), ((), ())), preferred_element_type=F32
        )
        first = scale_ref[b, 0, 0]
        left = block[:, :width] * (first * scale_ref[b, group + 1 - 2 * odd, place_round])
        right = block[:, width:] * (first * scale_ref[b, group, place_round])
        out = out + jnp.concatenate([left, right], axis=1)
    packed = pack(out[:, :width])
    cross[:width, :] = out[:, :width]
    cross[width:, :] = out[:, width:]
    for ref, place in ((same_ref, digit), (other_ref, 1 - digit)):
        theirs = cross[pl.ds(pl.multiple_of(place * half, half), half), :]
        ref[:half, :] = jnp.where(group == 1, packed[:half, :], theirs)
        ref[half:height, :] = packed[half:, :]
        ref[height:, :] = cross[pl.ds(pl.multiple_of(width + place * half, half), half), :]


def spread_kernel(rounds, even_ref, odd_ref, out_ref):
    width = even_ref.shape[1]
    rows = lax.broadcasted_iota(jnp.int32, even_ref.shape, 0) % rounds
    lead = leading(even_ref, odd_ref).astype(F32)
    for r in range(rounds):
        moved = lead if r == 0 else pltpu.roll(lead, r, 0)
        out_ref[:, r * width : (r + 1) * width] = jnp.where(rows == r, moved, 0.0).astype(BF16)


def factor_kernel(sums_ref, out_ref):
    width = sums_ref.shape[1]
    height = width // 2 + 8
    group = lax.axis_index("cols")

    @pl.when(group == 1)
    def _():
        gram = unpack(sums_ref[:height, :])
        out_ref[width:, :] = gram
        rows = [gram[8 * i : 8 * i + 8, :] for i in range(width // 8)]
        for i, row in enumerate(lower_inverse(rows, width)):
            out_ref[8 * i : 8 * i + 8, :] = row

    @pl.when(group != 1)
    def _():
        out_ref[:width, :] = jnp.zeros((width, width), F32)
        out_ref[width : width + height, :] = sums_ref[:height, :]
        out_ref[width + height :, :] = jnp.zeros((width - height, width), F32)


def finish_kernel(
    rounds, nblock, root, chunks, scale_ref, z_ref, lead_ref, kept_ref, recv_ref, same_ref, other_ref, across_ref,
    coef_ref, out_ref, cross, held, sems,
):
    group = lax.axis_index("cols")
    odd = group % 2 == 1
    digit = lax.axis_index("rows") % 2
    width = z_ref.shape[1]
    half = width // 2
    height = half + 8
    for place, own_ref, theirs in ((digit, same_ref, recv_ref[width : width + half, :]), (1 - digit, other_ref, across_ref[:half, :])):
        at = pl.ds(pl.multiple_of(place * half, half), half)
        gram = recv_ref[pl.ds(pl.multiple_of(width + place * half, half), half), :]
        mine = own_ref[height:, :]
        theirs = jnp.where(group == 0, gram, theirs)
        cross[at, :width] = jnp.where(odd, mine, theirs)
        cross[at, width:] = jnp.where(odd, theirs, mine)
    inverse = jnp.where(odd, kept_ref[:width, :], recv_ref[:width, :])
    across = inverse.T
    raw = jnp.dot(inverse, cross[...], precision=HIGH, preferred_element_type=F32)
    weights = jnp.dot(across, raw, precision=HIGH, preferred_element_type=F32)
    stacked = []
    for r in range(rounds):
        coef_ref[pl.ds(r, width, stride=rounds), :] = raw[:, r * width : (r + 1) * width] * (1.0 / root)
        weight = weights[:, r * width : (r + 1) * width]
        if r == 0:
            weight = jnp.where(group == 0, -root * across, weight)
        upper = weight.astype(BF16)
        stacked.append(jnp.concatenate([upper, (weight - upper.astype(F32)).astype(BF16)], axis=1))
    weight = jnp.concatenate(stacked, axis=0)
    span = z_ref.shape[0] // chunks
    row = lax.broadcasted_iota(jnp.int32, (span, width), 0) % rounds
    copies = []
    for c in range(chunks):
        block = c * nblock // chunks
        at = slice(c * span, (c + 1) * span)
        acc = jnp.dot(lead_ref[at, :], weight, preferred_element_type=F32)
        acc = (acc[:, :width] + acc[:, width:]) * scale_ref[block, 0, 0]
        factor = jnp.zeros((span, width), F32)
        for r in range(rounds):
            own = scale_ref[block, group, r]
            if r == 0:
                own = jnp.where(group == 0, 0.0, own)
            factor = jnp.where(row == r, own, factor)
        held[at, :] = (z_ref[at, :].astype(F32) * factor - acc).astype(BF16)
        copies.append(pltpu.make_async_copy(held.at[at, :], out_ref.at[at, :], sems.at[c]))
        copies[-1].start()
    for copy in copies:
        copy.wait()


def shards(snapshots, scales):
    points, _, rounds, width = snapshots.shape
    nblock = scales.shape[0]
    n_rows, n_cols = lax.axis_size("rows"), lax.axis_size("cols")
    root = math.sqrt(points * n_rows)
    long = points * rounds
    z = snapshots.reshape(long, width)
    group = lax.axis_index("cols")
    recv = partner(z, "cols", n_cols, 1)
    even = among_pairs(z, n_cols, group, 0)
    leads = (even, recv) if n_cols == 2 else (even, partner(even, "cols", n_cols, 1))
    phases = radices(n_rows)
    payload = width + 8
    params = pltpu.CompilerParams(vmem_limit_bytes=48 << 20)
    first, own = pl.pallas_call(
        functools.partial(split_kernel, rounds),
        out_shape=[jax.ShapeDtypeStruct((points, width), BF16)] * 2,
        in_specs=[VMEM],
        out_specs=[VMEM] * 2,
        scratch_shapes=[pltpu.VMEM((long, width), F32)],
        compiler_params=params,
        name="split",
    )(z)
    extra = () if n_cols == 2 else leads
    sent = pl.pallas_call(
        functools.partial(products_kernel, rounds, nblock),
        out_shape=[jax.ShapeDtypeStruct((payload, width), F32)] * 2,
        in_specs=[SMEM] + [VMEM] * (3 + len(extra)),
        out_specs=[VMEM] * 2,
        scratch_shapes=[pltpu.VMEM((long, width), F32), pltpu.VMEM((2 * width, width), F32)]
        + [pltpu.VMEM((long, width), F32)] * (len(extra) // 2),
        compiler_params=params,
        name="products",
    )(scales, first, own, recv, *extra)
    sums = sent[0]
    for step, (hop, base) in enumerate(phases):
        source = sent if step == 0 else [sums] * 2
        others = [partner(source[b % 2], "rows", n_rows, b * hop) for b in range(1, base)]
        if step == len(phases) - 1:
            lead = pl.pallas_call(
                functools.partial(spread_kernel, rounds),
                out_shape=jax.ShapeDtypeStruct((long, rounds * width), BF16),
                in_specs=[VMEM, VMEM],
                out_specs=VMEM,
                compiler_params=params,
                name="spread",
            )(*leads)
            *others, lead = lax.optimization_barrier((*others, lead))
        for other in others:
            sums = sums + other
    gathered = partner(sums, "rows", n_rows, 1)
    factored = pl.pallas_call(
        factor_kernel,
        out_shape=jax.ShapeDtypeStruct((2 * width, width), F32),
        in_specs=[VMEM],
        out_specs=VMEM,
        compiler_params=params,
        cost_estimate=pl.CostEstimate(flops=1 << 30, bytes_accessed=1 << 23, transcendentals=0),
        name="factor",
    )(sums)
    if n_cols > 2:
        shared = among_pairs(factored[:width], n_cols, group, 1)
        factored = jnp.concatenate([shared, factored[width:]], axis=0)
    crossed = partner(gathered, "cols", n_cols, 1)
    swapped = partner(factored, "cols", n_cols, 1)
    chunks = 2 * nblock
    coef, updated = pl.pallas_call(
        functools.partial(finish_kernel, rounds, nblock, root, chunks),
        out_shape=[
            jax.ShapeDtypeStruct((width * rounds, width), F32),
            jax.ShapeDtypeStruct((long, width), BF16),
        ],
        in_specs=[SMEM] + [VMEM] * 7,
        out_specs=[VMEM, pl.BlockSpec(memory_space=pl.ANY)],
        scratch_shapes=[
            pltpu.VMEM((width, rounds * width), F32),
            pltpu.VMEM((long, width), BF16),
            pltpu.SemaphoreType.DMA((chunks,)),
        ],
        compiler_params=params,
        name="finish",
    )(scales, z, lead, factored, swapped, sums, gathered, crossed)
    return coef.reshape(width, 1, rounds, width), updated.reshape(snapshots.shape)


def solution(mesh):
    return jax.shard_map(
        shards,
        mesh=mesh,
        in_specs=(P("rows", "cols", None, None), P("rows", None, None)),
        out_specs=(P(None, "cols", None, None), P("rows", "cols", None, None)),
        check_vma=False,
    )
```

```python
import functools
import math

import jax
import jax.numpy as jnp
from jax import lax
from jax.experimental import pallas as pl
from jax.experimental.pallas import tpu as pltpu
from jax.sharding import PartitionSpec as P

F32 = jnp.float32
BF16 = jnp.bfloat16
VMEM = pl.BlockSpec(memory_space=pltpu.VMEM)
SMEM = pl.BlockSpec(memory_space=pltpu.SMEM)


def partner(x, axis, count, offset):
    return lax.ppermute(x, axis, [(i, i ^ offset) for i in range(count)])


def radices(count):
    found = []
    stride = 1
    while stride < count:
        radix = 4 if (count // stride) % 4 == 0 else 2
        found.append((stride, radix))
        stride *= radix
    return found


def among_pairs(x, count, mine, root):
    stride = 2
    while stride < count:
        x = jnp.where(((mine ^ root) & stride) != 0, partner(x, "cols", count, stride), x)
        stride *= 2
    return x


def lanes(x, p):
    return jnp.broadcast_to(x[:, p : p + 1], x.shape)


def sublanes(x, j):
    return jnp.broadcast_to(x[j : j + 1, :], x.shape)


def thirds(x):
    high = x.astype(BF16)
    rest = x - high.astype(F32)
    middle = rest.astype(BF16)
    return high, middle, (rest - middle.astype(F32)).astype(BF16)


def product(left, right):
    return product_of_thirds(thirds(left), thirds(right))


def product_of_thirds(left, right):
    columns = right[0].shape[1]
    wide = jnp.concatenate(right[:2], axis=1)
    both = jnp.dot(
        jnp.concatenate(left[:2], axis=1), jnp.concatenate([wide, wide], axis=0), preferred_element_type=F32
    )
    small = jnp.dot(
        jnp.concatenate([left[0], left[2]], axis=1),
        jnp.concatenate([right[2], right[0]], axis=0),
        preferred_element_type=F32,
    )
    return (both[:, :columns] + both[:, columns:]) + small


def lower_inverse(rows, width):
    n = len(rows)
    rid = lax.broadcasted_iota(jnp.int32, (8, width), 0)
    cid = lax.broadcasted_iota(jnp.int32, (8, width), 1)
    done = []
    for k in range(n):
        base = 8 * k
        held = rows[k]
        columns = [lanes(held, base + j) for j in range(8)]
        inside = (cid >= base) & (cid < base + 8)
        eye = jnp.where(cid - base == rid, 1.0, 0.0).astype(F32)
        full = jnp.where(inside, eye, held)
        forward = full
        scale = jnp.zeros((8, width), F32)
        inverses = []
        for j in range(0, 8, 2):
            left, right = columns[j], columns[j + 1]
            a, b, c = sublanes(left, j), sublanes(right, j), sublanes(right, j + 1)
            det = a * c - b * b
            inverse, inverse_a = 1.0 / det, 1.0 / a
            pair = (rid == j) | (rid == j + 1)
            left, right = jnp.where(pair, 0.0, left), jnp.where(pair, 0.0, right)
            first, second = (left * c - right * b) * inverse, (right * a - left * b) * inverse
            for m in range(j + 2, 8):
                columns[m] = columns[m] - (first * sublanes(columns[m], j) + second * sublanes(columns[m], j + 1))
            full = full - (first * sublanes(full, j) + second * sublanes(full, j + 1))
            below = rid > j + 1
            first = jnp.where(below, first, jnp.where(rid == j + 1, b * inverse_a, 0.0))
            second = jnp.where(below, second, 0.0)
            forward = forward - (first * sublanes(forward, j) + second * sublanes(forward, j + 1))
            scale = jnp.where(rid == j, lax.rsqrt(a), jnp.where(rid == j + 1, lax.rsqrt(det * inverse_a), scale))
            inverses.append((a * inverse, b * inverse, c * inverse))
        done.append(jnp.where(cid <= rid + base, forward * scale, 0.0))
        if k + 1 == n:
            break
        spread = []
        for j, (a, b, c) in enumerate(inverses):
            above, under = sublanes(full, 2 * j), sublanes(full, 2 * j + 1)
            spread += [above * c - under * b, under * a - above * b]
        terms = [lanes(rows[k + 1], base + j) * spread[j] for j in range(8)]
        while len(terms) > 1:
            terms = [terms[q] + terms[q + 1] for q in range(0, len(terms), 2)]
        rows[k + 1] = jnp.where(inside, 0.0, rows[k + 1]) - terms[0]
        if k + 2 == n:
            continue
        solved = jnp.zeros((8, width), F32)
        for j in range(8):
            solved = jnp.where(rid == j, spread[j], solved)
        far = jnp.concatenate(rows[k + 2 :], axis=0)
        column = lax.broadcasted_iota(jnp.int32, far.shape, 1)
        within = (column >= base) & (column < base + 8)
        placed = []
        for third in thirds(solved):
            blocks = [jnp.zeros((base, width), F32)] if base else []
            blocks += [third.astype(F32), jnp.zeros((width - base - 8, width), F32)]
            placed.append(jnp.concatenate(blocks, axis=0).astype(BF16))
        update = product_of_thirds(thirds(jnp.where(within, far, 0.0)), placed)
        far = jnp.where(within, 0.0, far) - update
        for i in range(k + 2, n):
            rows[i] = far[8 * (i - k - 2) : 8 * (i - k - 1)]
    return done


def pack(gram):
    width = gram.shape[0]
    half = width // 2
    row = lax.broadcasted_iota(jnp.int32, (half, width), 0)
    col = lax.broadcasted_iota(jnp.int32, (half, width), 1)
    turned = pltpu.roll(gram[half:, :], half, 1)
    both = jnp.where((col < half) & (row < col), turned, gram[:half, :])
    diagonal = jnp.sum(jnp.where(row + half == col, gram[half:, :], 0.0), axis=0, keepdims=True)
    return jnp.concatenate([both, jnp.broadcast_to(diagonal, (8, width))], axis=0)


def unpack(packed):
    width = packed.shape[1]
    half = width // 2
    row = lax.broadcasted_iota(jnp.int32, (width, width), 0)
    col = lax.broadcasted_iota(jnp.int32, (width, width), 1)
    both = packed[:half, :]
    square = jnp.concatenate([both, pltpu.roll(both, half, 1)], axis=0)
    direct = ((row < half) & ((col >= half) | (col <= row))) | ((row >= half) & (col >= half) & (col > row))
    gram = jnp.where(direct, square, square.T)
    return jnp.where((row == col) & (row >= half), jnp.broadcast_to(packed[half : half + 1, :], gram.shape), gram)


def leading(even_ref, odd_ref):
    return jnp.where(lax.axis_index("cols") % 2 == 0, even_ref[...], odd_ref[...])


def split_kernel(rounds, z_ref, first_ref, own_ref, wide):
    points = z_ref.shape[0] // rounds
    wide[...] = z_ref[...].astype(F32)
    first = wide[pl.ds(0, points, stride=rounds), :].astype(BF16)
    last = wide[pl.ds(1, points, stride=rounds), :].astype(BF16)
    first_ref[...] = first
    own_ref[...] = jnp.where(lax.axis_index("cols") % 2 == 1, first, last)


def products_kernel(rounds, nblock, scale_ref, first_ref, own_ref, recv_ref, *rest):
    lead_ref = rest[:-4] if len(rest) == 4 else (*rest[:2], rest[-1])
    same_ref, other_ref, wide, cross = rest if len(rest) == 4 else rest[2:-1]
    group = lax.axis_index("cols")
    odd = group % 2
    place_round = 1 - odd
    digit = lax.axis_index("rows") % 2
    width = recv_ref.shape[1]
    points = own_ref.shape[0] // nblock
    half = width // 2
    height = half + 8
    wide[...] = recv_ref[...].astype(F32)
    if lead_ref:
        lead_ref[2][...] = leading(*lead_ref[:2]).astype(F32)
    out = jnp.zeros((width, 2 * width), F32)
    for b in range(nblock):
        at = slice(b * points, (b + 1) * points)
        start = b * points * rounds
        near = wide[pl.ds(start, points, stride=rounds), :]
        far = wide[pl.ds(start + 1, points, stride=rounds), :]
        theirs = jnp.where(odd == 1, near, far).astype(BF16)
        if lead_ref:
            panel = lead_ref[2][pl.ds(start, points, stride=rounds), :].astype(BF16)
        else:
            panel = jnp.where(odd == 1, theirs, first_ref[at, :])
        block = lax.dot_general(
            panel, jnp.concatenate([theirs, own_ref[at, :]], axis=1), (((0,), (0,)), ((), ())), preferred_element_type=F32
        )
        first = scale_ref[b, 0, 0]
        left = block[:, :width] * (first * scale_ref[b, group + 1 - 2 * odd, place_round])
        right = block[:, width:] * (first * scale_ref[b, group, place_round])
        out = out + jnp.concatenate([left, right], axis=1)
    packed = pack(out[:, :width])
    cross[:width, :] = out[:, :width]
    cross[width:, :] = out[:, width:]
    for ref, place in ((same_ref, digit), (other_ref, 1 - digit)):
        theirs = cross[pl.ds(pl.multiple_of(place * half, half), half), :]
        ref[:half, :] = jnp.where(group == 1, packed[:half, :], theirs)
        ref[half:height, :] = packed[half:, :]
        ref[height:, :] = cross[pl.ds(pl.multiple_of(width + place * half, half), half), :]


def spread_kernel(rounds, even_ref, odd_ref, out_ref):
    width = even_ref.shape[1]
    rows = lax.broadcasted_iota(jnp.int32, even_ref.shape, 0) % rounds
    lead = leading(even_ref, odd_ref).astype(F32)
    for r in range(rounds):
        moved = lead if r == 0 else pltpu.roll(lead, r, 0)
        out_ref[:, r * width : (r + 1) * width] = jnp.where(rows == r, moved, 0.0).astype(BF16)


def factor_kernel(sums_ref, out_ref):
    width = sums_ref.shape[1]
    height = width // 2 + 8
    group = lax.axis_index("cols")

    @pl.when(group == 1)
    def _():
        gram = unpack(sums_ref[:height, :])
        out_ref[width:, :] = gram
        rows = [gram[8 * i : 8 * i + 8, :] for i in range(width // 8)]
        for i, row in enumerate(lower_inverse(rows, width)):
            out_ref[8 * i : 8 * i + 8, :] = row

    @pl.when(group != 1)
    def _():
        out_ref[:width, :] = jnp.zeros((width, width), F32)
        out_ref[width : width + height, :] = sums_ref[:height, :]
        out_ref[width + height :, :] = jnp.zeros((width - height, width), F32)


def finish_kernel(
    rounds, nblock, root, chunks, scale_ref, z_ref, lead_ref, kept_ref, recv_ref, same_ref, other_ref, across_ref,
    coef_ref, out_ref, cross, coef, held, sems,
):
    group = lax.axis_index("cols")
    odd = group % 2 == 1
    digit = lax.axis_index("rows") % 2
    width = z_ref.shape[1]
    half = width // 2
    height = half + 8
    for place, own_ref, theirs in ((digit, same_ref, recv_ref[width : width + half, :]), (1 - digit, other_ref, across_ref[:half, :])):
        at = pl.ds(pl.multiple_of(place * half, half), half)
        gram = recv_ref[pl.ds(pl.multiple_of(width + place * half, half), half), :]
        mine = own_ref[height:, :]
        theirs = jnp.where(group == 0, gram, theirs)
        cross[at, :width] = jnp.where(odd, mine, theirs)
        cross[at, width:] = jnp.where(odd, theirs, mine)
    inverse = jnp.where(odd, kept_ref[:width, :], recv_ref[:width, :])
    across = inverse.T
    raw = product(inverse, cross[...])
    for r in range(rounds):
        coef[pl.ds(r, width, stride=rounds), :] = raw[:, r * width : (r + 1) * width] * (1.0 / root)
    copies = [pltpu.make_async_copy(coef, coef_ref, sems.at[chunks])]
    copies[0].start()
    weights = product(across, raw)
    stacked = []
    for r in range(rounds):
        weight = weights[:, r * width : (r + 1) * width]
        if r == 0:
            weight = jnp.where(group == 0, -root * across, weight)
        upper = weight.astype(BF16)
        stacked.append(jnp.concatenate([upper, (weight - upper.astype(F32)).astype(BF16)], axis=1))
    weight = jnp.concatenate(stacked, axis=0)
    span = z_ref.shape[0] // chunks
    row = lax.broadcasted_iota(jnp.int32, (span, width), 0) % rounds
    for c in range(chunks):
        block = c * nblock // chunks
        at = slice(c * span, (c + 1) * span)
        acc = jnp.dot(lead_ref[at, :], weight, preferred_element_type=F32)
        acc = (acc[:, :width] + acc[:, width:]) * scale_ref[block, 0, 0]
        first = jnp.where(group == 0, 0.0, scale_ref[block, group, 0])
        factor = jnp.where(row == 0, first, scale_ref[block, group, 1])
        held[at, :] = (z_ref[at, :].astype(F32) * factor - acc).astype(BF16)
        copies.append(pltpu.make_async_copy(held.at[at, :], out_ref.at[at, :], sems.at[c]))
        copies[-1].start()
    for copy in copies:
        copy.wait()


def shards(snapshots, scales):
    points, _, rounds, width = snapshots.shape
    nblock = scales.shape[0]
    n_rows, n_cols = lax.axis_size("rows"), lax.axis_size("cols")
    root = math.sqrt(points * n_rows)
    long = points * rounds
    z = snapshots.reshape(long, width)
    group = lax.axis_index("cols")
    recv = partner(z, "cols", n_cols, 1)
    even = among_pairs(z, n_cols, group, 0)
    leads = (even, recv) if n_cols == 2 else (even, partner(even, "cols", n_cols, 1))
    phases = radices(n_rows)
    payload = width + 8
    params = pltpu.CompilerParams(vmem_limit_bytes=48 << 20)
    first, own = pl.pallas_call(
        functools.partial(split_kernel, rounds),
        out_shape=[jax.ShapeDtypeStruct((points, width), BF16)] * 2,
        in_specs=[VMEM],
        out_specs=[VMEM] * 2,
        scratch_shapes=[pltpu.VMEM((long, width), F32)],
        compiler_params=params,
        name="split",
    )(z)
    extra = () if n_cols == 2 else leads
    sent = pl.pallas_call(
        functools.partial(products_kernel, rounds, nblock),
        out_shape=[jax.ShapeDtypeStruct((payload, width), F32)] * 2,
        in_specs=[SMEM] + [VMEM] * (3 + len(extra)),
        out_specs=[VMEM] * 2,
        scratch_shapes=[pltpu.VMEM((long, width), F32), pltpu.VMEM((2 * width, width), F32)]
        + [pltpu.VMEM((long, width), F32)] * (len(extra) // 2),
        compiler_params=params,
        name="products",
    )(scales, first, own, recv, *extra)
    sums = sent[0]
    for step, (hop, base) in enumerate(phases):
        source = sent if step == 0 else [sums] * 2
        others = [partner(source[b % 2], "rows", n_rows, b * hop) for b in range(1, base)]
        if step == len(phases) - 1:
            lead = pl.pallas_call(
                functools.partial(spread_kernel, rounds),
                out_shape=jax.ShapeDtypeStruct((long, rounds * width), BF16),
                in_specs=[VMEM, VMEM],
                out_specs=VMEM,
                compiler_params=params,
                name="spread",
            )(*leads)
            *others, lead = lax.optimization_barrier((*others, lead))
        for other in others:
            sums = sums + other
    gathered = partner(sums, "rows", n_rows, 1)
    factored = pl.pallas_call(
        factor_kernel,
        out_shape=jax.ShapeDtypeStruct((2 * width, width), F32),
        in_specs=[VMEM],
        out_specs=VMEM,
        compiler_params=params,
        cost_estimate=pl.CostEstimate(flops=1 << 30, bytes_accessed=1 << 23, transcendentals=0),
        name="factor",
    )(sums)
    if n_cols > 2:
        shared = among_pairs(factored[:width], n_cols, group, 1)
        factored = jnp.concatenate([shared, factored[width:]], axis=0)
    crossed = partner(gathered, "cols", n_cols, 1)
    swapped = partner(factored, "cols", n_cols, 1)
    chunks = 2 * nblock
    coef, updated = pl.pallas_call(
        functools.partial(finish_kernel, rounds, nblock, root, chunks),
        out_shape=[
            jax.ShapeDtypeStruct((width * rounds, width), F32),
            jax.ShapeDtypeStruct((long, width), BF16),
        ],
        in_specs=[SMEM] + [VMEM] * 7,
        out_specs=[pl.BlockSpec(memory_space=pl.ANY)] * 2,
        scratch_shapes=[
            pltpu.VMEM((width, rounds * width), F32),
            pltpu.VMEM((width * rounds, width), F32),
            pltpu.VMEM((long, width), BF16),
            pltpu.SemaphoreType.DMA((chunks + 1,)),
        ],
        compiler_params=params,
        name="finish",
    )(scales, z, lead, factored, swapped, sums, gathered, crossed)
    return coef.reshape(width, 1, rounds, width), updated.reshape(snapshots.shape)


def solution(mesh):
    return jax.shard_map(
        shards,
        mesh=mesh,
        in_specs=(P("rows", "cols", None, None), P("rows", None, None)),
        out_specs=(P(None, "cols", None, None), P("rows", "cols", None, None)),
        check_vma=False,
    )
```

```python
import functools
import math

import jax
import jax.numpy as jnp
from jax import lax
from jax.experimental import pallas as pl
from jax.experimental.pallas import tpu as pltpu
from jax.sharding import PartitionSpec as P

F32 = jnp.float32
BF16 = jnp.bfloat16
VMEM = pl.BlockSpec(memory_space=pltpu.VMEM)


def partner(x, axis, count, offset):
    return lax.ppermute(x, axis, [(i, i ^ offset) for i in range(count)])


def radices(count):
    found = []
    stride = 1
    while stride < count:
        radix = 4 if (count // stride) % 4 == 0 else 2
        found.append((stride, radix))
        stride *= radix
    return found


def among_pairs(x, count, mine, root):
    stride = 2
    while stride < count:
        x = jnp.where(((mine ^ root) & stride) != 0, partner(x, "cols", count, stride), x)
        stride *= 2
    return x


def lanes(x, p):
    return jnp.broadcast_to(x[:, p : p + 1], x.shape)


def sublanes(x, j):
    return jnp.broadcast_to(x[j : j + 1, :], x.shape)


def thirds(x):
    high = x.astype(BF16)
    rest = x - high.astype(F32)
    middle = rest.astype(BF16)
    return high, middle, (rest - middle.astype(F32)).astype(BF16)


def product(left, right):
    return product_of_thirds(thirds(left), thirds(right))


def product_of_thirds(left, right):
    columns = right[0].shape[1]
    wide = jnp.concatenate(right[:2], axis=1)
    both = jnp.dot(
        jnp.concatenate(left[:2], axis=1), jnp.concatenate([wide, wide], axis=0), preferred_element_type=F32
    )
    small = jnp.dot(
        jnp.concatenate([left[0], left[2]], axis=1),
        jnp.concatenate([right[2], right[0]], axis=0),
        preferred_element_type=F32,
    )
    return (both[:, :columns] + both[:, columns:]) + small


def lower_inverse(rows, width):
    n = len(rows)
    rid = lax.broadcasted_iota(jnp.int32, (8, width), 0)
    cid = lax.broadcasted_iota(jnp.int32, (8, width), 1)
    done = []
    for k in range(n):
        base = 8 * k
        held = rows[k]
        columns = [lanes(held, base + j) for j in range(8)]
        inside = (cid >= base) & (cid < base + 8)
        eye = jnp.where(cid - base == rid, 1.0, 0.0).astype(F32)
        full = jnp.where(inside, eye, held)
        forward = full
        scale = jnp.zeros((8, width), F32)
        inverses = []
        for j in range(0, 8, 2):
            left, right = columns[j], columns[j + 1]
            a, b, c = sublanes(left, j), sublanes(right, j), sublanes(right, j + 1)
            det = a * c - b * b
            inverse, inverse_a = 1.0 / det, 1.0 / a
            pair = (rid == j) | (rid == j + 1)
            left, right = jnp.where(pair, 0.0, left), jnp.where(pair, 0.0, right)
            first, second = (left * c - right * b) * inverse, (right * a - left * b) * inverse
            for m in range(j + 2, 8):
                columns[m] = columns[m] - (first * sublanes(columns[m], j) + second * sublanes(columns[m], j + 1))
            full = full - (first * sublanes(full, j) + second * sublanes(full, j + 1))
            below = rid > j + 1
            first = jnp.where(below, first, jnp.where(rid == j + 1, b * inverse_a, 0.0))
            second = jnp.where(below, second, 0.0)
            forward = forward - (first * sublanes(forward, j) + second * sublanes(forward, j + 1))
            scale = jnp.where(rid == j, lax.rsqrt(a), jnp.where(rid == j + 1, lax.rsqrt(det * inverse_a), scale))
            inverses.append((a * inverse, b * inverse, c * inverse))
        done.append(jnp.where(cid <= rid + base, forward * scale, 0.0))
        if k + 1 == n:
            break
        spread = []
        for j, (a, b, c) in enumerate(inverses):
            above, under = sublanes(full, 2 * j), sublanes(full, 2 * j + 1)
            spread += [above * c - under * b, under * a - above * b]
        terms = [lanes(rows[k + 1], base + j) * spread[j] for j in range(8)]
        while len(terms) > 1:
            terms = [terms[q] + terms[q + 1] for q in range(0, len(terms), 2)]
        rows[k + 1] = jnp.where(inside, 0.0, rows[k + 1]) - terms[0]
        if k + 2 == n:
            continue
        solved = jnp.zeros((8, width), F32)
        for j in range(8):
            solved = jnp.where(rid == j, spread[j], solved)
        far = jnp.concatenate(rows[k + 2 :], axis=0)
        column = lax.broadcasted_iota(jnp.int32, far.shape, 1)
        within = (column >= base) & (column < base + 8)
        placed = []
        for third in thirds(solved):
            blocks = [jnp.zeros((base, width), F32)] if base else []
            blocks += [third.astype(F32), jnp.zeros((width - base - 8, width), F32)]
            placed.append(jnp.concatenate(blocks, axis=0).astype(BF16))
        update = product_of_thirds(thirds(jnp.where(within, far, 0.0)), placed)
        far = jnp.where(within, 0.0, far) - update
        for i in range(k + 2, n):
            rows[i] = far[8 * (i - k - 2) : 8 * (i - k - 1)]
    return done


def pack(gram):
    width = gram.shape[0]
    half = width // 2
    row = lax.broadcasted_iota(jnp.int32, (half, width), 0)
    col = lax.broadcasted_iota(jnp.int32, (half, width), 1)
    turned = pltpu.roll(gram[half:, :], half, 1)
    both = jnp.where((col < half) & (row < col), turned, gram[:half, :])
    diagonal = jnp.sum(jnp.where(row + half == col, gram[half:, :], 0.0), axis=0, keepdims=True)
    return jnp.concatenate([both, jnp.broadcast_to(diagonal, (8, width))], axis=0)


def unpack(packed):
    width = packed.shape[1]
    half = width // 2
    row = lax.broadcasted_iota(jnp.int32, (width, width), 0)
    col = lax.broadcasted_iota(jnp.int32, (width, width), 1)
    both = packed[:half, :]
    square = jnp.concatenate([both, pltpu.roll(both, half, 1)], axis=0)
    direct = ((row < half) & ((col >= half) | (col <= row))) | ((row >= half) & (col >= half) & (col > row))
    gram = jnp.where(direct, square, square.T)
    return jnp.where((row == col) & (row >= half), jnp.broadcast_to(packed[half : half + 1, :], gram.shape), gram)


def leading(even_ref, odd_ref):
    return jnp.where(lax.axis_index("cols") % 2 == 0, even_ref[...], odd_ref[...])


def tall(tile, rows):
    return jnp.broadcast_to(tile[None], (rows // 8, *tile.shape)).reshape(rows, tile.shape[1])


def split_kernel(rounds, nblock, scale_ref, z_ref, first_ref, own_ref, factor_ref, wide):
    group = lax.axis_index("cols")
    odd = group % 2
    width = z_ref.shape[1]
    points = z_ref.shape[0] // rounds
    row = lax.broadcasted_iota(jnp.int32, (8, width), 0)
    for b in range(nblock):
        lead = jnp.broadcast_to(scale_ref[b, 0:1, 0:1], (8, width))
        mine = scale_ref[b, pl.ds(group, 1), :]
        theirs = scale_ref[b, pl.ds(group + 1 - 2 * odd, 1), :]
        mine, theirs = [[jnp.broadcast_to(x[:, r : r + 1], (8, width)) for r in range(2)] for x in (mine, theirs)]
        factor_ref[4 * b] = lead * jnp.where(odd == 1, theirs[0], theirs[1])
        factor_ref[4 * b + 1] = lead * jnp.where(odd == 1, mine[0], mine[1])
        factor_ref[4 * b + 2] = lead
        factor_ref[4 * b + 3] = jnp.where(row % rounds == 0, jnp.where(group == 0, 0.0, mine[0]), mine[1])
    wide[...] = z_ref[...].astype(F32)
    first = wide[pl.ds(0, points, stride=rounds), :].astype(BF16)
    last = wide[pl.ds(1, points, stride=rounds), :].astype(BF16)
    first_ref[...] = first
    own_ref[...] = jnp.where(odd == 1, first, last)


def products_kernel(rounds, nblock, factor_ref, first_ref, own_ref, recv_ref, *rest):
    lead_ref = rest[:-4] if len(rest) == 4 else (*rest[:2], rest[-1])
    same_ref, other_ref, wide, cross = rest if len(rest) == 4 else rest[2:-1]
    group = lax.axis_index("cols")
    odd = group % 2
    digit = lax.axis_index("rows") % 2
    width = recv_ref.shape[1]
    points = own_ref.shape[0] // nblock
    half = width // 2
    height = half + 8
    wide[...] = recv_ref[...].astype(F32)
    if lead_ref:
        lead_ref[2][...] = leading(*lead_ref[:2]).astype(F32)
    out = jnp.zeros((width, 2 * width), F32)
    for b in range(nblock):
        at = slice(b * points, (b + 1) * points)
        start = b * points * rounds
        theirs = wide[pl.ds(start + 1 - odd, points, stride=rounds), :].astype(BF16)
        if lead_ref:
            panel = lead_ref[2][pl.ds(start, points, stride=rounds), :].astype(BF16)
        else:
            panel = jnp.where(odd == 1, theirs, first_ref[at, :])
        block = lax.dot_general(
            panel, jnp.concatenate([theirs, own_ref[at, :]], axis=1), (((0,), (0,)), ((), ())), preferred_element_type=F32
        )
        left = block[:, :width] * tall(factor_ref[4 * b], width)
        right = block[:, width:] * tall(factor_ref[4 * b + 1], width)
        out = out + jnp.concatenate([left, right], axis=1)
    packed = pack(out[:, :width])
    cross[:width, :] = out[:, :width]
    cross[width:, :] = out[:, width:]
    for ref, place in ((same_ref, digit), (other_ref, 1 - digit)):
        theirs = cross[pl.ds(pl.multiple_of(place * half, half), half), :]
        ref[:half, :] = jnp.where(group == 1, packed[:half, :], theirs)
        ref[half:height, :] = packed[half:, :]
        ref[height:, :] = cross[pl.ds(pl.multiple_of(width + place * half, half), half), :]


def spread_kernel(rounds, even_ref, odd_ref, out_ref):
    width = even_ref.shape[1]
    rows = lax.broadcasted_iota(jnp.int32, even_ref.shape, 0) % rounds
    lead = leading(even_ref, odd_ref).astype(F32)
    for r in range(rounds):
        moved = lead if r == 0 else pltpu.roll(lead, r, 0)
        out_ref[:, r * width : (r + 1) * width] = jnp.where(rows == r, moved, 0.0).astype(BF16)


def factor_kernel(sums_ref, out_ref):
    width = sums_ref.shape[1]
    height = width // 2 + 8
    group = lax.axis_index("cols")

    @pl.when(group == 1)
    def _():
        gram = unpack(sums_ref[:height, :])
        out_ref[width:, :] = gram
        rows = [gram[8 * i : 8 * i + 8, :] for i in range(width // 8)]
        for i, row in enumerate(lower_inverse(rows, width)):
            out_ref[8 * i : 8 * i + 8, :] = row

    @pl.when(group != 1)
    def _():
        out_ref[:width, :] = jnp.zeros((width, width), F32)
        out_ref[width : width + height, :] = sums_ref[:height, :]
        out_ref[width + height :, :] = jnp.zeros((width - height, width), F32)


def finish_kernel(
    rounds, nblock, root, chunks, factor_ref, z_ref, lead_ref, kept_ref, recv_ref, same_ref, other_ref, across_ref,
    coef_ref, out_ref, cross, coef, held, sems,
):
    group = lax.axis_index("cols")
    odd = group % 2 == 1
    digit = lax.axis_index("rows") % 2
    width = z_ref.shape[1]
    half = width // 2
    height = half + 8
    for place, own_ref, theirs in ((digit, same_ref, recv_ref[width : width + half, :]), (1 - digit, other_ref, across_ref[:half, :])):
        at = pl.ds(pl.multiple_of(place * half, half), half)
        gram = recv_ref[pl.ds(pl.multiple_of(width + place * half, half), half), :]
        mine = own_ref[height:, :]
        theirs = jnp.where(group == 0, gram, theirs)
        cross[at, :width] = jnp.where(odd, mine, theirs)
        cross[at, width:] = jnp.where(odd, theirs, mine)
    inverse = jnp.where(odd, kept_ref[:width, :], recv_ref[:width, :])
    across = inverse.T
    raw = product(inverse, cross[...])
    for r in range(rounds):
        coef[pl.ds(r, width, stride=rounds), :] = raw[:, r * width : (r + 1) * width] * (1.0 / root)
    copies = [pltpu.make_async_copy(coef, coef_ref, sems.at[chunks])]
    copies[0].start()
    weights = product(across, raw)
    stacked = []
    for r in range(rounds):
        weight = weights[:, r * width : (r + 1) * width]
        if r == 0:
            weight = jnp.where(group == 0, -root * across, weight)
        upper = weight.astype(BF16)
        stacked.append(jnp.concatenate([upper, (weight - upper.astype(F32)).astype(BF16)], axis=1))
    weight = jnp.concatenate(stacked, axis=0)
    span = z_ref.shape[0] // chunks
    for c in range(chunks):
        block = c * nblock // chunks
        at = slice(c * span, (c + 1) * span)
        acc = jnp.dot(lead_ref[at, :], weight, preferred_element_type=F32)
        acc = (acc[:, :width] + acc[:, width:]) * tall(factor_ref[4 * block + 2], span)
        factor = tall(factor_ref[4 * block + 3], span)
        held[at, :] = (z_ref[at, :].astype(F32) * factor - acc).astype(BF16)
        copies.append(pltpu.make_async_copy(held.at[at, :], out_ref.at[at, :], sems.at[c]))
        copies[-1].start()
    for copy in copies:
        copy.wait()


def shards(snapshots, scales):
    points, _, rounds, width = snapshots.shape
    nblock = scales.shape[0]
    n_rows, n_cols = lax.axis_size("rows"), lax.axis_size("cols")
    root = math.sqrt(points * n_rows)
    long = points * rounds
    z = snapshots.reshape(long, width)
    group = lax.axis_index("cols")
    recv = partner(z, "cols", n_cols, 1)
    even = among_pairs(z, n_cols, group, 0)
    leads = (even, recv) if n_cols == 2 else (even, partner(even, "cols", n_cols, 1))
    phases = radices(n_rows)
    payload = width + 8
    params = pltpu.CompilerParams(vmem_limit_bytes=48 << 20)
    first, own, factors = pl.pallas_call(
        functools.partial(split_kernel, rounds, nblock),
        out_shape=[jax.ShapeDtypeStruct((points, width), BF16)] * 2 + [jax.ShapeDtypeStruct((4 * nblock, 8, width), F32)],
        in_specs=[VMEM] * 2,
        out_specs=[VMEM] * 3,
        scratch_shapes=[pltpu.VMEM((long, width), F32)],
        compiler_params=params,
        name="split",
    )(scales, z)
    extra = () if n_cols == 2 else leads
    sent = pl.pallas_call(
        functools.partial(products_kernel, rounds, nblock),
        out_shape=[jax.ShapeDtypeStruct((payload, width), F32)] * 2,
        in_specs=[VMEM] * (4 + len(extra)),
        out_specs=[VMEM] * 2,
        scratch_shapes=[pltpu.VMEM((long, width), F32), pltpu.VMEM((2 * width, width), F32)]
        + [pltpu.VMEM((long, width), F32)] * (len(extra) // 2),
        compiler_params=params,
        name="products",
    )(factors, first, own, recv, *extra)
    sums = sent[0]
    for step, (hop, base) in enumerate(phases):
        source = sent if step == 0 else [sums] * 2
        others = [partner(source[b % 2], "rows", n_rows, b * hop) for b in range(1, base)]
        if step == len(phases) - 1:
            lead = pl.pallas_call(
                functools.partial(spread_kernel, rounds),
                out_shape=jax.ShapeDtypeStruct((long, rounds * width), BF16),
                in_specs=[VMEM, VMEM],
                out_specs=VMEM,
                compiler_params=params,
                name="spread",
            )(*leads)
            *others, lead = lax.optimization_barrier((*others, lead))
        for other in others:
            sums = sums + other
    gathered = partner(sums, "rows", n_rows, 1)
    factored = pl.pallas_call(
        factor_kernel,
        out_shape=jax.ShapeDtypeStruct((2 * width, width), F32),
        in_specs=[VMEM],
        out_specs=VMEM,
        compiler_params=params,
        cost_estimate=pl.CostEstimate(flops=1 << 30, bytes_accessed=1 << 23, transcendentals=0),
        name="factor",
    )(sums)
    if n_cols > 2:
        shared = among_pairs(factored[:width], n_cols, group, 1)
        factored = jnp.concatenate([shared, factored[width:]], axis=0)
    crossed = partner(gathered, "cols", n_cols, 1)
    swapped = partner(factored, "cols", n_cols, 1)
    chunks = 2 * nblock
    coef, updated = pl.pallas_call(
        functools.partial(finish_kernel, rounds, nblock, root, chunks),
        out_shape=[
            jax.ShapeDtypeStruct((width * rounds, width), F32),
            jax.ShapeDtypeStruct((long, width), BF16),
        ],
        in_specs=[VMEM] * 8,
        out_specs=[pl.BlockSpec(memory_space=pl.ANY)] * 2,
        scratch_shapes=[
            pltpu.VMEM((width, rounds * width), F32),
            pltpu.VMEM((width * rounds, width), F32),
            pltpu.VMEM((long, width), BF16),
            pltpu.SemaphoreType.DMA((chunks + 1,)),
        ],
        compiler_params=params,
        name="finish",
    )(factors, z, lead, factored, swapped, sums, gathered, crossed)
    return coef.reshape(width, 1, rounds, width), updated.reshape(snapshots.shape)


def solution(mesh):
    return jax.shard_map(
        shards,
        mesh=mesh,
        in_specs=(P("rows", "cols", None, None), P("rows", None, None)),
        out_specs=(P(None, "cols", None, None), P("rows", "cols", None, None)),
        check_vma=False,
    )
```

```python
import functools
import math

import jax
import jax.numpy as jnp
from jax import lax
from jax.experimental import pallas as pl
from jax.experimental.pallas import tpu as pltpu
from jax.sharding import PartitionSpec as P

F32 = jnp.float32
BF16 = jnp.bfloat16
VMEM = pl.BlockSpec(memory_space=pltpu.VMEM)


def partner(x, axis, count, offset):
    return lax.ppermute(x, axis, [(i, i ^ offset) for i in range(count)])


def radices(count):
    found = []
    stride = 1
    while stride < count:
        radix = 4 if (count // stride) % 4 == 0 else 2
        found.append((stride, radix))
        stride *= radix
    return found


def order(phases, parity):
    if parity == 0 and len({radix for _, radix in phases}) == 1:
        return phases[::-1]
    return phases


def hop(x, n_rows, n_cols, offset, turn=0):
    pairs = []
    for row in range(n_rows):
        for col in range(n_cols):
            pairs.append((row * n_cols + col, (row ^ offset(col % 2)) * n_cols + (col ^ turn)))
    return lax.ppermute(x, ("rows", "cols"), pairs)


def half_digit(phases, parity):
    even, odd = [(lax.axis_index("rows") // order(phases, p)[0][0]) % 2 for p in range(2)]
    return jnp.where(parity == 0, even, odd)


def among_pairs(x, count, mine, root):
    stride = 2
    while stride < count:
        x = jnp.where(((mine ^ root) & stride) != 0, partner(x, "cols", count, stride), x)
        stride *= 2
    return x


def lanes(x, p):
    return jnp.broadcast_to(x[:, p : p + 1], x.shape)


def sublanes(x, j):
    return jnp.broadcast_to(x[j : j + 1, :], x.shape)


def thirds(x):
    high = x.astype(BF16)
    rest = x - high.astype(F32)
    middle = rest.astype(BF16)
    return high, middle, (rest - middle.astype(F32)).astype(BF16)


def product(left, right):
    return product_of_thirds(thirds(left), thirds(right))


def product_of_thirds(left, right):
    columns = right[0].shape[1]
    wide = jnp.concatenate(right[:2], axis=1)
    both = jnp.dot(
        jnp.concatenate(left[:2], axis=1), jnp.concatenate([wide, wide], axis=0), preferred_element_type=F32
    )
    small = jnp.dot(
        jnp.concatenate([left[0], left[2]], axis=1),
        jnp.concatenate([right[2], right[0]], axis=0),
        preferred_element_type=F32,
    )
    return (both[:, :columns] + both[:, columns:]) + small


def lower_inverse(rows, width):
    n = len(rows)
    rid = lax.broadcasted_iota(jnp.int32, (8, width), 0)
    cid = lax.broadcasted_iota(jnp.int32, (8, width), 1)
    done = []
    for k in range(n):
        base = 8 * k
        held = rows[k]
        columns = [lanes(held, base + j) for j in range(8)]
        inside = (cid >= base) & (cid < base + 8)
        eye = jnp.where(cid - base == rid, 1.0, 0.0).astype(F32)
        full = jnp.where(inside, eye, held)
        forward = full
        scale = jnp.zeros((8, width), F32)
        inverses = []
        for j in range(0, 8, 2):
            left, right = columns[j], columns[j + 1]
            a, b, c = sublanes(left, j), sublanes(right, j), sublanes(right, j + 1)
            det = a * c - b * b
            inverse, inverse_a = 1.0 / det, 1.0 / a
            pair = (rid == j) | (rid == j + 1)
            left, right = jnp.where(pair, 0.0, left), jnp.where(pair, 0.0, right)
            first, second = (left * c - right * b) * inverse, (right * a - left * b) * inverse
            for m in range(j + 2, 8):
                columns[m] = columns[m] - (first * sublanes(columns[m], j) + second * sublanes(columns[m], j + 1))
            full = full - (first * sublanes(full, j) + second * sublanes(full, j + 1))
            below = rid > j + 1
            first = jnp.where(below, first, jnp.where(rid == j + 1, b * inverse_a, 0.0))
            second = jnp.where(below, second, 0.0)
            forward = forward - (first * sublanes(forward, j) + second * sublanes(forward, j + 1))
            scale = jnp.where(rid == j, lax.rsqrt(a), jnp.where(rid == j + 1, lax.rsqrt(det * inverse_a), scale))
            inverses.append((a * inverse, b * inverse, c * inverse))
        done.append(jnp.where(cid <= rid + base, forward * scale, 0.0))
        if k + 1 == n:
            break
        spread = []
        for j, (a, b, c) in enumerate(inverses):
            above, under = sublanes(full, 2 * j), sublanes(full, 2 * j + 1)
            spread += [above * c - under * b, under * a - above * b]
        terms = [lanes(rows[k + 1], base + j) * spread[j] for j in range(8)]
        while len(terms) > 1:
            terms = [terms[q] + terms[q + 1] for q in range(0, len(terms), 2)]
        rows[k + 1] = jnp.where(inside, 0.0, rows[k + 1]) - terms[0]
        if k + 2 == n:
            continue
        solved = jnp.zeros((8, width), F32)
        for j in range(8):
            solved = jnp.where(rid == j, spread[j], solved)
        far = jnp.concatenate(rows[k + 2 :], axis=0)
        column = lax.broadcasted_iota(jnp.int32, far.shape, 1)
        within = (column >= base) & (column < base + 8)
        placed = []
        for third in thirds(solved):
            blocks = [jnp.zeros((base, width), F32)] if base else []
            blocks += [third.astype(F32), jnp.zeros((width - base - 8, width), F32)]
            placed.append(jnp.concatenate(blocks, axis=0).astype(BF16))
        update = product_of_thirds(thirds(jnp.where(within, far, 0.0)), placed)
        far = jnp.where(within, 0.0, far) - update
        for i in range(k + 2, n):
            rows[i] = far[8 * (i - k - 2) : 8 * (i - k - 1)]
    return done


def pack(gram):
    width = gram.shape[0]
    half = width // 2
    row = lax.broadcasted_iota(jnp.int32, (half, width), 0)
    col = lax.broadcasted_iota(jnp.int32, (half, width), 1)
    turned = pltpu.roll(gram[half:, :], half, 1)
    both = jnp.where((col < half) & (row < col), turned, gram[:half, :])
    diagonal = jnp.sum(jnp.where(row + half == col, gram[half:, :], 0.0), axis=0, keepdims=True)
    return jnp.concatenate([both, jnp.broadcast_to(diagonal, (8, width))], axis=0)


def unpack(packed):
    width = packed.shape[1]
    half = width // 2
    row = lax.broadcasted_iota(jnp.int32, (width, width), 0)
    col = lax.broadcasted_iota(jnp.int32, (width, width), 1)
    both = packed[:half, :]
    square = jnp.concatenate([both, pltpu.roll(both, half, 1)], axis=0)
    direct = ((row < half) & ((col >= half) | (col <= row))) | ((row >= half) & (col >= half) & (col > row))
    gram = jnp.where(direct, square, square.T)
    return jnp.where((row == col) & (row >= half), jnp.broadcast_to(packed[half : half + 1, :], gram.shape), gram)


def leading(even_ref, odd_ref):
    return jnp.where(lax.axis_index("cols") % 2 == 0, even_ref[...], odd_ref[...])


def tall(tile, rows):
    return jnp.broadcast_to(tile[None], (rows // 8, *tile.shape)).reshape(rows, tile.shape[1])


def split_kernel(rounds, nblock, scale_ref, z_ref, first_ref, own_ref, factor_ref, wide):
    group = lax.axis_index("cols")
    odd = group % 2
    width = z_ref.shape[1]
    points = z_ref.shape[0] // rounds
    row = lax.broadcasted_iota(jnp.int32, (8, width), 0)
    for b in range(nblock):
        lead = jnp.broadcast_to(scale_ref[b, 0:1, 0:1], (8, width))
        mine = scale_ref[b, pl.ds(group, 1), :]
        theirs = scale_ref[b, pl.ds(group + 1 - 2 * odd, 1), :]
        mine, theirs = [[jnp.broadcast_to(x[:, r : r + 1], (8, width)) for r in range(2)] for x in (mine, theirs)]
        factor_ref[4 * b] = lead * jnp.where(odd == 1, theirs[0], theirs[1])
        factor_ref[4 * b + 1] = lead * jnp.where(odd == 1, mine[0], mine[1])
        factor_ref[4 * b + 2] = lead
        factor_ref[4 * b + 3] = jnp.where(row % rounds == 0, jnp.where(group == 0, 0.0, mine[0]), mine[1])
    wide[...] = z_ref[...].astype(F32)
    first = wide[pl.ds(0, points, stride=rounds), :].astype(BF16)
    last = wide[pl.ds(1, points, stride=rounds), :].astype(BF16)
    first_ref[...] = first
    own_ref[...] = jnp.where(odd == 1, first, last)


def products_kernel(rounds, nblock, phases, factor_ref, first_ref, own_ref, recv_ref, *rest):
    lead_ref = rest[:-4] if len(rest) == 4 else (*rest[:2], rest[-1])
    same_ref, other_ref, wide, cross = rest if len(rest) == 4 else rest[2:-1]
    group = lax.axis_index("cols")
    odd = group % 2
    digit = half_digit(phases, odd)
    width = recv_ref.shape[1]
    points = own_ref.shape[0] // nblock
    half = width // 2
    height = half + 8
    wide[...] = recv_ref[...].astype(F32)
    if lead_ref:
        lead_ref[2][...] = leading(*lead_ref[:2]).astype(F32)
    out = jnp.zeros((width, 2 * width), F32)
    for b in range(nblock):
        at = slice(b * points, (b + 1) * points)
        start = b * points * rounds
        theirs = wide[pl.ds(start + 1 - odd, points, stride=rounds), :].astype(BF16)
        if lead_ref:
            panel = lead_ref[2][pl.ds(start, points, stride=rounds), :].astype(BF16)
        else:
            panel = jnp.where(odd == 1, theirs, first_ref[at, :])
        block = lax.dot_general(
            panel, jnp.concatenate([theirs, own_ref[at, :]], axis=1), (((0,), (0,)), ((), ())), preferred_element_type=F32
        )
        left = block[:, :width] * tall(factor_ref[4 * b], width)
        right = block[:, width:] * tall(factor_ref[4 * b + 1], width)
        out = out + jnp.concatenate([left, right], axis=1)
    packed = pack(out[:, :width])
    cross[:width, :] = out[:, :width]
    cross[width:, :] = out[:, width:]
    for ref, place in ((same_ref, digit), (other_ref, 1 - digit)):
        theirs = cross[pl.ds(pl.multiple_of(place * half, half), half), :]
        ref[:half, :] = jnp.where(group == 1, packed[:half, :], theirs)
        ref[half:height, :] = packed[half:, :]
        ref[height:, :] = cross[pl.ds(pl.multiple_of(width + place * half, half), half), :]


def spread_kernel(rounds, even_ref, odd_ref, out_ref):
    width = even_ref.shape[1]
    rows = lax.broadcasted_iota(jnp.int32, even_ref.shape, 0) % rounds
    lead = leading(even_ref, odd_ref).astype(F32)
    for r in range(rounds):
        moved = lead if r == 0 else pltpu.roll(lead, r, 0)
        out_ref[:, r * width : (r + 1) * width] = jnp.where(rows == r, moved, 0.0).astype(BF16)


def factor_kernel(sums_ref, inverse_ref, block_ref):
    width = sums_ref.shape[1]
    height = width // 2 + 8
    group = lax.axis_index("cols")

    @pl.when(group == 1)
    def _():
        gram = unpack(sums_ref[:height, :])
        block_ref[...] = gram
        rows = [gram[8 * i : 8 * i + 8, :] for i in range(width // 8)]
        for i, row in enumerate(lower_inverse(rows, width)):
            inverse_ref[8 * i : 8 * i + 8, :] = row

    @pl.when(group != 1)
    def _():
        inverse_ref[...] = jnp.zeros((width, width), F32)
        block_ref[:height, :] = sums_ref[:height, :]
        block_ref[height:, :] = jnp.zeros((width - height, width), F32)


def finish_kernel(
    rounds, nblock, phases, root, chunks, factor_ref, z_ref, lead_ref, kept_ref, recv_ref, same_ref, gathered_ref, block_ref, across_ref,
    coef_ref, out_ref, mine, theirs, coef, held, sems,
):
    group = lax.axis_index("cols")
    odd = group % 2 == 1
    width = z_ref.shape[1]
    half = width // 2
    height = half + 8
    own_digit, pair_digit = half_digit(phases, group % 2), half_digit(phases, 1 - group % 2)
    for own_rows, pair_rows, other in ((same_ref[height:, :], block_ref[:half, :], 0), (gathered_ref[height:, :], across_ref[:half, :], 1)):
        mine[pl.ds(pl.multiple_of((own_digit ^ other) * half, half), half), :] = own_rows
        theirs[pl.ds(pl.multiple_of((pair_digit ^ other) * half, half), half), :] = pair_rows
    own_block = mine[...]
    pair_block = jnp.where(group == 0, block_ref[...], theirs[...])
    cross = jnp.concatenate([jnp.where(odd, own_block, pair_block), jnp.where(odd, pair_block, own_block)], axis=1)
    inverse = jnp.where(odd, kept_ref[...], recv_ref[...])
    across = inverse.T
    raw = product(inverse, cross)
    for r in range(rounds):
        coef[pl.ds(r, width, stride=rounds), :] = raw[:, r * width : (r + 1) * width] * (1.0 / root)
    copies = [pltpu.make_async_copy(coef, coef_ref, sems.at[chunks])]
    copies[0].start()
    weights = product(across, raw)
    stacked = []
    for r in range(rounds):
        weight = weights[:, r * width : (r + 1) * width]
        if r == 0:
            weight = jnp.where(group == 0, -root * across, weight)
        upper = weight.astype(BF16)
        stacked.append(jnp.concatenate([upper, (weight - upper.astype(F32)).astype(BF16)], axis=1))
    weight = jnp.concatenate(stacked, axis=0)
    span = z_ref.shape[0] // chunks
    for c in range(chunks):
        block = c * nblock // chunks
        at = slice(c * span, (c + 1) * span)
        acc = jnp.dot(lead_ref[at, :], weight, preferred_element_type=F32)
        acc = (acc[:, :width] + acc[:, width:]) * tall(factor_ref[4 * block + 2], span)
        factor = tall(factor_ref[4 * block + 3], span)
        held[at, :] = (z_ref[at, :].astype(F32) * factor - acc).astype(BF16)
        copies.append(pltpu.make_async_copy(held.at[at, :], out_ref.at[at, :], sems.at[c]))
        copies[-1].start()
    for copy in copies:
        copy.wait()


def shards(snapshots, scales):
    points, _, rounds, width = snapshots.shape
    nblock = scales.shape[0]
    n_rows, n_cols = lax.axis_size("rows"), lax.axis_size("cols")
    root = math.sqrt(points * n_rows)
    long = points * rounds
    z = snapshots.reshape(long, width)
    group = lax.axis_index("cols")
    recv = partner(z, "cols", n_cols, 1)
    even = among_pairs(z, n_cols, group, 0)
    leads = (even, recv) if n_cols == 2 else (even, partner(even, "cols", n_cols, 1))
    phases = radices(n_rows)
    payload = width + 8
    params = pltpu.CompilerParams(vmem_limit_bytes=48 << 20)
    first, own, factors = pl.pallas_call(
        functools.partial(split_kernel, rounds, nblock),
        out_shape=[jax.ShapeDtypeStruct((points, width), BF16)] * 2 + [jax.ShapeDtypeStruct((4 * nblock, 8, width), F32)],
        in_specs=[VMEM] * 2,
        out_specs=[VMEM] * 3,
        scratch_shapes=[pltpu.VMEM((long, width), F32)],
        compiler_params=params,
        name="split",
    )(scales, z)
    extra = () if n_cols == 2 else leads
    sent = pl.pallas_call(
        functools.partial(products_kernel, rounds, nblock, phases),
        out_shape=[jax.ShapeDtypeStruct((payload, width), F32)] * 2,
        in_specs=[VMEM] * (4 + len(extra)),
        out_specs=[VMEM] * 2,
        scratch_shapes=[pltpu.VMEM((long, width), F32), pltpu.VMEM((2 * width, width), F32)]
        + [pltpu.VMEM((long, width), F32)] * (len(extra) // 2),
        compiler_params=params,
        name="products",
    )(factors, first, own, recv, *extra)
    sums = sent[0]
    for step, (_, base) in enumerate(phases):
        source = sent if step == 0 else [sums] * 2
        others = [
            hop(source[b % 2], n_rows, n_cols, lambda parity: b * order(phases, parity)[step][0]) for b in range(1, base)
        ]
        if step == len(phases) - 1:
            lead = pl.pallas_call(
                functools.partial(spread_kernel, rounds),
                out_shape=jax.ShapeDtypeStruct((long, rounds * width), BF16),
                in_specs=[VMEM, VMEM],
                out_specs=VMEM,
                compiler_params=params,
                name="spread",
            )(*leads)
            *others, lead = lax.optimization_barrier((*others, lead))
        for other in others:
            sums = sums + other
    height = width // 2 + 8
    beside = lambda parity: order(phases, parity)[0][0]
    gathered = hop(sums, n_rows, n_cols, beside)
    inverse, block = pl.pallas_call(
        factor_kernel,
        out_shape=[jax.ShapeDtypeStruct((width, width), F32)] * 2,
        in_specs=[VMEM],
        out_specs=[VMEM] * 2,
        compiler_params=params,
        cost_estimate=pl.CostEstimate(flops=1 << 30, bytes_accessed=1 << 23, transcendentals=0),
        name="factor",
    )(sums)
    inverse = among_pairs(inverse, n_cols, group, 1)
    swapped = partner(inverse, "cols", n_cols, 1)
    blocks = partner(block, "cols", n_cols, 1)
    crossed = hop(block[:height], n_rows, n_cols, beside, 1)
    chunks = 2 * nblock
    coef, updated = pl.pallas_call(
        functools.partial(finish_kernel, rounds, nblock, phases, root, chunks),
        out_shape=[
            jax.ShapeDtypeStruct((width * rounds, width), F32),
            jax.ShapeDtypeStruct((long, width), BF16),
        ],
        in_specs=[VMEM] * 9,
        out_specs=[pl.BlockSpec(memory_space=pl.ANY)] * 2,
        scratch_shapes=[
            pltpu.VMEM((width, width), F32),
            pltpu.VMEM((width, width), F32),
            pltpu.VMEM((width * rounds, width), F32),
            pltpu.VMEM((long, width), BF16),
            pltpu.SemaphoreType.DMA((chunks + 1,)),
        ],
        compiler_params=params,
        name="finish",
    )(factors, z, lead, inverse, swapped, sums, gathered, blocks, crossed)
    return coef.reshape(width, 1, rounds, width), updated.reshape(snapshots.shape)


def solution(mesh):
    return jax.shard_map(
        shards,
        mesh=mesh,
        in_specs=(P("rows", "cols", None, None), P("rows", None, None)),
        out_specs=(P(None, "cols", None, None), P("rows", "cols", None, None)),
        check_vma=False,
    )
```

```python
import functools
import math

import jax
import jax.numpy as jnp
from jax import lax
from jax.experimental import pallas as pl
from jax.experimental.pallas import tpu as pltpu
from jax.sharding import PartitionSpec as P

F32 = jnp.float32
BF16 = jnp.bfloat16
VMEM = pl.BlockSpec(memory_space=pltpu.VMEM)


def partner(x, axis, count, offset):
    return lax.ppermute(x, axis, [(i, i ^ offset) for i in range(count)])


def radices(count):
    found = []
    stride = 1
    while stride < count:
        radix = 4 if (count // stride) % 4 == 0 else 2
        found.append((stride, radix))
        stride *= radix
    return found


def order(phases, parity):
    if parity == 0 and len({radix for _, radix in phases}) == 1:
        return phases[::-1]
    return phases


def hop(x, n_rows, n_cols, offset, turn=0):
    pairs = []
    for row in range(n_rows):
        for col in range(n_cols):
            pairs.append((row * n_cols + col, (row ^ offset(col % 2)) * n_cols + (col ^ turn)))
    return lax.ppermute(x, ("rows", "cols"), pairs)


def half_digit(phases, parity):
    even, odd = [(lax.axis_index("rows") // order(phases, p)[0][0]) % 2 for p in range(2)]
    return jnp.where(parity == 0, even, odd)


def among_pairs(x, count, mine, root):
    stride = 2
    while stride < count:
        x = jnp.where(((mine ^ root) & stride) != 0, partner(x, "cols", count, stride), x)
        stride *= 2
    return x


def lanes(x, p):
    return jnp.broadcast_to(x[:, p : p + 1], x.shape)


def sublanes(x, j):
    return jnp.broadcast_to(x[j : j + 1, :], x.shape)


def thirds(x):
    high = x.astype(BF16)
    rest = x - high.astype(F32)
    middle = rest.astype(BF16)
    return high, middle, (rest - middle.astype(F32)).astype(BF16)


def product(left, right):
    return product_of_thirds(thirds(left), thirds(right))


def product_of_thirds(left, right):
    columns = right[0].shape[1]
    wide = jnp.concatenate(right[:2], axis=1)
    both = jnp.dot(
        jnp.concatenate(left[:2], axis=1), jnp.concatenate([wide, wide], axis=0), preferred_element_type=F32
    )
    small = jnp.dot(
        jnp.concatenate([left[0], left[2]], axis=1),
        jnp.concatenate([right[2], right[0]], axis=0),
        preferred_element_type=F32,
    )
    return (both[:, :columns] + both[:, columns:]) + small


def lower_inverse(rows, width):
    n = len(rows)
    rid = lax.broadcasted_iota(jnp.int32, (8, width), 0)
    cid = lax.broadcasted_iota(jnp.int32, (8, width), 1)
    done = []
    for k in range(n):
        base = 8 * k
        held = rows[k]
        columns = [lanes(held, base + j) for j in range(8)]
        inside = (cid >= base) & (cid < base + 8)
        eye = jnp.where(cid - base == rid, 1.0, 0.0).astype(F32)
        full = jnp.where(inside, eye, held)
        forward = full
        scale = jnp.zeros((8, width), F32)
        inverses = []
        for j in range(0, 8, 2):
            left, right = columns[j], columns[j + 1]
            a, b, c = sublanes(left, j), sublanes(right, j), sublanes(right, j + 1)
            det = a * c - b * b
            inverse, inverse_a = 1.0 / det, 1.0 / a
            pair = (rid == j) | (rid == j + 1)
            left, right = jnp.where(pair, 0.0, left), jnp.where(pair, 0.0, right)
            first, second = (left * c - right * b) * inverse, (right * a - left * b) * inverse
            for m in range(j + 2, 8):
                columns[m] = columns[m] - (first * sublanes(columns[m], j) + second * sublanes(columns[m], j + 1))
            full = full - (first * sublanes(full, j) + second * sublanes(full, j + 1))
            below = rid > j + 1
            first = jnp.where(below, first, jnp.where(rid == j + 1, b * inverse_a, 0.0))
            second = jnp.where(below, second, 0.0)
            forward = forward - (first * sublanes(forward, j) + second * sublanes(forward, j + 1))
            scale = jnp.where(rid == j, lax.rsqrt(a), jnp.where(rid == j + 1, lax.rsqrt(det * inverse_a), scale))
            inverses.append((a * inverse, b * inverse, c * inverse))
        done.append(jnp.where(cid <= rid + base, forward * scale, 0.0))
        if k + 1 == n:
            break
        spread = []
        for j, (a, b, c) in enumerate(inverses):
            above, under = sublanes(full, 2 * j), sublanes(full, 2 * j + 1)
            spread += [above * c - under * b, under * a - above * b]
        terms = [lanes(rows[k + 1], base + j) * spread[j] for j in range(8)]
        while len(terms) > 1:
            terms = [terms[q] + terms[q + 1] for q in range(0, len(terms), 2)]
        rows[k + 1] = jnp.where(inside, 0.0, rows[k + 1]) - terms[0]
        if k + 2 == n:
            continue
        solved = jnp.zeros((8, width), F32)
        for j in range(8):
            solved = jnp.where(rid == j, spread[j], solved)
        far = jnp.concatenate(rows[k + 2 :], axis=0)
        column = lax.broadcasted_iota(jnp.int32, far.shape, 1)
        within = (column >= base) & (column < base + 8)
        placed = []
        for third in thirds(solved):
            blocks = [jnp.zeros((base, width), F32)] if base else []
            blocks += [third.astype(F32), jnp.zeros((width - base - 8, width), F32)]
            placed.append(jnp.concatenate(blocks, axis=0).astype(BF16))
        update = product_of_thirds(thirds(jnp.where(within, far, 0.0)), placed)
        far = jnp.where(within, 0.0, far) - update
        for i in range(k + 2, n):
            rows[i] = far[8 * (i - k - 2) : 8 * (i - k - 1)]
    return done


def pack(gram):
    width = gram.shape[0]
    half = width // 2
    row = lax.broadcasted_iota(jnp.int32, (half, width), 0)
    col = lax.broadcasted_iota(jnp.int32, (half, width), 1)
    turned = pltpu.roll(gram[half:, :], half, 1)
    both = jnp.where((col < half) & (row < col), turned, gram[:half, :])
    diagonal = jnp.sum(jnp.where(row + half == col, gram[half:, :], 0.0), axis=0, keepdims=True)
    return jnp.concatenate([both, jnp.broadcast_to(diagonal, (8, width))], axis=0)


def unpack(packed):
    width = packed.shape[1]
    half = width // 2
    row = lax.broadcasted_iota(jnp.int32, (width, width), 0)
    col = lax.broadcasted_iota(jnp.int32, (width, width), 1)
    both = packed[:half, :]
    square = jnp.concatenate([both, pltpu.roll(both, half, 1)], axis=0)
    direct = ((row < half) & ((col >= half) | (col <= row))) | ((row >= half) & (col >= half) & (col > row))
    gram = jnp.where(direct, square, square.T)
    return jnp.where((row == col) & (row >= half), jnp.broadcast_to(packed[half : half + 1, :], gram.shape), gram)


def leading(even_ref, odd_ref):
    return jnp.where(lax.axis_index("cols") % 2 == 0, even_ref[...], odd_ref[...])


def tall(tile, rows):
    return jnp.broadcast_to(tile[None], (rows // 8, *tile.shape)).reshape(rows, tile.shape[1])


def split_kernel(rounds, nblock, scale_hbm, z_hbm, first_ref, own_ref, factor_ref, scale_ref, z_ref, wide, sems):
    group = lax.axis_index("cols")
    odd = group % 2
    width = z_ref.shape[1]
    span = z_ref.shape[0] // nblock
    points = span // rounds
    scale_copy = pltpu.make_async_copy(scale_hbm, scale_ref, sems.at[nblock])
    scale_copy.start()
    copies = []
    for b in range(nblock):
        at = slice(b * span, (b + 1) * span)
        copies.append(pltpu.make_async_copy(z_hbm.at[at, :], z_ref.at[at, :], sems.at[b]))
        copies[b].start()
    scale_copy.wait()
    row = lax.broadcasted_iota(jnp.int32, (8, width), 0)
    for b in range(nblock):
        lead = jnp.broadcast_to(scale_ref[b, 0:1, 0:1], (8, width))
        mine = scale_ref[b, pl.ds(group, 1), :]
        theirs = scale_ref[b, pl.ds(group + 1 - 2 * odd, 1), :]
        mine, theirs = [[jnp.broadcast_to(x[:, r : r + 1], (8, width)) for r in range(2)] for x in (mine, theirs)]
        factor_ref[4 * b] = lead * jnp.where(odd == 1, theirs[0], theirs[1])
        factor_ref[4 * b + 1] = lead * jnp.where(odd == 1, mine[0], mine[1])
        factor_ref[4 * b + 2] = lead
        factor_ref[4 * b + 3] = jnp.where(row % rounds == 0, jnp.where(group == 0, 0.0, mine[0]), mine[1])
    for b in range(nblock):
        copies[b].wait()
        at = slice(b * span, (b + 1) * span)
        wide[at, :] = z_ref[at, :].astype(F32)
        first = wide[pl.ds(b * span, points, stride=rounds), :].astype(BF16)
        last = wide[pl.ds(b * span + 1, points, stride=rounds), :].astype(BF16)
        first_ref[b * points : (b + 1) * points, :] = first
        own_ref[b * points : (b + 1) * points, :] = jnp.where(odd == 1, first, last)


def products_kernel(rounds, nblock, phases, factor_ref, first_ref, own_ref, recv_ref, *rest):
    lead_ref = rest[:-4] if len(rest) == 4 else (*rest[:2], rest[-1])
    same_ref, other_ref, wide, cross = rest if len(rest) == 4 else rest[2:-1]
    group = lax.axis_index("cols")
    odd = group % 2
    digit = half_digit(phases, odd)
    width = recv_ref.shape[1]
    points = own_ref.shape[0] // nblock
    half = width // 2
    height = half + 8
    wide[...] = recv_ref[...].astype(F32)
    if lead_ref:
        lead_ref[2][...] = leading(*lead_ref[:2]).astype(F32)
    out = jnp.zeros((width, 2 * width), F32)
    for b in range(nblock):
        at = slice(b * points, (b + 1) * points)
        start = b * points * rounds
        theirs = wide[pl.ds(start + 1 - odd, points, stride=rounds), :].astype(BF16)
        if lead_ref:
            panel = lead_ref[2][pl.ds(start, points, stride=rounds), :].astype(BF16)
        else:
            panel = jnp.where(odd == 1, theirs, first_ref[at, :])
        block = lax.dot_general(
            panel, jnp.concatenate([theirs, own_ref[at, :]], axis=1), (((0,), (0,)), ((), ())), preferred_element_type=F32
        )
        left = block[:, :width] * tall(factor_ref[4 * b], width)
        right = block[:, width:] * tall(factor_ref[4 * b + 1], width)
        out = out + jnp.concatenate([left, right], axis=1)
    packed = pack(out[:, :width])
    cross[:width, :] = out[:, :width]
    cross[width:, :] = out[:, width:]
    for ref, place in ((same_ref, digit), (other_ref, 1 - digit)):
        theirs = cross[pl.ds(pl.multiple_of(place * half, half), half), :]
        ref[:half, :] = jnp.where(group == 1, packed[:half, :], theirs)
        ref[half:height, :] = packed[half:, :]
        ref[height : height + half, :] = cross[pl.ds(pl.multiple_of(width + place * half, half), half), :]
        ref[height + half :, :] = jnp.zeros((8, width), F32)


def spread_kernel(rounds, even_ref, odd_ref, out_ref):
    width = even_ref.shape[1]
    rows = lax.broadcasted_iota(jnp.int32, even_ref.shape, 0) % rounds
    lead = leading(even_ref, odd_ref).astype(F32)
    for r in range(rounds):
        moved = lead if r == 0 else pltpu.roll(lead, r, 0)
        out_ref[:, r * width : (r + 1) * width] = jnp.where(rows == r, moved, 0.0).astype(BF16)


def factor_kernel(sums_ref, inverse_ref, block_ref):
    width = sums_ref.shape[1]
    height = width // 2 + 8
    group = lax.axis_index("cols")

    @pl.when(group == 1)
    def _():
        gram = unpack(sums_ref[:height, :])
        block_ref[:width, :] = gram
        block_ref[width:, :] = jnp.zeros((8, width), F32)
        rows = [gram[8 * i : 8 * i + 8, :] for i in range(width // 8)]
        for i, row in enumerate(lower_inverse(rows, width)):
            inverse_ref[8 * i : 8 * i + 8, :] = row

    @pl.when(group != 1)
    def _():
        inverse_ref[...] = jnp.zeros((width, width), F32)
        block_ref[:height, :] = sums_ref[:height, :]
        block_ref[height:, :] = jnp.zeros((width + 8 - height, width), F32)


def finish_kernel(
    rounds, nblock, phases, root, chunks, factor_ref, z_ref, lead_ref, kept_ref, recv_ref, same_ref, gathered_ref, block_ref, across_ref,
    coef_ref, out_ref, mine, theirs, coef, held, sems,
):
    group = lax.axis_index("cols")
    odd = group % 2 == 1
    width = z_ref.shape[1]
    half = width // 2
    height = half + 8
    own_digit, pair_digit = half_digit(phases, group % 2), half_digit(phases, 1 - group % 2)
    for own_rows, pair_rows, other in ((same_ref, block_ref, 0), (gathered_ref, across_ref, 1)):
        mine[pl.ds(pl.multiple_of((own_digit ^ other) * half, half), half), :] = own_rows[height : height + half, :]
        theirs[pl.ds(pl.multiple_of((pair_digit ^ other) * half, half), half), :] = pair_rows[:half, :]
    own_block = mine[...]
    pair_block = jnp.where(group == 0, block_ref[...], theirs[...])
    cross = jnp.concatenate([jnp.where(odd, own_block, pair_block), jnp.where(odd, pair_block, own_block)], axis=1)
    inverse = jnp.where(odd, kept_ref[...], recv_ref[...])
    across = inverse.T
    raw = product(inverse, cross)
    for r in range(rounds):
        coef[pl.ds(r, width, stride=rounds), :] = raw[:, r * width : (r + 1) * width] * (1.0 / root)
    copies = [pltpu.make_async_copy(coef, coef_ref, sems.at[chunks])]
    copies[0].start()
    weights = product(across, raw)
    stacked = []
    for r in range(rounds):
        weight = weights[:, r * width : (r + 1) * width]
        if r == 0:
            weight = jnp.where(group == 0, -root * across, weight)
        upper = weight.astype(BF16)
        stacked.append(jnp.concatenate([upper, (weight - upper.astype(F32)).astype(BF16)], axis=1))
    weight = jnp.concatenate(stacked, axis=0)
    span = z_ref.shape[0] // chunks
    for c in range(chunks):
        block = c * nblock // chunks
        at = slice(c * span, (c + 1) * span)
        acc = jnp.dot(lead_ref[at, :], weight, preferred_element_type=F32)
        acc = (acc[:, :width] + acc[:, width:]) * tall(factor_ref[4 * block + 2], span)
        factor = tall(factor_ref[4 * block + 3], span)
        held[at, :] = (z_ref[at, :].astype(F32) * factor - acc).astype(BF16)
        copies.append(pltpu.make_async_copy(held.at[at, :], out_ref.at[at, :], sems.at[c]))
        copies[-1].start()
    for copy in copies:
        copy.wait()


def shards(snapshots, scales):
    points, _, rounds, width = snapshots.shape
    nblock = scales.shape[0]
    n_rows, n_cols = lax.axis_size("rows"), lax.axis_size("cols")
    root = math.sqrt(points * n_rows)
    long = points * rounds
    z = snapshots.reshape(long, width)
    group = lax.axis_index("cols")
    recv = partner(z, "cols", n_cols, 1)
    even = among_pairs(z, n_cols, group, 0)
    leads = (even, recv) if n_cols == 2 else (even, partner(even, "cols", n_cols, 1))
    phases = radices(n_rows)
    payload = width + 16
    params = pltpu.CompilerParams(vmem_limit_bytes=48 << 20)
    first, own, factors = pl.pallas_call(
        functools.partial(split_kernel, rounds, nblock),
        out_shape=[jax.ShapeDtypeStruct((points, width), BF16)] * 2 + [jax.ShapeDtypeStruct((4 * nblock, 8, width), F32)],
        in_specs=[pl.BlockSpec(memory_space=pltpu.HBM)] * 2,
        out_specs=[VMEM] * 3,
        scratch_shapes=[
            pltpu.VMEM(scales.shape, F32),
            pltpu.VMEM((long, width), BF16),
            pltpu.VMEM((long, width), F32),
            pltpu.SemaphoreType.DMA((nblock + 1,)),
        ],
        compiler_params=params,
        name="split",
    )(*[pltpu.with_memory_space_constraint(x, pltpu.HBM) for x in (scales, z)])
    extra = () if n_cols == 2 else leads
    sent = pl.pallas_call(
        functools.partial(products_kernel, rounds, nblock, phases),
        out_shape=[jax.ShapeDtypeStruct((payload, width), F32)] * 2,
        in_specs=[VMEM] * (4 + len(extra)),
        out_specs=[VMEM] * 2,
        scratch_shapes=[pltpu.VMEM((long, width), F32), pltpu.VMEM((2 * width, width), F32)]
        + [pltpu.VMEM((long, width), F32)] * (len(extra) // 2),
        compiler_params=params,
        name="products",
    )(factors, first, own, recv, *extra)
    sums = sent[0]
    for step, (_, base) in enumerate(phases):
        source = sent if step == 0 else [sums] * 2
        others = [
            hop(source[b % 2], n_rows, n_cols, lambda parity: b * order(phases, parity)[step][0]) for b in range(1, base)
        ]
        if step == len(phases) - 1:
            lead = pl.pallas_call(
                functools.partial(spread_kernel, rounds),
                out_shape=jax.ShapeDtypeStruct((long, rounds * width), BF16),
                in_specs=[VMEM, VMEM],
                out_specs=VMEM,
                compiler_params=params,
                name="spread",
            )(*leads)
            *others, lead = lax.optimization_barrier((*others, lead))
        for other in others:
            sums = sums + other
    beside = lambda parity: order(phases, parity)[0][0]
    gathered = hop(sums, n_rows, n_cols, beside)
    inverse, block = pl.pallas_call(
        factor_kernel,
        out_shape=[jax.ShapeDtypeStruct((width + pad, width), F32) for pad in (0, 8)],
        in_specs=[VMEM],
        out_specs=[VMEM] * 2,
        compiler_params=params,
        cost_estimate=pl.CostEstimate(flops=1 << 30, bytes_accessed=1 << 23, transcendentals=0),
        name="factor",
    )(sums)
    inverse = among_pairs(inverse, n_cols, group, 1)
    swapped = partner(inverse, "cols", n_cols, 1)
    blocks = partner(block[:width], "cols", n_cols, 1)
    crossed = hop(block, n_rows, n_cols, beside, 1)
    chunks = 2 * nblock
    coef, updated = pl.pallas_call(
        functools.partial(finish_kernel, rounds, nblock, phases, root, chunks),
        out_shape=[
            jax.ShapeDtypeStruct((width * rounds, width), F32),
            jax.ShapeDtypeStruct((long, width), BF16),
        ],
        in_specs=[VMEM] * 9,
        out_specs=[pl.BlockSpec(memory_space=pl.ANY)] * 2,
        scratch_shapes=[
            pltpu.VMEM((width, width), F32),
            pltpu.VMEM((width, width), F32),
            pltpu.VMEM((width * rounds, width), F32),
            pltpu.VMEM((long, width), BF16),
            pltpu.SemaphoreType.DMA((chunks + 1,)),
        ],
        compiler_params=params,
        name="finish",
    )(factors, z, lead, inverse, swapped, sums, gathered, blocks, crossed)
    return coef.reshape(width, 1, rounds, width), updated.reshape(snapshots.shape)


def solution(mesh):
    return jax.shard_map(
        shards,
        mesh=mesh,
        in_specs=(P("rows", "cols", None, None), P("rows", None, None)),
        out_specs=(P(None, "cols", None, None), P("rows", "cols", None, None)),
        check_vma=False,
    )
```

```python
import functools
import math

import jax
import jax.numpy as jnp
from jax import lax
from jax.experimental import pallas as pl
from jax.experimental.pallas import tpu as pltpu
from jax.sharding import PartitionSpec as P

F32 = jnp.float32
BF16 = jnp.bfloat16
VMEM = pl.BlockSpec(memory_space=pltpu.VMEM)


def partner(x, axis, count, offset):
    return lax.ppermute(x, axis, [(i, i ^ offset) for i in range(count)])


def radices(count):
    found = []
    stride = 1
    while stride < count:
        radix = 4 if (count // stride) % 4 == 0 else 2
        found.append((stride, radix))
        stride *= radix
    return found


def order(phases, parity):
    if parity == 0 and len({radix for _, radix in phases}) == 1:
        return phases[::-1]
    return phases


def hop(x, n_rows, n_cols, offset):
    pairs = []
    for row in range(n_rows):
        for col in range(n_cols):
            pairs.append((row * n_cols + col, (row ^ offset(col % 2)) * n_cols + col))
    return lax.ppermute(x, ("rows", "cols"), pairs)


def half_digit(phases, parity):
    even, odd = [(lax.axis_index("rows") // order(phases, p)[0][0]) % 2 for p in range(2)]
    return jnp.where(parity == 0, even, odd)


def among_pairs(x, count, mine, root):
    stride = 2
    while stride < count:
        x = jnp.where(((mine ^ root) & stride) != 0, partner(x, "cols", count, stride), x)
        stride *= 2
    return x


def lanes(x, p):
    return jnp.broadcast_to(x[:, p : p + 1], x.shape)


def sublanes(x, j):
    return jnp.broadcast_to(x[j : j + 1, :], x.shape)


def thirds(x):
    high = x.astype(BF16)
    rest = x - high.astype(F32)
    middle = rest.astype(BF16)
    return high, middle, (rest - middle.astype(F32)).astype(BF16)


def product(left, right):
    return product_of_thirds(thirds(left), thirds(right))


def product_of_thirds(left, right):
    columns = right[0].shape[1]
    wide = jnp.concatenate(right[:2], axis=1)
    both = jnp.dot(
        jnp.concatenate(left[:2], axis=1), jnp.concatenate([wide, wide], axis=0), preferred_element_type=F32
    )
    small = jnp.dot(
        jnp.concatenate([left[0], left[2]], axis=1),
        jnp.concatenate([right[2], right[0]], axis=0),
        preferred_element_type=F32,
    )
    return (both[:, :columns] + both[:, columns:]) + small


def lower_inverse(rows, width):
    n = len(rows)
    rid = lax.broadcasted_iota(jnp.int32, (8, width), 0)
    cid = lax.broadcasted_iota(jnp.int32, (8, width), 1)
    done = []
    for k in range(n):
        base = 8 * k
        held = rows[k]
        columns = [lanes(held, base + j) for j in range(8)]
        inside = (cid >= base) & (cid < base + 8)
        eye = jnp.where(cid - base == rid, 1.0, 0.0).astype(F32)
        full = jnp.where(inside, eye, held)
        forward = full
        scale = jnp.zeros((8, width), F32)
        inverses = []
        for j in range(0, 8, 2):
            left, right = columns[j], columns[j + 1]
            a, b, c = sublanes(left, j), sublanes(right, j), sublanes(right, j + 1)
            det = a * c - b * b
            inverse, inverse_a = 1.0 / det, 1.0 / a
            pair = (rid == j) | (rid == j + 1)
            left, right = jnp.where(pair, 0.0, left), jnp.where(pair, 0.0, right)
            first, second = (left * c - right * b) * inverse, (right * a - left * b) * inverse
            for m in range(j + 2, 8):
                columns[m] = columns[m] - (first * sublanes(columns[m], j) + second * sublanes(columns[m], j + 1))
            full = full - (first * sublanes(full, j) + second * sublanes(full, j + 1))
            below = rid > j + 1
            first = jnp.where(below, first, jnp.where(rid == j + 1, b * inverse_a, 0.0))
            second = jnp.where(below, second, 0.0)
            forward = forward - (first * sublanes(forward, j) + second * sublanes(forward, j + 1))
            scale = jnp.where(rid == j, lax.rsqrt(a), jnp.where(rid == j + 1, lax.rsqrt(det * inverse_a), scale))
            inverses.append((a * inverse, b * inverse, c * inverse))
        done.append(jnp.where(cid <= rid + base, forward * scale, 0.0))
        if k + 1 == n:
            break
        spread = []
        for j, (a, b, c) in enumerate(inverses):
            above, under = sublanes(full, 2 * j), sublanes(full, 2 * j + 1)
            spread += [above * c - under * b, under * a - above * b]
        terms = [lanes(rows[k + 1], base + j) * spread[j] for j in range(8)]
        while len(terms) > 1:
            terms = [terms[q] + terms[q + 1] for q in range(0, len(terms), 2)]
        rows[k + 1] = jnp.where(inside, 0.0, rows[k + 1]) - terms[0]
        if k + 2 == n:
            continue
        solved = jnp.zeros((8, width), F32)
        for j in range(8):
            solved = jnp.where(rid == j, spread[j], solved)
        far = jnp.concatenate(rows[k + 2 :], axis=0)
        column = lax.broadcasted_iota(jnp.int32, far.shape, 1)
        within = (column >= base) & (column < base + 8)
        placed = []
        for third in thirds(solved):
            blocks = [jnp.zeros((base, width), F32)] if base else []
            blocks += [third.astype(F32), jnp.zeros((width - base - 8, width), F32)]
            placed.append(jnp.concatenate(blocks, axis=0).astype(BF16))
        update = product_of_thirds(thirds(jnp.where(within, far, 0.0)), placed)
        far = jnp.where(within, 0.0, far) - update
        for i in range(k + 2, n):
            rows[i] = far[8 * (i - k - 2) : 8 * (i - k - 1)]
    return done


def pack(gram):
    width = gram.shape[0]
    half = width // 2
    row = lax.broadcasted_iota(jnp.int32, (half, width), 0)
    col = lax.broadcasted_iota(jnp.int32, (half, width), 1)
    turned = pltpu.roll(gram[half:, :], half, 1)
    both = jnp.where((col < half) & (row < col), turned, gram[:half, :])
    diagonal = jnp.sum(jnp.where(row + half == col, gram[half:, :], 0.0), axis=0, keepdims=True)
    return jnp.concatenate([both, jnp.broadcast_to(diagonal, (8, width))], axis=0)


def unpack(packed):
    width = packed.shape[1]
    half = width // 2
    row = lax.broadcasted_iota(jnp.int32, (width, width), 0)
    col = lax.broadcasted_iota(jnp.int32, (width, width), 1)
    both = packed[:half, :]
    square = jnp.concatenate([both, pltpu.roll(both, half, 1)], axis=0)
    direct = ((row < half) & ((col >= half) | (col <= row))) | ((row >= half) & (col >= half) & (col > row))
    gram = jnp.where(direct, square, square.T)
    return jnp.where((row == col) & (row >= half), jnp.broadcast_to(packed[half : half + 1, :], gram.shape), gram)


def leading(even_ref, odd_ref):
    return jnp.where(lax.axis_index("cols") % 2 == 0, even_ref[...], odd_ref[...])


def tall(tile, rows):
    return jnp.broadcast_to(tile[None], (rows // 8, *tile.shape)).reshape(rows, tile.shape[1])


def split_kernel(rounds, nblock, scale_hbm, z_hbm, first_ref, own_ref, factor_ref, scale_ref, z_ref, wide, sems):
    group = lax.axis_index("cols")
    odd = group % 2
    width = z_ref.shape[1]
    span = z_ref.shape[0] // nblock
    points = span // rounds
    scale_copy = pltpu.make_async_copy(scale_hbm, scale_ref, sems.at[nblock])
    scale_copy.start()
    copies = []
    for b in range(nblock):
        at = slice(b * span, (b + 1) * span)
        copies.append(pltpu.make_async_copy(z_hbm.at[at, :], z_ref.at[at, :], sems.at[b]))
        copies[b].start()
    scale_copy.wait()
    row = lax.broadcasted_iota(jnp.int32, (8, width), 0)
    for b in range(nblock):
        lead = jnp.broadcast_to(scale_ref[b, 0:1, 0:1], (8, width))
        mine = scale_ref[b, pl.ds(group, 1), :]
        theirs = scale_ref[b, pl.ds(group + 1 - 2 * odd, 1), :]
        mine, theirs = [[jnp.broadcast_to(x[:, r : r + 1], (8, width)) for r in range(2)] for x in (mine, theirs)]
        factor_ref[4 * b] = lead * jnp.where(odd == 1, theirs[0], theirs[1])
        factor_ref[4 * b + 1] = lead * jnp.where(odd == 1, mine[0], mine[1])
        factor_ref[4 * b + 2] = lead
        factor_ref[4 * b + 3] = jnp.where(row % rounds == 0, jnp.where(group == 0, 0.0, mine[0]), mine[1])
    for b in range(nblock):
        copies[b].wait()
        at = slice(b * span, (b + 1) * span)
        wide[at, :] = z_ref[at, :].astype(F32)
        first = wide[pl.ds(b * span, points, stride=rounds), :].astype(BF16)
        last = wide[pl.ds(b * span + 1, points, stride=rounds), :].astype(BF16)
        first_ref[b * points : (b + 1) * points, :] = first
        own_ref[b * points : (b + 1) * points, :] = jnp.where(odd == 1, first, last)


def products_kernel(rounds, nblock, phases, factor_ref, first_ref, own_ref, recv_ref, *rest):
    lead_ref = rest[:-4] if len(rest) == 4 else (*rest[:2], rest[-1])
    same_ref, other_ref, wide, cross = rest if len(rest) == 4 else rest[2:-1]
    group = lax.axis_index("cols")
    odd = group % 2
    digit = half_digit(phases, odd)
    width = recv_ref.shape[1]
    points = own_ref.shape[0] // nblock
    half = width // 2
    height = half + 8
    wide[...] = recv_ref[...].astype(F32)
    if lead_ref:
        lead_ref[2][...] = leading(*lead_ref[:2]).astype(F32)
    out = jnp.zeros((width, 2 * width), F32)
    for b in range(nblock):
        at = slice(b * points, (b + 1) * points)
        start = b * points * rounds
        theirs = wide[pl.ds(start + 1 - odd, points, stride=rounds), :].astype(BF16)
        if lead_ref:
            panel = lead_ref[2][pl.ds(start, points, stride=rounds), :].astype(BF16)
        else:
            panel = jnp.where(odd == 1, theirs, first_ref[at, :])
        block = lax.dot_general(
            panel, jnp.concatenate([theirs, own_ref[at, :]], axis=1), (((0,), (0,)), ((), ())), preferred_element_type=F32
        )
        left = block[:, :width] * tall(factor_ref[4 * b], width)
        right = block[:, width:] * tall(factor_ref[4 * b + 1], width)
        out = out + jnp.concatenate([left, right], axis=1)
    packed = pack(out[:, :width])
    cross[:width, :] = out[:, :width]
    cross[width:, :] = out[:, width:]
    for ref, place in ((same_ref, digit), (other_ref, 1 - digit)):
        theirs = cross[pl.ds(pl.multiple_of(place * half, half), half), :]
        ref[:half, :] = jnp.where(group == 1, packed[:half, :], theirs)
        ref[half:height, :] = packed[half:, :]
        ref[height:, :] = cross[pl.ds(pl.multiple_of(width + place * half, half), half), :]


def spread_kernel(rounds, even_ref, odd_ref, out_ref):
    width = even_ref.shape[1]
    rows = lax.broadcasted_iota(jnp.int32, even_ref.shape, 0) % rounds
    lead = leading(even_ref, odd_ref).astype(F32)
    for r in range(rounds):
        moved = lead if r == 0 else pltpu.roll(lead, r, 0)
        out_ref[:, r * width : (r + 1) * width] = jnp.where(rows == r, moved, 0.0).astype(BF16)


def factor_kernel(sums_ref, inverse_ref, block_ref):
    width = sums_ref.shape[1]
    height = width // 2 + 8
    group = lax.axis_index("cols")

    @pl.when(group == 1)
    def _():
        gram = unpack(sums_ref[:height, :])
        block_ref[...] = gram
        rows = [gram[8 * i : 8 * i + 8, :] for i in range(width // 8)]
        for i, row in enumerate(lower_inverse(rows, width)):
            inverse_ref[8 * i : 8 * i + 8, :] = row

    @pl.when(group != 1)
    def _():
        inverse_ref[...] = jnp.zeros((width, width), F32)
        block_ref[:height, :] = sums_ref[:height, :]
        block_ref[height:, :] = jnp.zeros((width - height, width), F32)


def finish_kernel(
    rounds, nblock, phases, root, chunks, factor_ref, z_ref, lead_ref, kept_ref, recv_ref, same_ref, gathered_ref, block_ref, across_ref,
    coef_ref, out_ref, mine, theirs, coef, held, sems,
):
    group = lax.axis_index("cols")
    odd = group % 2 == 1
    width = z_ref.shape[1]
    half = width // 2
    height = half + 8
    own_digit, pair_digit = half_digit(phases, group % 2), half_digit(phases, 1 - group % 2)
    for own_rows, pair_rows, other in ((same_ref, block_ref, 0), (gathered_ref, across_ref, 1)):
        mine[pl.ds(pl.multiple_of((own_digit ^ other) * half, half), half), :] = own_rows[height : height + half, :]
        theirs[pl.ds(pl.multiple_of((pair_digit ^ other) * half, half), half), :] = pair_rows[:half, :]
    own_block = mine[...]
    pair_block = jnp.where(group == 0, block_ref[...], theirs[...])
    cross = jnp.concatenate([jnp.where(odd, own_block, pair_block), jnp.where(odd, pair_block, own_block)], axis=1)
    inverse = jnp.where(odd, kept_ref[...], recv_ref[...])
    across = inverse.T
    raw = product(inverse, cross)
    for r in range(rounds):
        coef[pl.ds(r, width, stride=rounds), :] = raw[:, r * width : (r + 1) * width] * (1.0 / root)
    copies = [pltpu.make_async_copy(coef, coef_ref, sems.at[chunks])]
    copies[0].start()
    weights = product(across, raw)
    stacked = []
    for r in range(rounds):
        weight = weights[:, r * width : (r + 1) * width]
        if r == 0:
            weight = jnp.where(group == 0, -root * across, weight)
        upper = weight.astype(BF16)
        stacked.append(jnp.concatenate([upper, (weight - upper.astype(F32)).astype(BF16)], axis=1))
    weight = jnp.concatenate(stacked, axis=0)
    span = z_ref.shape[0] // chunks
    for c in range(chunks):
        block = c * nblock // chunks
        at = slice(c * span, (c + 1) * span)
        acc = jnp.dot(lead_ref[at, :], weight, preferred_element_type=F32)
        acc = (acc[:, :width] + acc[:, width:]) * tall(factor_ref[4 * block + 2], span)
        factor = tall(factor_ref[4 * block + 3], span)
        held[at, :] = (z_ref[at, :].astype(F32) * factor - acc).astype(BF16)
        copies.append(pltpu.make_async_copy(held.at[at, :], out_ref.at[at, :], sems.at[c]))
        copies[-1].start()
    for copy in copies:
        copy.wait()


def shards(snapshots, scales):
    points, _, rounds, width = snapshots.shape
    nblock = scales.shape[0]
    n_rows, n_cols = lax.axis_size("rows"), lax.axis_size("cols")
    root = math.sqrt(points * n_rows)
    long = points * rounds
    z = snapshots.reshape(long, width)
    group = lax.axis_index("cols")
    recv = partner(z, "cols", n_cols, 1)
    even = among_pairs(z, n_cols, group, 0)
    leads = (even, recv) if n_cols == 2 else (even, partner(even, "cols", n_cols, 1))
    phases = radices(n_rows)
    payload = width + 8
    params = pltpu.CompilerParams(vmem_limit_bytes=48 << 20)
    first, own, factors = pl.pallas_call(
        functools.partial(split_kernel, rounds, nblock),
        out_shape=[jax.ShapeDtypeStruct((points, width), BF16)] * 2 + [jax.ShapeDtypeStruct((4 * nblock, 8, width), F32)],
        in_specs=[pl.BlockSpec(memory_space=pltpu.HBM)] * 2,
        out_specs=[VMEM] * 3,
        scratch_shapes=[
            pltpu.VMEM(scales.shape, F32),
            pltpu.VMEM((long, width), BF16),
            pltpu.VMEM((long, width), F32),
            pltpu.SemaphoreType.DMA((nblock + 1,)),
        ],
        compiler_params=params,
        name="split",
    )(*[pltpu.with_memory_space_constraint(x, pltpu.HBM) for x in (scales, z)])
    extra = () if n_cols == 2 else leads
    sent = pl.pallas_call(
        functools.partial(products_kernel, rounds, nblock, phases),
        out_shape=[jax.ShapeDtypeStruct((payload, width), F32)] * 2,
        in_specs=[VMEM] * (4 + len(extra)),
        out_specs=[VMEM] * 2,
        scratch_shapes=[pltpu.VMEM((long, width), F32), pltpu.VMEM((2 * width, width), F32)]
        + [pltpu.VMEM((long, width), F32)] * (len(extra) // 2),
        compiler_params=params,
        name="products",
    )(factors, first, own, recv, *extra)
    sums = sent[0]
    for step, (_, base) in enumerate(phases):
        source = sent if step == 0 else [sums] * 2
        others = [
            hop(source[b % 2], n_rows, n_cols, lambda parity: b * order(phases, parity)[step][0]) for b in range(1, base)
        ]
        if step == len(phases) - 1:
            lead = pl.pallas_call(
                functools.partial(spread_kernel, rounds),
                out_shape=jax.ShapeDtypeStruct((long, rounds * width), BF16),
                in_specs=[VMEM, VMEM],
                out_specs=VMEM,
                compiler_params=params,
                name="spread",
            )(*leads)
            *others, lead = lax.optimization_barrier((*others, lead))
        for other in others:
            sums = sums + other
    beside = lambda parity: order(phases, parity)[0][0]
    gathered = hop(sums, n_rows, n_cols, beside)
    inverse, block = pl.pallas_call(
        factor_kernel,
        out_shape=[jax.ShapeDtypeStruct((width, width), F32)] * 2,
        in_specs=[VMEM],
        out_specs=[VMEM] * 2,
        compiler_params=params,
        cost_estimate=pl.CostEstimate(flops=1 << 30, bytes_accessed=1 << 23, transcendentals=0),
        name="factor",
    )(sums)
    inverse = among_pairs(inverse, n_cols, group, 1)
    swapped = partner(inverse, "cols", n_cols, 1)
    blocks = partner(block, "cols", n_cols, 1)
    crossed = partner(gathered, "cols", n_cols, 1)
    chunks = 2 * nblock
    coef, updated = pl.pallas_call(
        functools.partial(finish_kernel, rounds, nblock, phases, root, chunks),
        out_shape=[
            jax.ShapeDtypeStruct((width * rounds, width), F32),
            jax.ShapeDtypeStruct((long, width), BF16),
        ],
        in_specs=[VMEM] * 9,
        out_specs=[pl.BlockSpec(memory_space=pl.ANY)] * 2,
        scratch_shapes=[
            pltpu.VMEM((width, width), F32),
            pltpu.VMEM((width, width), F32),
            pltpu.VMEM((width * rounds, width), F32),
            pltpu.VMEM((long, width), BF16),
            pltpu.SemaphoreType.DMA((chunks + 1,)),
        ],
        compiler_params=params,
        name="finish",
    )(factors, z, lead, inverse, swapped, sums, gathered, blocks, crossed)
    return coef.reshape(width, 1, rounds, width), updated.reshape(snapshots.shape)


def solution(mesh):
    return jax.shard_map(
        shards,
        mesh=mesh,
        in_specs=(P("rows", "cols", None, None), P("rows", None, None)),
        out_specs=(P(None, "cols", None, None), P("rows", "cols", None, None)),
        check_vma=False,
    )
```

```python
import functools
import math

import jax
import jax.numpy as jnp
from jax import lax
from jax.experimental import pallas as pl
from jax.experimental.pallas import tpu as pltpu
from jax.sharding import PartitionSpec as P

F32 = jnp.float32
BF16 = jnp.bfloat16
VMEM = pl.BlockSpec(memory_space=pltpu.VMEM)


def partner(x, axis, count, offset):
    return lax.ppermute(x, axis, [(i, i ^ offset) for i in range(count)])


def radices(count):
    found = []
    stride = 1
    while stride < count:
        radix = 4 if (count // stride) % 4 == 0 else 2
        found.append((stride, radix))
        stride *= radix
    return found


def order(phases, parity):
    if parity == 0 and len({radix for _, radix in phases}) == 1:
        return phases[::-1]
    return phases


def hop(x, n_rows, n_cols, offset):
    pairs = []
    for row in range(n_rows):
        for col in range(n_cols):
            pairs.append((row * n_cols + col, (row ^ offset(col % 2)) * n_cols + col))
    return lax.ppermute(x, ("rows", "cols"), pairs)


def half_digit(phases, parity):
    even, odd = [(lax.axis_index("rows") // order(phases, p)[0][0]) % 2 for p in range(2)]
    return jnp.where(parity == 0, even, odd)


def among_pairs(x, count, mine, root):
    stride = 2
    while stride < count:
        x = jnp.where(((mine ^ root) & stride) != 0, partner(x, "cols", count, stride), x)
        stride *= 2
    return x


def lanes(x, p):
    return jnp.broadcast_to(x[:, p : p + 1], x.shape)


def sublanes(x, j):
    return jnp.broadcast_to(x[j : j + 1, :], x.shape)


def thirds(x):
    high = x.astype(BF16)
    rest = x - high.astype(F32)
    middle = rest.astype(BF16)
    return high, middle, (rest - middle.astype(F32)).astype(BF16)


def product(left, right):
    return product_of_thirds(thirds(left), thirds(right))


def product_of_thirds(left, right):
    columns = right[0].shape[1]
    wide = jnp.concatenate(right[:2], axis=1)
    both = jnp.dot(
        jnp.concatenate(left[:2], axis=1), jnp.concatenate([wide, wide], axis=0), preferred_element_type=F32
    )
    small = jnp.dot(
        jnp.concatenate([left[0], left[2]], axis=1),
        jnp.concatenate([right[2], right[0]], axis=0),
        preferred_element_type=F32,
    )
    return (both[:, :columns] + both[:, columns:]) + small


def lower_inverse(rows, width):
    n = len(rows)
    rid = lax.broadcasted_iota(jnp.int32, (8, width), 0)
    cid = lax.broadcasted_iota(jnp.int32, (8, width), 1)
    done = []
    for k in range(n):
        base = 8 * k
        held = rows[k]
        columns = [lanes(held, base + j) for j in range(8)]
        inside = (cid >= base) & (cid < base + 8)
        eye = jnp.where(cid - base == rid, 1.0, 0.0).astype(F32)
        full = jnp.where(inside, eye, held)
        forward = full
        scale = jnp.zeros((8, width), F32)
        inverses = []
        for j in range(0, 8, 2):
            left, right = columns[j], columns[j + 1]
            a, b, c = sublanes(left, j), sublanes(right, j), sublanes(right, j + 1)
            det = a * c - b * b
            inverse, inverse_a = 1.0 / det, 1.0 / a
            pair = (rid == j) | (rid == j + 1)
            left, right = jnp.where(pair, 0.0, left), jnp.where(pair, 0.0, right)
            first, second = (left * c - right * b) * inverse, (right * a - left * b) * inverse
            for m in range(j + 2, 8):
                columns[m] = columns[m] - (first * sublanes(columns[m], j) + second * sublanes(columns[m], j + 1))
            full = full - (first * sublanes(full, j) + second * sublanes(full, j + 1))
            below = rid > j + 1
            first = jnp.where(below, first, jnp.where(rid == j + 1, b * inverse_a, 0.0))
            second = jnp.where(below, second, 0.0)
            forward = forward - (first * sublanes(forward, j) + second * sublanes(forward, j + 1))
            scale = jnp.where(rid == j, lax.rsqrt(a), jnp.where(rid == j + 1, lax.rsqrt(det * inverse_a), scale))
            inverses.append((a * inverse, b * inverse, c * inverse))
        done.append(jnp.where(cid <= rid + base, forward * scale, 0.0))
        if k + 1 == n:
            break
        spread = []
        for j, (a, b, c) in enumerate(inverses):
            above, under = sublanes(full, 2 * j), sublanes(full, 2 * j + 1)
            spread += [above * c - under * b, under * a - above * b]
        terms = [lanes(rows[k + 1], base + j) * spread[j] for j in range(8)]
        while len(terms) > 1:
            terms = [terms[q] + terms[q + 1] for q in range(0, len(terms), 2)]
        rows[k + 1] = jnp.where(inside, 0.0, rows[k + 1]) - terms[0]
        if k + 2 == n:
            continue
        solved = jnp.zeros((8, width), F32)
        for j in range(8):
            solved = jnp.where(rid == j, spread[j], solved)
        far = jnp.concatenate(rows[k + 2 :], axis=0)
        column = lax.broadcasted_iota(jnp.int32, far.shape, 1)
        within = (column >= base) & (column < base + 8)
        placed = []
        for third in thirds(solved):
            blocks = [jnp.zeros((base, width), F32)] if base else []
            blocks += [third.astype(F32), jnp.zeros((width - base - 8, width), F32)]
            placed.append(jnp.concatenate(blocks, axis=0).astype(BF16))
        update = product_of_thirds(thirds(jnp.where(within, far, 0.0)), placed)
        far = jnp.where(within, 0.0, far) - update
        for i in range(k + 2, n):
            rows[i] = far[8 * (i - k - 2) : 8 * (i - k - 1)]
    return done


def pack(gram):
    width = gram.shape[0]
    half = width // 2
    row = lax.broadcasted_iota(jnp.int32, (half, width), 0)
    col = lax.broadcasted_iota(jnp.int32, (half, width), 1)
    turned = pltpu.roll(gram[half:, :], half, 1)
    both = jnp.where((col < half) & (row < col), turned, gram[:half, :])
    diagonal = jnp.sum(jnp.where(row + half == col, gram[half:, :], 0.0), axis=0, keepdims=True)
    return jnp.concatenate([both, jnp.broadcast_to(diagonal, (8, width))], axis=0)


def unpack(packed):
    width = packed.shape[1]
    half = width // 2
    row = lax.broadcasted_iota(jnp.int32, (width, width), 0)
    col = lax.broadcasted_iota(jnp.int32, (width, width), 1)
    both = packed[:half, :]
    square = jnp.concatenate([both, pltpu.roll(both, half, 1)], axis=0)
    direct = ((row < half) & ((col >= half) | (col <= row))) | ((row >= half) & (col >= half) & (col > row))
    gram = jnp.where(direct, square, square.T)
    return jnp.where((row == col) & (row >= half), jnp.broadcast_to(packed[half : half + 1, :], gram.shape), gram)


def leading(even_ref, odd_ref):
    return jnp.where(lax.axis_index("cols") % 2 == 0, even_ref[...], odd_ref[...])


def tall(tile, rows):
    return jnp.broadcast_to(tile[None], (rows // 8, *tile.shape)).reshape(rows, tile.shape[1])


def split_kernel(rounds, nblock, scale_hbm, z_hbm, first_ref, own_ref, factor_ref, scale_ref, z_ref, wide, sems):
    group = lax.axis_index("cols")
    odd = group % 2
    width = z_ref.shape[1]
    span = z_ref.shape[0] // nblock
    points = span // rounds
    scale_copy = pltpu.make_async_copy(scale_hbm, scale_ref, sems.at[nblock])
    scale_copy.start()
    copies = []
    for b in range(nblock):
        at = slice(b * span, (b + 1) * span)
        copies.append(pltpu.make_async_copy(z_hbm.at[at, :], z_ref.at[at, :], sems.at[b]))
        copies[b].start()
    scale_copy.wait()
    row = lax.broadcasted_iota(jnp.int32, (8, width), 0)
    for b in range(nblock):
        lead = jnp.broadcast_to(scale_ref[b, 0:1, 0:1], (8, width))
        mine = scale_ref[b, pl.ds(group, 1), :]
        theirs = scale_ref[b, pl.ds(group + 1 - 2 * odd, 1), :]
        mine, theirs = [[jnp.broadcast_to(x[:, r : r + 1], (8, width)) for r in range(2)] for x in (mine, theirs)]
        factor_ref[4 * b] = lead * jnp.where(odd == 1, theirs[0], theirs[1])
        factor_ref[4 * b + 1] = lead * jnp.where(odd == 1, mine[0], mine[1])
        factor_ref[4 * b + 2] = lead
        factor_ref[4 * b + 3] = jnp.where(row % rounds == 0, jnp.where(group == 0, 0.0, mine[0]), mine[1])
    for b in range(nblock):
        copies[b].wait()
        at = slice(b * span, (b + 1) * span)
        wide[at, :] = z_ref[at, :].astype(F32)
        first = wide[pl.ds(b * span, points, stride=rounds), :].astype(BF16)
        last = wide[pl.ds(b * span + 1, points, stride=rounds), :].astype(BF16)
        first_ref[b * points : (b + 1) * points, :] = first
        own_ref[b * points : (b + 1) * points, :] = jnp.where(odd == 1, first, last)


def products_kernel(rounds, nblock, phases, factor_ref, first_ref, own_ref, recv_ref, *rest):
    lead_ref = rest[:-4] if len(rest) == 4 else (*rest[:2], rest[-1])
    same_ref, other_ref, wide, cross = rest if len(rest) == 4 else rest[2:-1]
    group = lax.axis_index("cols")
    odd = group % 2
    digit = half_digit(phases, odd)
    width = recv_ref.shape[1]
    points = own_ref.shape[0] // nblock
    half = width // 2
    height = half + 8
    wide[...] = recv_ref[...].astype(F32)
    if lead_ref:
        lead_ref[2][...] = leading(*lead_ref[:2]).astype(F32)
    out = jnp.zeros((width, 2 * width), F32)
    for b in range(nblock):
        at = slice(b * points, (b + 1) * points)
        start = b * points * rounds
        theirs = wide[pl.ds(start + 1 - odd, points, stride=rounds), :].astype(BF16)
        if lead_ref:
            panel = lead_ref[2][pl.ds(start, points, stride=rounds), :].astype(BF16)
        else:
            panel = jnp.where(odd == 1, theirs, first_ref[at, :])
        block = lax.dot_general(
            panel, jnp.concatenate([theirs, own_ref[at, :]], axis=1), (((0,), (0,)), ((), ())), preferred_element_type=F32
        )
        left = block[:, :width] * tall(factor_ref[4 * b], width)
        right = block[:, width:] * tall(factor_ref[4 * b + 1], width)
        out = out + jnp.concatenate([left, right], axis=1)
    packed = pack(out[:, :width])
    cross[:width, :] = out[:, :width]
    cross[width:, :] = out[:, width:]
    for ref, place in ((same_ref, digit), (other_ref, 1 - digit)):
        theirs = cross[pl.ds(pl.multiple_of(place * half, half), half), :]
        ref[:half, :] = jnp.where(group == 1, packed[:half, :], theirs)
        ref[half:height, :] = packed[half:, :]
        ref[height:, :] = cross[pl.ds(pl.multiple_of(width + place * half, half), half), :]


def spread_kernel(rounds, even_ref, odd_ref, out_ref):
    width = even_ref.shape[1]
    rows = lax.broadcasted_iota(jnp.int32, even_ref.shape, 0) % rounds
    lead = leading(even_ref, odd_ref).astype(F32)
    for r in range(rounds):
        moved = lead if r == 0 else pltpu.roll(lead, r, 0)
        out_ref[:, r * width : (r + 1) * width] = jnp.where(rows == r, moved, 0.0).astype(BF16)


def factor_kernel(sums_ref, inverse_ref, block_ref):
    width = sums_ref.shape[1]
    height = width // 2 + 8
    group = lax.axis_index("cols")

    @pl.when(group == 1)
    def _():
        gram = unpack(sums_ref[:height, :])
        block_ref[...] = gram
        rows = [gram[8 * i : 8 * i + 8, :] for i in range(width // 8)]
        for i, row in enumerate(lower_inverse(rows, width)):
            inverse_ref[8 * i : 8 * i + 8, :] = row

    @pl.when(group != 1)
    def _():
        inverse_ref[...] = jnp.zeros((width, width), F32)
        block_ref[:height, :] = sums_ref[:height, :]
        block_ref[height:, :] = jnp.zeros((width - height, width), F32)


def finish_kernel(
    rounds, nblock, phases, root, chunks, factor_ref, z_ref, lead_ref, kept_ref, recv_ref, same_ref, gathered_ref, block_ref, across_ref,
    coef_ref, out_ref, mine, theirs, coef, held, sems,
):
    group = lax.axis_index("cols")
    odd = group % 2 == 1
    width = z_ref.shape[1]
    half = width // 2
    height = half + 8
    own_digit, pair_digit = half_digit(phases, group % 2), half_digit(phases, 1 - group % 2)
    for own_rows, pair_rows, other in ((same_ref, block_ref, 0), (gathered_ref, across_ref, 1)):
        mine[pl.ds(pl.multiple_of((own_digit ^ other) * half, half), half), :] = own_rows[height : height + half, :]
        theirs[pl.ds(pl.multiple_of((pair_digit ^ other) * half, half), half), :] = pair_rows[:half, :]
    own_block = mine[...]
    pair_block = jnp.where(group == 0, block_ref[...], theirs[...])
    cross = jnp.concatenate([jnp.where(odd, own_block, pair_block), jnp.where(odd, pair_block, own_block)], axis=1)
    inverse = jnp.where(odd, kept_ref[...], recv_ref[...])
    across = inverse.T
    raw = product(inverse, cross)
    for r in range(rounds):
        coef[pl.ds(r, width, stride=rounds), :] = raw[:, r * width : (r + 1) * width] * (1.0 / root)
    copies = [pltpu.make_async_copy(coef, coef_ref, sems.at[chunks])]
    copies[0].start()
    weights = product(across, raw)
    stacked = []
    for r in range(rounds):
        weight = weights[:, r * width : (r + 1) * width]
        if r == 0:
            weight = jnp.where(group == 0, -root * across, weight)
        upper = weight.astype(BF16)
        stacked.append(jnp.concatenate([upper, (weight - upper.astype(F32)).astype(BF16)], axis=1))
    weight = jnp.concatenate(stacked, axis=0)
    span = z_ref.shape[0] // chunks
    for c in range(chunks):
        block = c * nblock // chunks
        at = slice(c * span, (c + 1) * span)
        acc = jnp.dot(lead_ref[at, :], weight, preferred_element_type=F32)
        acc = (acc[:, :width] + acc[:, width:]) * tall(factor_ref[4 * block + 2], span)
        factor = tall(factor_ref[4 * block + 3], span)
        held[at, :] = (z_ref[at, :].astype(F32) * factor - acc).astype(BF16)
        copies.append(pltpu.make_async_copy(held.at[at, :], out_ref.at[at, :], sems.at[c]))
        copies[-1].start()
    for copy in copies:
        copy.wait()


def shards(snapshots, scales):
    points, _, rounds, width = snapshots.shape
    nblock = scales.shape[0]
    n_rows, n_cols = lax.axis_size("rows"), lax.axis_size("cols")
    root = math.sqrt(points * n_rows)
    long = points * rounds
    z = snapshots.reshape(long, width)
    group = lax.axis_index("cols")
    recv = partner(z, "cols", n_cols, 1)
    even = among_pairs(z, n_cols, group, 0)
    leads = (even, recv) if n_cols == 2 else (even, partner(even, "cols", n_cols, 1))
    phases = radices(n_rows)
    payload = width + 8
    params = pltpu.CompilerParams(vmem_limit_bytes=48 << 20)
    first, own, factors = pl.pallas_call(
        functools.partial(split_kernel, rounds, nblock),
        out_shape=[jax.ShapeDtypeStruct((points, width), BF16)] * 2 + [jax.ShapeDtypeStruct((4 * nblock, 8, width), F32)],
        in_specs=[pl.BlockSpec(memory_space=pltpu.HBM)] * 2,
        out_specs=[VMEM] * 3,
        scratch_shapes=[
            pltpu.VMEM(scales.shape, F32),
            pltpu.VMEM((long, width), BF16),
            pltpu.VMEM((long, width), F32),
            pltpu.SemaphoreType.DMA((nblock + 1,)),
        ],
        compiler_params=params,
        name="split",
    )(*[pltpu.with_memory_space_constraint(x, pltpu.HBM) for x in (scales, z)])
    extra = () if n_cols == 2 else leads
    sent = pl.pallas_call(
        functools.partial(products_kernel, rounds, nblock, phases),
        out_shape=[jax.ShapeDtypeStruct((payload, width), F32)] * 2,
        in_specs=[VMEM] * (4 + len(extra)),
        out_specs=[VMEM] * 2,
        scratch_shapes=[pltpu.VMEM((long, width), F32), pltpu.VMEM((2 * width, width), F32)]
        + [pltpu.VMEM((long, width), F32)] * (len(extra) // 2),
        compiler_params=params,
        name="products",
    )(factors, first, own, recv, *extra)
    sums = sent[0]
    for step, (_, base) in enumerate(phases):
        source = sent if step == 0 else [sums] * 2
        others = [
            hop(source[b % 2], n_rows, n_cols, lambda parity: b * order(phases, parity)[step][0]) for b in range(1, base)
        ]
        if step == len(phases) - 1:
            lead = pl.pallas_call(
                functools.partial(spread_kernel, rounds),
                out_shape=jax.ShapeDtypeStruct((long, rounds * width), BF16),
                in_specs=[VMEM, VMEM],
                out_specs=VMEM,
                compiler_params=params,
                name="spread",
            )(*leads)
            *others, lead = lax.optimization_barrier((*others, lead))
        for other in others:
            sums = sums + other
    beside = lambda parity: order(phases, parity)[0][0]
    gathered = hop(sums, n_rows, n_cols, beside)
    inverse, block = pl.pallas_call(
        factor_kernel,
        out_shape=[jax.ShapeDtypeStruct((width, width), F32)] * 2,
        in_specs=[VMEM],
        out_specs=[VMEM] * 2,
        compiler_params=params,
        cost_estimate=pl.CostEstimate(flops=1 << 30, bytes_accessed=1 << 23, transcendentals=0),
        name="factor",
    )(sums)
    inverse = among_pairs(inverse, n_cols, group, 1)
    swapped = partner(inverse, "cols", n_cols, 1)
    blocks = partner(block, "cols", n_cols, 1)
    gathered, _ = lax.optimization_barrier((gathered, block))
    crossed = partner(gathered[: width // 2 + 8], "cols", n_cols, 1)
    chunks = 2 * nblock
    coef, updated = pl.pallas_call(
        functools.partial(finish_kernel, rounds, nblock, phases, root, chunks),
        out_shape=[
            jax.ShapeDtypeStruct((width * rounds, width), F32),
            jax.ShapeDtypeStruct((long, width), BF16),
        ],
        in_specs=[VMEM] * 9,
        out_specs=[pl.BlockSpec(memory_space=pl.ANY)] * 2,
        scratch_shapes=[
            pltpu.VMEM((width, width), F32),
            pltpu.VMEM((width, width), F32),
            pltpu.VMEM((width * rounds, width), F32),
            pltpu.VMEM((long, width), BF16),
            pltpu.SemaphoreType.DMA((chunks + 1,)),
        ],
        compiler_params=params,
        name="finish",
    )(factors, z, lead, inverse, swapped, sums, gathered, blocks, crossed)
    return coef.reshape(width, 1, rounds, width), updated.reshape(snapshots.shape)


def solution(mesh):
    return jax.shard_map(
        shards,
        mesh=mesh,
        in_specs=(P("rows", "cols", None, None), P("rows", None, None)),
        out_specs=(P(None, "cols", None, None), P("rows", "cols", None, None)),
        check_vma=False,
    )
```

```python
import functools
import math

import jax
import jax.numpy as jnp
from jax import lax
from jax.experimental import pallas as pl
from jax.experimental.pallas import tpu as pltpu
from jax.sharding import PartitionSpec as P

F32 = jnp.float32
BF16 = jnp.bfloat16
VMEM = pl.BlockSpec(memory_space=pltpu.VMEM)


def partner(x, axis, count, offset):
    return lax.ppermute(x, axis, [(i, i ^ offset) for i in range(count)])


def radices(count):
    found = []
    stride = 1
    while stride < count:
        radix = 4 if (count // stride) % 4 == 0 else 2
        found.append((stride, radix))
        stride *= radix
    return found


def order(phases, parity):
    if parity == 0 and len({radix for _, radix in phases}) == 1:
        return phases[::-1]
    return phases


def hop(x, n_rows, n_cols, offset, turn=0):
    pairs = []
    for row in range(n_rows):
        for col in range(n_cols):
            pairs.append((row * n_cols + col, (row ^ offset(col % 2)) * n_cols + (col ^ turn)))
    return lax.ppermute(x, ("rows", "cols"), pairs)


def half_digit(phases, parity):
    even, odd = [(lax.axis_index("rows") // order(phases, p)[0][0]) % 2 for p in range(2)]
    return jnp.where(parity == 0, even, odd)


def among_pairs(x, count, mine, root):
    stride = 2
    while stride < count:
        x = jnp.where(((mine ^ root) & stride) != 0, partner(x, "cols", count, stride), x)
        stride *= 2
    return x


def lanes(x, p):
    return jnp.broadcast_to(x[:, p : p + 1], x.shape)


def sublanes(x, j):
    return jnp.broadcast_to(x[j : j + 1, :], x.shape)


def thirds(x):
    high = x.astype(BF16)
    rest = x - high.astype(F32)
    middle = rest.astype(BF16)
    return high, middle, (rest - middle.astype(F32)).astype(BF16)


def product(left, right):
    return product_of_thirds(thirds(left), thirds(right))


def product_of_thirds(left, right):
    columns = right[0].shape[1]
    wide = jnp.concatenate(right[:2], axis=1)
    both = jnp.dot(
        jnp.concatenate(left[:2], axis=1), jnp.concatenate([wide, wide], axis=0), preferred_element_type=F32
    )
    small = jnp.dot(
        jnp.concatenate([left[0], left[2]], axis=1),
        jnp.concatenate([right[2], right[0]], axis=0),
        preferred_element_type=F32,
    )
    return (both[:, :columns] + both[:, columns:]) + small


def lower_inverse(rows, width):
    n = len(rows)
    rid = lax.broadcasted_iota(jnp.int32, (8, width), 0)
    cid = lax.broadcasted_iota(jnp.int32, (8, width), 1)
    done = []
    for k in range(n):
        base = 8 * k
        held = rows[k]
        columns = [lanes(held, base + j) for j in range(8)]
        inside = (cid >= base) & (cid < base + 8)
        eye = jnp.where(cid - base == rid, 1.0, 0.0).astype(F32)
        full = jnp.where(inside, eye, held)
        forward = full
        scale = jnp.zeros((8, width), F32)
        inverses = []
        for j in range(0, 8, 2):
            left, right = columns[j], columns[j + 1]
            a, b, c = sublanes(left, j), sublanes(right, j), sublanes(right, j + 1)
            det = a * c - b * b
            inverse, inverse_a = 1.0 / det, 1.0 / a
            pair = (rid == j) | (rid == j + 1)
            left, right = jnp.where(pair, 0.0, left), jnp.where(pair, 0.0, right)
            first, second = (left * c - right * b) * inverse, (right * a - left * b) * inverse
            for m in range(j + 2, 8):
                columns[m] = columns[m] - (first * sublanes(columns[m], j) + second * sublanes(columns[m], j + 1))
            full = full - (first * sublanes(full, j) + second * sublanes(full, j + 1))
            below = rid > j + 1
            first = jnp.where(below, first, jnp.where(rid == j + 1, b * inverse_a, 0.0))
            second = jnp.where(below, second, 0.0)
            forward = forward - (first * sublanes(forward, j) + second * sublanes(forward, j + 1))
            scale = jnp.where(rid == j, lax.rsqrt(a), jnp.where(rid == j + 1, lax.rsqrt(det * inverse_a), scale))
            inverses.append((a * inverse, b * inverse, c * inverse))
        done.append(jnp.where(cid <= rid + base, forward * scale, 0.0))
        if k + 1 == n:
            break
        spread = []
        for j, (a, b, c) in enumerate(inverses):
            above, under = sublanes(full, 2 * j), sublanes(full, 2 * j + 1)
            spread += [above * c - under * b, under * a - above * b]
        terms = [lanes(rows[k + 1], base + j) * spread[j] for j in range(8)]
        while len(terms) > 1:
            terms = [terms[q] + terms[q + 1] for q in range(0, len(terms), 2)]
        rows[k + 1] = jnp.where(inside, 0.0, rows[k + 1]) - terms[0]
        if k + 2 == n:
            continue
        solved = jnp.zeros((8, width), F32)
        for j in range(8):
            solved = jnp.where(rid == j, spread[j], solved)
        far = jnp.concatenate(rows[k + 2 :], axis=0)
        column = lax.broadcasted_iota(jnp.int32, far.shape, 1)
        within = (column >= base) & (column < base + 8)
        placed = []
        for third in thirds(solved):
            blocks = [jnp.zeros((base, width), F32)] if base else []
            blocks += [third.astype(F32), jnp.zeros((width - base - 8, width), F32)]
            placed.append(jnp.concatenate(blocks, axis=0).astype(BF16))
        update = product_of_thirds(thirds(jnp.where(within, far, 0.0)), placed)
        far = jnp.where(within, 0.0, far) - update
        for i in range(k + 2, n):
            rows[i] = far[8 * (i - k - 2) : 8 * (i - k - 1)]
    return done


def pack(gram):
    width = gram.shape[0]
    half = width // 2
    row = lax.broadcasted_iota(jnp.int32, (half, width), 0)
    col = lax.broadcasted_iota(jnp.int32, (half, width), 1)
    turned = pltpu.roll(gram[half:, :], half, 1)
    both = jnp.where((col < half) & (row < col), turned, gram[:half, :])
    diagonal = jnp.sum(jnp.where(row + half == col, gram[half:, :], 0.0), axis=0, keepdims=True)
    return jnp.concatenate([both, jnp.broadcast_to(diagonal, (8, width))], axis=0)


def unpack(packed):
    width = packed.shape[1]
    half = width // 2
    row = lax.broadcasted_iota(jnp.int32, (width, width), 0)
    col = lax.broadcasted_iota(jnp.int32, (width, width), 1)
    both = packed[:half, :]
    square = jnp.concatenate([both, pltpu.roll(both, half, 1)], axis=0)
    direct = ((row < half) & ((col >= half) | (col <= row))) | ((row >= half) & (col >= half) & (col > row))
    gram = jnp.where(direct, square, square.T)
    return jnp.where((row == col) & (row >= half), jnp.broadcast_to(packed[half : half + 1, :], gram.shape), gram)


def leading(even_ref, odd_ref):
    return jnp.where(lax.axis_index("cols") % 2 == 0, even_ref[...], odd_ref[...])


def tall(tile, rows):
    return jnp.broadcast_to(tile[None], (rows // 8, *tile.shape)).reshape(rows, tile.shape[1])


def split_kernel(rounds, nblock, scale_hbm, z_hbm, first_ref, own_ref, factor_ref, scale_ref, z_ref, wide, sems):
    group = lax.axis_index("cols")
    odd = group % 2
    width = z_ref.shape[1]
    span = z_ref.shape[0] // nblock
    points = span // rounds
    scale_copy = pltpu.make_async_copy(scale_hbm, scale_ref, sems.at[nblock])
    scale_copy.start()
    copies = []
    for b in range(nblock):
        at = slice(b * span, (b + 1) * span)
        copies.append(pltpu.make_async_copy(z_hbm.at[at, :], z_ref.at[at, :], sems.at[b]))
        copies[b].start()
    scale_copy.wait()
    row = lax.broadcasted_iota(jnp.int32, (8, width), 0)
    for b in range(nblock):
        lead = jnp.broadcast_to(scale_ref[b, 0:1, 0:1], (8, width))
        mine = scale_ref[b, pl.ds(group, 1), :]
        theirs = scale_ref[b, pl.ds(group + 1 - 2 * odd, 1), :]
        mine, theirs = [[jnp.broadcast_to(x[:, r : r + 1], (8, width)) for r in range(2)] for x in (mine, theirs)]
        factor_ref[4 * b] = lead * jnp.where(odd == 1, theirs[0], theirs[1])
        factor_ref[4 * b + 1] = lead * jnp.where(odd == 1, mine[0], mine[1])
        factor_ref[4 * b + 2] = lead
        factor_ref[4 * b + 3] = jnp.where(row % rounds == 0, jnp.where(group == 0, 0.0, mine[0]), mine[1])
    for b in range(nblock):
        copies[b].wait()
        at = slice(b * span, (b + 1) * span)
        wide[at, :] = z_ref[at, :].astype(F32)
        first = wide[pl.ds(b * span, points, stride=rounds), :].astype(BF16)
        last = wide[pl.ds(b * span + 1, points, stride=rounds), :].astype(BF16)
        first_ref[b * points : (b + 1) * points, :] = first
        own_ref[b * points : (b + 1) * points, :] = jnp.where(odd == 1, first, last)


def products_kernel(rounds, nblock, phases, factor_ref, first_ref, own_ref, recv_ref, *rest):
    lead_ref = () if len(rest) == 6 else (*rest[:2], rest[-1])
    same_ref, other_ref, again_ref, fourth_ref, wide, cross = rest if len(rest) == 6 else rest[2:-1]
    group = lax.axis_index("cols")
    odd = group % 2
    digit = half_digit(phases, odd)
    width = recv_ref.shape[1]
    points = own_ref.shape[0] // nblock
    half = width // 2
    height = half + 8
    wide[...] = recv_ref[...].astype(F32)
    if lead_ref:
        lead_ref[2][...] = leading(*lead_ref[:2]).astype(F32)
    out = jnp.zeros((width, 2 * width), F32)
    for b in range(nblock):
        at = slice(b * points, (b + 1) * points)
        start = b * points * rounds
        theirs = wide[pl.ds(start + 1 - odd, points, stride=rounds), :].astype(BF16)
        if lead_ref:
            panel = lead_ref[2][pl.ds(start, points, stride=rounds), :].astype(BF16)
        else:
            panel = jnp.where(odd == 1, theirs, first_ref[at, :])
        block = lax.dot_general(
            panel, jnp.concatenate([theirs, own_ref[at, :]], axis=1), (((0,), (0,)), ((), ())), preferred_element_type=F32
        )
        left = block[:, :width] * tall(factor_ref[4 * b], width)
        right = block[:, width:] * tall(factor_ref[4 * b + 1], width)
        out = out + jnp.concatenate([left, right], axis=1)
    packed = pack(out[:, :width])
    cross[:width, :] = out[:, :width]
    cross[width:, :] = out[:, width:]
    for ref, place in ((same_ref, digit), (other_ref, 1 - digit), (again_ref, 1 - digit), (fourth_ref, digit)):
        theirs = cross[pl.ds(pl.multiple_of(place * half, half), half), :]
        ref[:half, :] = jnp.where(group == 1, packed[:half, :], theirs)
        ref[half:height, :] = packed[half:, :]
        ref[height : height + half, :] = cross[pl.ds(pl.multiple_of(width + place * half, half), half), :]
        ref[height + half :, :] = jnp.zeros((8, width), F32)


def spread_kernel(rounds, even_ref, odd_ref, out_ref):
    width = even_ref.shape[1]
    rows = lax.broadcasted_iota(jnp.int32, even_ref.shape, 0) % rounds
    lead = leading(even_ref, odd_ref).astype(F32)
    for r in range(rounds):
        moved = lead if r == 0 else pltpu.roll(lead, r, 0)
        out_ref[:, r * width : (r + 1) * width] = jnp.where(rows == r, moved, 0.0).astype(BF16)


def factor_kernel(sums_ref, inverse_ref, block_ref):
    width = sums_ref.shape[1]
    height = width // 2 + 8
    group = lax.axis_index("cols")

    @pl.when(group == 1)
    def _():
        gram = unpack(sums_ref[:height, :])
        block_ref[:width, :] = gram
        block_ref[width:, :] = jnp.zeros((8, width), F32)
        rows = [gram[8 * i : 8 * i + 8, :] for i in range(width // 8)]
        for i, row in enumerate(lower_inverse(rows, width)):
            inverse_ref[8 * i : 8 * i + 8, :] = row

    @pl.when(group != 1)
    def _():
        inverse_ref[...] = jnp.zeros((width, width), F32)
        block_ref[:height, :] = sums_ref[:height, :]
        block_ref[height:, :] = jnp.zeros((width + 8 - height, width), F32)


def finish_kernel(
    rounds, nblock, phases, root, chunks, factor_ref, z_ref, lead_ref, kept_ref, recv_ref, same_ref, gathered_ref, block_ref, across_ref,
    coef_ref, out_ref, mine, theirs, coef, held, sems,
):
    group = lax.axis_index("cols")
    odd = group % 2 == 1
    width = z_ref.shape[1]
    half = width // 2
    height = half + 8
    own_digit, pair_digit = half_digit(phases, group % 2), half_digit(phases, 1 - group % 2)
    for own_rows, pair_rows, other in ((same_ref, block_ref, 0), (gathered_ref, across_ref, 1)):
        mine[pl.ds(pl.multiple_of((own_digit ^ other) * half, half), half), :] = own_rows[height : height + half, :]
        theirs[pl.ds(pl.multiple_of((pair_digit ^ other) * half, half), half), :] = pair_rows[:half, :]
    own_block = mine[...]
    pair_block = jnp.where(group == 0, block_ref[...], theirs[...])
    cross = jnp.concatenate([jnp.where(odd, own_block, pair_block), jnp.where(odd, pair_block, own_block)], axis=1)
    inverse = jnp.where(odd, kept_ref[...], recv_ref[...])
    across = inverse.T
    raw = product(inverse, cross)
    for r in range(rounds):
        coef[pl.ds(r, width, stride=rounds), :] = raw[:, r * width : (r + 1) * width] * (1.0 / root)
    copies = [pltpu.make_async_copy(coef, coef_ref, sems.at[chunks])]
    copies[0].start()
    weights = product(across, raw)
    stacked = []
    for r in range(rounds):
        weight = weights[:, r * width : (r + 1) * width]
        if r == 0:
            weight = jnp.where(group == 0, -root * across, weight)
        upper = weight.astype(BF16)
        stacked.append(jnp.concatenate([upper, (weight - upper.astype(F32)).astype(BF16)], axis=1))
    weight = jnp.concatenate(stacked, axis=0)
    span = z_ref.shape[0] // chunks
    for c in range(chunks):
        block = c * nblock // chunks
        at = slice(c * span, (c + 1) * span)
        acc = jnp.dot(lead_ref[at, :], weight, preferred_element_type=F32)
        acc = (acc[:, :width] + acc[:, width:]) * tall(factor_ref[4 * block + 2], span)
        factor = tall(factor_ref[4 * block + 3], span)
        held[at, :] = (z_ref[at, :].astype(F32) * factor - acc).astype(BF16)
        copies.append(pltpu.make_async_copy(held.at[at, :], out_ref.at[at, :], sems.at[c]))
        copies[-1].start()
    for copy in copies:
        copy.wait()


def shards(snapshots, scales):
    points, _, rounds, width = snapshots.shape
    nblock = scales.shape[0]
    n_rows, n_cols = lax.axis_size("rows"), lax.axis_size("cols")
    root = math.sqrt(points * n_rows)
    long = points * rounds
    z = snapshots.reshape(long, width)
    group = lax.axis_index("cols")
    recv = partner(z, "cols", n_cols, 1)
    even = among_pairs(z, n_cols, group, 0)
    leads = (even, recv) if n_cols == 2 else (even, partner(even, "cols", n_cols, 1))
    phases = radices(n_rows)
    payload = width + 16
    params = pltpu.CompilerParams(vmem_limit_bytes=48 << 20)
    first, own, factors = pl.pallas_call(
        functools.partial(split_kernel, rounds, nblock),
        out_shape=[jax.ShapeDtypeStruct((points, width), BF16)] * 2 + [jax.ShapeDtypeStruct((4 * nblock, 8, width), F32)],
        in_specs=[pl.BlockSpec(memory_space=pltpu.HBM)] * 2,
        out_specs=[VMEM] * 3,
        scratch_shapes=[
            pltpu.VMEM(scales.shape, F32),
            pltpu.VMEM((long, width), BF16),
            pltpu.VMEM((long, width), F32),
            pltpu.SemaphoreType.DMA((nblock + 1,)),
        ],
        compiler_params=params,
        name="split",
    )(*[pltpu.with_memory_space_constraint(x, pltpu.HBM) for x in (scales, z)])
    extra = () if n_cols == 2 else leads
    sent = pl.pallas_call(
        functools.partial(products_kernel, rounds, nblock, phases),
        out_shape=[jax.ShapeDtypeStruct((payload, width), F32)] * 4,
        in_specs=[VMEM] * (4 + len(extra)),
        out_specs=[VMEM] * 4,
        scratch_shapes=[pltpu.VMEM((long, width), F32), pltpu.VMEM((2 * width, width), F32)]
        + [pltpu.VMEM((long, width), F32)] * (len(extra) // 2),
        compiler_params=params,
        name="products",
    )(factors, first, own, recv, *extra)
    sums = sent[0]
    for step, (_, base) in enumerate(phases):
        source = (sent[0], sent[1], sent[3], sent[2]) if step == 0 else [sums] * base
        others = [
            hop(source[b], n_rows, n_cols, lambda parity: b * order(phases, parity)[step][0]) for b in (range(base - 1, 0, -1) if step == 0 else range(1, base))
        ]
        if step == len(phases) - 1:
            lead = pl.pallas_call(
                functools.partial(spread_kernel, rounds),
                out_shape=jax.ShapeDtypeStruct((long, rounds * width), BF16),
                in_specs=[VMEM, VMEM],
                out_specs=VMEM,
                compiler_params=params,
                name="spread",
            )(*leads)
            *others, lead = lax.optimization_barrier((*others, lead))
        for other in others:
            sums = sums + other
    beside = lambda parity: order(phases, parity)[0][0]
    gathered = hop(sums, n_rows, n_cols, beside)
    inverse, block = pl.pallas_call(
        factor_kernel,
        out_shape=[jax.ShapeDtypeStruct((width + pad, width), F32) for pad in (0, 8)],
        in_specs=[VMEM],
        out_specs=[VMEM] * 2,
        compiler_params=params,
        cost_estimate=pl.CostEstimate(flops=1 << 30, bytes_accessed=1 << 23, transcendentals=0),
        name="factor",
    )(sums)
    inverse = among_pairs(inverse, n_cols, group, 1)
    swapped = partner(inverse, "cols", n_cols, 1)
    blocks = partner(block[:width], "cols", n_cols, 1)
    crossed = hop(block, n_rows, n_cols, beside, 1)
    chunks = 2 * nblock
    coef, updated = pl.pallas_call(
        functools.partial(finish_kernel, rounds, nblock, phases, root, chunks),
        out_shape=[
            jax.ShapeDtypeStruct((width * rounds, width), F32),
            jax.ShapeDtypeStruct((long, width), BF16),
        ],
        in_specs=[VMEM] * 9,
        out_specs=[pl.BlockSpec(memory_space=pl.ANY)] * 2,
        scratch_shapes=[
            pltpu.VMEM((width, width), F32),
            pltpu.VMEM((width, width), F32),
            pltpu.VMEM((width * rounds, width), F32),
            pltpu.VMEM((long, width), BF16),
            pltpu.SemaphoreType.DMA((chunks + 1,)),
        ],
        compiler_params=params,
        name="finish",
    )(factors, z, lead, inverse, swapped, sums, gathered, blocks, crossed)
    return coef.reshape(width, 1, rounds, width), updated.reshape(snapshots.shape)


def solution(mesh):
    return jax.shard_map(
        shards,
        mesh=mesh,
        in_specs=(P("rows", "cols", None, None), P("rows", None, None)),
        out_specs=(P(None, "cols", None, None), P("rows", "cols", None, None)),
        check_vma=False,
    )
```

```python
import functools
import math

import jax
import jax.numpy as jnp
from jax import lax
from jax.experimental import pallas as pl
from jax.experimental.pallas import tpu as pltpu
from jax.sharding import PartitionSpec as P

F32 = jnp.float32
BF16 = jnp.bfloat16
VMEM = pl.BlockSpec(memory_space=pltpu.VMEM)


def partner(x, axis, count, offset):
    return lax.ppermute(x, axis, [(i, i ^ offset) for i in range(count)])


def radices(count):
    found = []
    stride = 1
    while stride < count:
        radix = 4 if (count // stride) % 4 == 0 else 2
        found.append((stride, radix))
        stride *= radix
    return found


def order(phases, parity):
    if parity == 0 and len({radix for _, radix in phases}) == 1:
        return phases[::-1]
    return phases


def hop(x, n_rows, n_cols, offset, turn=0):
    pairs = []
    for row in range(n_rows):
        for col in range(n_cols):
            pairs.append((row * n_cols + col, (row ^ offset(col % 2)) * n_cols + (col ^ turn)))
    return lax.ppermute(x, ("rows", "cols"), pairs)


def half_digit(phases, parity):
    even, odd = [(lax.axis_index("rows") // order(phases, p)[0][0]) % 2 for p in range(2)]
    return jnp.where(parity == 0, even, odd)


def among_pairs(x, count, mine, root):
    stride = 2
    while stride < count:
        x = jnp.where(((mine ^ root) & stride) != 0, partner(x, "cols", count, stride), x)
        stride *= 2
    return x


def lanes(x, p):
    return jnp.broadcast_to(x[:, p : p + 1], x.shape)


def sublanes(x, j):
    return jnp.broadcast_to(x[j : j + 1, :], x.shape)


def thirds(x):
    high = x.astype(BF16)
    rest = x - high.astype(F32)
    middle = rest.astype(BF16)
    return high, middle, (rest - middle.astype(F32)).astype(BF16)


def product(left, right):
    return product_of_thirds(thirds(left), thirds(right))


def product_of_thirds(left, right):
    columns = right[0].shape[1]
    wide = jnp.concatenate(right[:2], axis=1)
    both = jnp.dot(
        jnp.concatenate(left[:2], axis=1), jnp.concatenate([wide, wide], axis=0), preferred_element_type=F32
    )
    small = jnp.dot(
        jnp.concatenate([left[0], left[2]], axis=1),
        jnp.concatenate([right[2], right[0]], axis=0),
        preferred_element_type=F32,
    )
    return (both[:, :columns] + both[:, columns:]) + small


def lower_inverse(rows, width):
    n = len(rows)
    rid = lax.broadcasted_iota(jnp.int32, (8, width), 0)
    cid = lax.broadcasted_iota(jnp.int32, (8, width), 1)
    done = []
    for k in range(n):
        base = 8 * k
        held = rows[k]
        columns = [lanes(held, base + j) for j in range(8)]
        inside = (cid >= base) & (cid < base + 8)
        eye = jnp.where(cid - base == rid, 1.0, 0.0).astype(F32)
        full = jnp.where(inside, eye, held)
        forward = full
        scale = jnp.zeros((8, width), F32)
        inverses = []
        for j in range(0, 8, 2):
            left, right = columns[j], columns[j + 1]
            a, b, c = sublanes(left, j), sublanes(right, j), sublanes(right, j + 1)
            det = a * c - b * b
            inverse, inverse_a = 1.0 / det, 1.0 / a
            pair = (rid == j) | (rid == j + 1)
            left, right = jnp.where(pair, 0.0, left), jnp.where(pair, 0.0, right)
            first, second = (left * c - right * b) * inverse, (right * a - left * b) * inverse
            for m in range(j + 2, 8):
                columns[m] = columns[m] - (first * sublanes(columns[m], j) + second * sublanes(columns[m], j + 1))
            full = full - (first * sublanes(full, j) + second * sublanes(full, j + 1))
            below = rid > j + 1
            first = jnp.where(below, first, jnp.where(rid == j + 1, b * inverse_a, 0.0))
            second = jnp.where(below, second, 0.0)
            forward = forward - (first * sublanes(forward, j) + second * sublanes(forward, j + 1))
            scale = jnp.where(rid == j, lax.rsqrt(a), jnp.where(rid == j + 1, lax.rsqrt(det * inverse_a), scale))
            inverses.append((a * inverse, b * inverse, c * inverse))
        done.append(jnp.where(cid <= rid + base, forward * scale, 0.0))
        if k + 1 == n:
            break
        spread = []
        for j, (a, b, c) in enumerate(inverses):
            above, under = sublanes(full, 2 * j), sublanes(full, 2 * j + 1)
            spread += [above * c - under * b, under * a - above * b]
        terms = [lanes(rows[k + 1], base + j) * spread[j] for j in range(8)]
        while len(terms) > 1:
            terms = [terms[q] + terms[q + 1] for q in range(0, len(terms), 2)]
        rows[k + 1] = jnp.where(inside, 0.0, rows[k + 1]) - terms[0]
        if k + 2 == n:
            continue
        solved = jnp.zeros((8, width), F32)
        for j in range(8):
            solved = jnp.where(rid == j, spread[j], solved)
        far = jnp.concatenate(rows[k + 2 :], axis=0)
        column = lax.broadcasted_iota(jnp.int32, far.shape, 1)
        within = (column >= base) & (column < base + 8)
        placed = []
        for third in thirds(solved):
            blocks = [jnp.zeros((base, width), F32)] if base else []
            blocks += [third.astype(F32), jnp.zeros((width - base - 8, width), F32)]
            placed.append(jnp.concatenate(blocks, axis=0).astype(BF16))
        update = product_of_thirds(thirds(jnp.where(within, far, 0.0)), placed)
        far = jnp.where(within, 0.0, far) - update
        for i in range(k + 2, n):
            rows[i] = far[8 * (i - k - 2) : 8 * (i - k - 1)]
    return done


def pack(gram):
    width = gram.shape[0]
    half = width // 2
    row = lax.broadcasted_iota(jnp.int32, (half, width), 0)
    col = lax.broadcasted_iota(jnp.int32, (half, width), 1)
    turned = pltpu.roll(gram[half:, :], half, 1)
    both = jnp.where((col < half) & (row < col), turned, gram[:half, :])
    diagonal = jnp.sum(jnp.where(row + half == col, gram[half:, :], 0.0), axis=0, keepdims=True)
    return jnp.concatenate([both, jnp.broadcast_to(diagonal, (8, width))], axis=0)


def unpack(packed):
    width = packed.shape[1]
    half = width // 2
    row = lax.broadcasted_iota(jnp.int32, (width, width), 0)
    col = lax.broadcasted_iota(jnp.int32, (width, width), 1)
    both = packed[:half, :]
    square = jnp.concatenate([both, pltpu.roll(both, half, 1)], axis=0)
    direct = ((row < half) & ((col >= half) | (col <= row))) | ((row >= half) & (col >= half) & (col > row))
    gram = jnp.where(direct, square, square.T)
    return jnp.where((row == col) & (row >= half), jnp.broadcast_to(packed[half : half + 1, :], gram.shape), gram)


def leading(even_ref, odd_ref):
    return jnp.where(lax.axis_index("cols") % 2 == 0, even_ref[...], odd_ref[...])


def tall(tile, rows):
    return jnp.broadcast_to(tile[None], (rows // 8, *tile.shape)).reshape(rows, tile.shape[1])


def split_kernel(rounds, nblock, scale_hbm, z_hbm, first_ref, own_ref, factor_ref, scale_ref, z_ref, wide, sems):
    group = lax.axis_index("cols")
    odd = group % 2
    width = z_ref.shape[1]
    span = z_ref.shape[0] // nblock
    points = span // rounds
    scale_copy = pltpu.make_async_copy(scale_hbm, scale_ref, sems.at[nblock])
    scale_copy.start()
    copies = []
    for b in range(nblock):
        at = slice(b * span, (b + 1) * span)
        copies.append(pltpu.make_async_copy(z_hbm.at[at, :], z_ref.at[at, :], sems.at[b]))
        copies[b].start()
    scale_copy.wait()
    row = lax.broadcasted_iota(jnp.int32, (8, width), 0)
    for b in range(nblock):
        lead = jnp.broadcast_to(scale_ref[b, 0:1, 0:1], (8, width))
        mine = scale_ref[b, pl.ds(group, 1), :]
        theirs = scale_ref[b, pl.ds(group + 1 - 2 * odd, 1), :]
        mine, theirs = [[jnp.broadcast_to(x[:, r : r + 1], (8, width)) for r in range(2)] for x in (mine, theirs)]
        factor_ref[4 * b] = lead * jnp.where(odd == 1, theirs[0], theirs[1])
        factor_ref[4 * b + 1] = lead * jnp.where(odd == 1, mine[0], mine[1])
        factor_ref[4 * b + 2] = lead
        factor_ref[4 * b + 3] = jnp.where(row % rounds == 0, jnp.where(group == 0, 0.0, mine[0]), mine[1])
    for b in range(nblock):
        copies[b].wait()
        at = slice(b * span, (b + 1) * span)
        wide[at, :] = z_ref[at, :].astype(F32)
        first = wide[pl.ds(b * span, points, stride=rounds), :].astype(BF16)
        last = wide[pl.ds(b * span + 1, points, stride=rounds), :].astype(BF16)
        first_ref[b * points : (b + 1) * points, :] = first
        own_ref[b * points : (b + 1) * points, :] = jnp.where(odd == 1, first, last)


def products_kernel(rounds, nblock, phases, factor_ref, first_ref, own_ref, recv_ref, *rest):
    lead_ref = () if len(rest) == 6 else (*rest[:2], rest[-1])
    same_ref, other_ref, again_ref, fourth_ref, wide, cross = rest if len(rest) == 6 else rest[2:-1]
    group = lax.axis_index("cols")
    odd = group % 2
    digit = half_digit(phases, odd)
    width = recv_ref.shape[1]
    points = own_ref.shape[0] // nblock
    half = width // 2
    height = half + 8
    wide[...] = recv_ref[...].astype(F32)
    if lead_ref:
        lead_ref[2][...] = leading(*lead_ref[:2]).astype(F32)
    out = jnp.zeros((width, 2 * width), F32)
    for b in range(nblock):
        at = slice(b * points, (b + 1) * points)
        start = b * points * rounds
        theirs = wide[pl.ds(start + 1 - odd, points, stride=rounds), :].astype(BF16)
        if lead_ref:
            panel = lead_ref[2][pl.ds(start, points, stride=rounds), :].astype(BF16)
        else:
            panel = jnp.where(odd == 1, theirs, first_ref[at, :])
        block = lax.dot_general(
            panel, jnp.concatenate([theirs, own_ref[at, :]], axis=1), (((0,), (0,)), ((), ())), preferred_element_type=F32
        )
        left = block[:, :width] * tall(factor_ref[4 * b], width)
        right = block[:, width:] * tall(factor_ref[4 * b + 1], width)
        out = out + jnp.concatenate([left, right], axis=1)
    packed = pack(out[:, :width])
    cross[:width, :] = out[:, :width]
    cross[width:, :] = out[:, width:]
    for ref, place in ((same_ref, digit), (other_ref, 1 - digit), (again_ref, 1 - digit), (fourth_ref, digit)):
        theirs = cross[pl.ds(pl.multiple_of(place * half, half), half), :]
        ref[:half, :] = jnp.where(group == 1, packed[:half, :], theirs)
        ref[half:height, :] = packed[half:, :]
        ref[height : height + half, :] = cross[pl.ds(pl.multiple_of(width + place * half, half), half), :]
        ref[height + half :, :] = jnp.zeros((8, width), F32)


def spread_kernel(rounds, even_ref, odd_ref, out_ref):
    width = even_ref.shape[1]
    rows = lax.broadcasted_iota(jnp.int32, even_ref.shape, 0) % rounds
    lead = leading(even_ref, odd_ref).astype(F32)
    for r in range(rounds):
        moved = lead if r == 0 else pltpu.roll(lead, r, 0)
        out_ref[:, r * width : (r + 1) * width] = jnp.where(rows == r, moved, 0.0).astype(BF16)


def factor_kernel(sums_ref, inverse_ref, block_ref):
    width = sums_ref.shape[1]
    height = width // 2 + 8
    group = lax.axis_index("cols")

    @pl.when(group == 1)
    def _():
        gram = unpack(sums_ref[:height, :])
        block_ref[:width, :] = gram
        block_ref[width:, :] = jnp.zeros((8, width), F32)
        rows = [gram[8 * i : 8 * i + 8, :] for i in range(width // 8)]
        for i, row in enumerate(lower_inverse(rows, width)):
            inverse_ref[8 * i : 8 * i + 8, :] = row

    @pl.when(group != 1)
    def _():
        inverse_ref[...] = jnp.zeros((width, width), F32)
        block_ref[:height, :] = sums_ref[:height, :]
        block_ref[height:, :] = jnp.zeros((width + 8 - height, width), F32)


def finish_kernel(
    rounds, nblock, phases, root, chunks, factor_ref, z_ref, lead_ref, kept_ref, recv_ref, same_ref, gathered_ref, block_ref, across_ref,
    coef_ref, out_ref, mine, theirs, coef, held, sems,
):
    group = lax.axis_index("cols")
    odd = group % 2 == 1
    width = z_ref.shape[1]
    half = width // 2
    height = half + 8
    own_digit, pair_digit = half_digit(phases, group % 2), half_digit(phases, 1 - group % 2)
    for own_rows, pair_rows, other in ((same_ref, block_ref, 0), (gathered_ref, across_ref, 1)):
        mine[pl.ds(pl.multiple_of((own_digit ^ other) * half, half), half), :] = own_rows[height : height + half, :]
        theirs[pl.ds(pl.multiple_of((pair_digit ^ other) * half, half), half), :] = pair_rows[:half, :]
    own_block = mine[...]
    pair_block = jnp.where(group == 0, block_ref[...], theirs[...])
    cross = jnp.concatenate([jnp.where(odd, own_block, pair_block), jnp.where(odd, pair_block, own_block)], axis=1)
    inverse = jnp.where(odd, kept_ref[...], recv_ref[...])
    across = inverse.T
    raw = product(inverse, cross)
    for r in range(rounds):
        coef[pl.ds(r, width, stride=rounds), :] = raw[:, r * width : (r + 1) * width] * (1.0 / root)
    copies = [pltpu.make_async_copy(coef, coef_ref, sems.at[chunks])]
    copies[0].start()
    weights = product(across, raw)
    stacked = []
    for r in range(rounds):
        weight = weights[:, r * width : (r + 1) * width]
        if r == 0:
            weight = jnp.where(group == 0, -root * across, weight)
        upper = weight.astype(BF16)
        stacked.append(jnp.concatenate([upper, (weight - upper.astype(F32)).astype(BF16)], axis=1))
    weight = jnp.concatenate(stacked, axis=0)
    span = z_ref.shape[0] // chunks
    for c in range(chunks):
        block = c * nblock // chunks
        at = slice(c * span, (c + 1) * span)
        acc = jnp.dot(lead_ref[at, :], weight, preferred_element_type=F32)
        acc = (acc[:, :width] + acc[:, width:]) * tall(factor_ref[4 * block + 2], span)
        factor = tall(factor_ref[4 * block + 3], span)
        held[at, :] = (z_ref[at, :].astype(F32) * factor - acc).astype(BF16)
        copies.append(pltpu.make_async_copy(held.at[at, :], out_ref.at[at, :], sems.at[c]))
        copies[-1].start()
    for copy in copies:
        copy.wait()


def shards(snapshots, scales):
    points, _, rounds, width = snapshots.shape
    nblock = scales.shape[0]
    n_rows, n_cols = lax.axis_size("rows"), lax.axis_size("cols")
    root = math.sqrt(points * n_rows)
    long = points * rounds
    z = snapshots.reshape(long, width)
    group = lax.axis_index("cols")
    recv = partner(z, "cols", n_cols, 1)
    even = among_pairs(z, n_cols, group, 0)
    leads = (even, recv) if n_cols == 2 else (even, partner(even, "cols", n_cols, 1))
    phases = radices(n_rows)
    payload = width + 16
    params = pltpu.CompilerParams(vmem_limit_bytes=48 << 20)
    first, own, factors = pl.pallas_call(
        functools.partial(split_kernel, rounds, nblock),
        out_shape=[jax.ShapeDtypeStruct((points, width), BF16)] * 2 + [jax.ShapeDtypeStruct((4 * nblock, 8, width), F32)],
        in_specs=[pl.BlockSpec(memory_space=pltpu.HBM)] * 2,
        out_specs=[VMEM] * 3,
        scratch_shapes=[
            pltpu.VMEM(scales.shape, F32),
            pltpu.VMEM((long, width), BF16),
            pltpu.VMEM((long, width), F32),
            pltpu.SemaphoreType.DMA((nblock + 1,)),
        ],
        compiler_params=params,
        name="split",
    )(*[pltpu.with_memory_space_constraint(x, pltpu.HBM) for x in (scales, z)])
    extra = () if n_cols == 2 else leads
    sent = pl.pallas_call(
        functools.partial(products_kernel, rounds, nblock, phases),
        out_shape=[jax.ShapeDtypeStruct((payload, width), F32)] * 4,
        in_specs=[VMEM] * (4 + len(extra)),
        out_specs=[VMEM] * 4,
        scratch_shapes=[pltpu.VMEM((long, width), F32), pltpu.VMEM((2 * width, width), F32)]
        + [pltpu.VMEM((long, width), F32)] * (len(extra) // 2),
        compiler_params=params,
        name="products",
    )(factors, first, own, recv, *extra)
    sums = sent[0]
    for step, (_, base) in enumerate(phases):
        source = (sent[0], sent[1], sent[3], sent[2]) if step == 0 else [sums] * base
        others = [
            hop(source[b], n_rows, n_cols, lambda parity: b * order(phases, parity)[step][0]) for b in (range(base - 1, 0, -1) if step == 0 else range(1, base))
        ]
        if step == len(phases) - 1:
            lead = pl.pallas_call(
                functools.partial(spread_kernel, rounds),
                out_shape=jax.ShapeDtypeStruct((long, rounds * width), BF16),
                in_specs=[VMEM, VMEM],
                out_specs=VMEM,
                compiler_params=params,
                name="spread",
            )(*leads)
            *others, lead = lax.optimization_barrier((*others, lead))
        for other in others:
            sums = sums + other
    beside = lambda parity: order(phases, parity)[0][0]
    gathered = hop(sums, n_rows, n_cols, beside)
    inverse, block = pl.pallas_call(
        factor_kernel,
        out_shape=[jax.ShapeDtypeStruct((width + pad, width), F32) for pad in (0, 8)],
        in_specs=[VMEM],
        out_specs=[VMEM] * 2,
        compiler_params=params,
        cost_estimate=pl.CostEstimate(flops=1 << 30, bytes_accessed=1 << 23, transcendentals=0),
        name="factor",
    )(sums)
    inverse = among_pairs(inverse, n_cols, group, 1)
    swapped = partner(inverse, "cols", n_cols, 1)
    blocks = partner(block[:width], "cols", n_cols, 1)
    crossed = hop(block, n_rows, n_cols, beside if n_cols > 2 else lambda parity: beside(0), 1)
    chunks = 2 * nblock
    coef, updated = pl.pallas_call(
        functools.partial(finish_kernel, rounds, nblock, phases, root, chunks),
        out_shape=[
            jax.ShapeDtypeStruct((width * rounds, width), F32),
            jax.ShapeDtypeStruct((long, width), BF16),
        ],
        in_specs=[VMEM] * 9,
        out_specs=[pl.BlockSpec(memory_space=pl.ANY)] * 2,
        scratch_shapes=[
            pltpu.VMEM((width, width), F32),
            pltpu.VMEM((width, width), F32),
            pltpu.VMEM((width * rounds, width), F32),
            pltpu.VMEM((long, width), BF16),
            pltpu.SemaphoreType.DMA((chunks + 1,)),
        ],
        compiler_params=params,
        name="finish",
    )(factors, z, lead, inverse, swapped, sums, gathered, blocks, crossed)
    return coef.reshape(width, 1, rounds, width), updated.reshape(snapshots.shape)


def solution(mesh):
    return jax.shard_map(
        shards,
        mesh=mesh,
        in_specs=(P("rows", "cols", None, None), P("rows", None, None)),
        out_specs=(P(None, "cols", None, None), P("rows", "cols", None, None)),
        check_vma=False,
    )
```

```python
import functools
import math

import jax
import jax.numpy as jnp
from jax import lax
from jax.experimental import pallas as pl
from jax.experimental.pallas import tpu as pltpu
from jax.sharding import PartitionSpec as P

F32 = jnp.float32
BF16 = jnp.bfloat16
VMEM = pl.BlockSpec(memory_space=pltpu.VMEM)


def partner(x, axis, count, offset):
    return lax.ppermute(x, axis, [(i, i ^ offset) for i in range(count)])


def radices(count):
    found = []
    stride = 1
    while stride < count:
        radix = 4 if (count // stride) % 4 == 0 else 2
        found.append((stride, radix))
        stride *= radix
    return found


def order(phases, parity):
    if parity == 0 and len({radix for _, radix in phases}) == 1:
        return phases[::-1]
    return phases


def hop(x, n_rows, n_cols, offset, turn=0):
    pairs = []
    for row in range(n_rows):
        for col in range(n_cols):
            pairs.append((row * n_cols + col, (row ^ offset(col % 2)) * n_cols + (col ^ turn)))
    return lax.ppermute(x, ("rows", "cols"), pairs)


def half_digit(phases, parity):
    even, odd = [(lax.axis_index("rows") // order(phases, p)[0][0]) % 2 for p in range(2)]
    return jnp.where(parity == 0, even, odd)


def among_pairs(x, count, mine, root):
    stride = 2
    while stride < count:
        x = jnp.where(((mine ^ root) & stride) != 0, partner(x, "cols", count, stride), x)
        stride *= 2
    return x


def lanes(x, p):
    return jnp.broadcast_to(x[:, p : p + 1], x.shape)


def sublanes(x, j):
    return jnp.broadcast_to(x[j : j + 1, :], x.shape)


def thirds(x):
    high = x.astype(BF16)
    rest = x - high.astype(F32)
    middle = rest.astype(BF16)
    return high, middle, (rest - middle.astype(F32)).astype(BF16)


def product(left, right):
    return product_of_thirds(thirds(left), thirds(right))


def product_of_thirds(left, right):
    columns = right[0].shape[1]
    wide = jnp.concatenate(right[:2], axis=1)
    both = jnp.dot(
        jnp.concatenate(left[:2], axis=1), jnp.concatenate([wide, wide], axis=0), preferred_element_type=F32
    )
    small = jnp.dot(
        jnp.concatenate([left[0], left[2]], axis=1),
        jnp.concatenate([right[2], right[0]], axis=0),
        preferred_element_type=F32,
    )
    return (both[:, :columns] + both[:, columns:]) + small


def lower_inverse(rows, width):
    n = len(rows)
    rid = lax.broadcasted_iota(jnp.int32, (8, width), 0)
    cid = lax.broadcasted_iota(jnp.int32, (8, width), 1)
    done = []
    for k in range(n):
        base = 8 * k
        held = rows[k]
        columns = [lanes(held, base + j) for j in range(8)]
        inside = (cid >= base) & (cid < base + 8)
        eye = jnp.where(cid - base == rid, 1.0, 0.0).astype(F32)
        full = jnp.where(inside, eye, held)
        forward = full
        scale = jnp.zeros((8, width), F32)
        inverses = []
        for j in range(0, 8, 2):
            left, right = columns[j], columns[j + 1]
            a, b, c = sublanes(left, j), sublanes(right, j), sublanes(right, j + 1)
            det = a * c - b * b
            inverse, inverse_a = 1.0 / det, 1.0 / a
            pair = (rid == j) | (rid == j + 1)
            left, right = jnp.where(pair, 0.0, left), jnp.where(pair, 0.0, right)
            first, second = (left * c - right * b) * inverse, (right * a - left * b) * inverse
            for m in range(j + 2, 8):
                columns[m] = columns[m] - (first * sublanes(columns[m], j) + second * sublanes(columns[m], j + 1))
            full = full - (first * sublanes(full, j) + second * sublanes(full, j + 1))
            below = rid > j + 1
            first = jnp.where(below, first, jnp.where(rid == j + 1, b * inverse_a, 0.0))
            second = jnp.where(below, second, 0.0)
            forward = forward - (first * sublanes(forward, j) + second * sublanes(forward, j + 1))
            scale = jnp.where(rid == j, lax.rsqrt(a), jnp.where(rid == j + 1, lax.rsqrt(det * inverse_a), scale))
            inverses.append((a * inverse, b * inverse, c * inverse))
        done.append(jnp.where(cid <= rid + base, forward * scale, 0.0))
        if k + 1 == n:
            break
        spread = []
        for j, (a, b, c) in enumerate(inverses):
            above, under = sublanes(full, 2 * j), sublanes(full, 2 * j + 1)
            spread += [above * c - under * b, under * a - above * b]
        terms = [lanes(rows[k + 1], base + j) * spread[j] for j in range(8)]
        while len(terms) > 1:
            terms = [terms[q] + terms[q + 1] for q in range(0, len(terms), 2)]
        rows[k + 1] = jnp.where(inside, 0.0, rows[k + 1]) - terms[0]
        if k + 2 == n:
            continue
        solved = jnp.zeros((8, width), F32)
        for j in range(8):
            solved = jnp.where(rid == j, spread[j], solved)
        far = jnp.concatenate(rows[k + 2 :], axis=0)
        column = lax.broadcasted_iota(jnp.int32, far.shape, 1)
        within = (column >= base) & (column < base + 8)
        placed = []
        for third in thirds(solved):
            blocks = [jnp.zeros((base, width), F32)] if base else []
            blocks += [third.astype(F32), jnp.zeros((width - base - 8, width), F32)]
            placed.append(jnp.concatenate(blocks, axis=0).astype(BF16))
        update = product_of_thirds(thirds(jnp.where(within, far, 0.0)), placed)
        far = jnp.where(within, 0.0, far) - update
        for i in range(k + 2, n):
            rows[i] = far[8 * (i - k - 2) : 8 * (i - k - 1)]
    return done


def pack(gram):
    width = gram.shape[0]
    half = width // 2
    row = lax.broadcasted_iota(jnp.int32, (half, width), 0)
    col = lax.broadcasted_iota(jnp.int32, (half, width), 1)
    turned = pltpu.roll(gram[half:, :], half, 1)
    both = jnp.where((col < half) & (row < col), turned, gram[:half, :])
    diagonal = jnp.sum(jnp.where(row + half == col, gram[half:, :], 0.0), axis=0, keepdims=True)
    return jnp.concatenate([both, jnp.broadcast_to(diagonal, (8, width))], axis=0)


def unpack(packed):
    width = packed.shape[1]
    half = width // 2
    row = lax.broadcasted_iota(jnp.int32, (width, width), 0)
    col = lax.broadcasted_iota(jnp.int32, (width, width), 1)
    both = packed[:half, :]
    square = jnp.concatenate([both, pltpu.roll(both, half, 1)], axis=0)
    direct = ((row < half) & ((col >= half) | (col <= row))) | ((row >= half) & (col >= half) & (col > row))
    gram = jnp.where(direct, square, square.T)
    return jnp.where((row == col) & (row >= half), jnp.broadcast_to(packed[half : half + 1, :], gram.shape), gram)


def leading(even_ref, odd_ref):
    return jnp.where(lax.axis_index("cols") % 2 == 0, even_ref[...], odd_ref[...])


def tall(tile, rows):
    return jnp.broadcast_to(tile[None], (rows // 8, *tile.shape)).reshape(rows, tile.shape[1])


def split_kernel(rounds, nblock, scale_hbm, z_hbm, first_ref, own_ref, factor_ref, scale_ref, z_ref, wide, sems):
    group = lax.axis_index("cols")
    odd = group % 2
    width = z_ref.shape[1]
    span = z_ref.shape[0] // nblock
    points = span // rounds
    scale_copy = pltpu.make_async_copy(scale_hbm, scale_ref, sems.at[nblock])
    scale_copy.start()
    copies = []
    for b in range(nblock):
        at = slice(b * span, (b + 1) * span)
        copies.append(pltpu.make_async_copy(z_hbm.at[at, :], z_ref.at[at, :], sems.at[b]))
        copies[b].start()
    scale_copy.wait()
    row = lax.broadcasted_iota(jnp.int32, (8, width), 0)
    for b in range(nblock):
        lead = jnp.broadcast_to(scale_ref[b, 0:1, 0:1], (8, width))
        mine = scale_ref[b, pl.ds(group, 1), :]
        theirs = scale_ref[b, pl.ds(group + 1 - 2 * odd, 1), :]
        mine, theirs = [[jnp.broadcast_to(x[:, r : r + 1], (8, width)) for r in range(2)] for x in (mine, theirs)]
        factor_ref[4 * b] = lead * jnp.where(odd == 1, theirs[0], theirs[1])
        factor_ref[4 * b + 1] = lead * jnp.where(odd == 1, mine[0], mine[1])
        factor_ref[4 * b + 2] = lead
        factor_ref[4 * b + 3] = jnp.where(row % rounds == 0, jnp.where(group == 0, 0.0, mine[0]), mine[1])
    for b in range(nblock):
        copies[b].wait()
        at = slice(b * span, (b + 1) * span)
        wide[at, :] = z_ref[at, :].astype(F32)
        first = wide[pl.ds(b * span, points, stride=rounds), :].astype(BF16)
        last = wide[pl.ds(b * span + 1, points, stride=rounds), :].astype(BF16)
        first_ref[b * points : (b + 1) * points, :] = first
        own_ref[b * points : (b + 1) * points, :] = jnp.where(odd == 1, first, last)


def products_kernel(rounds, nblock, phases, factor_ref, first_ref, own_ref, recv_ref, *rest):
    lead_ref = () if len(rest) == 6 else (*rest[:2], rest[-1])
    same_ref, other_ref, again_ref, fourth_ref, wide, cross = rest if len(rest) == 6 else rest[2:-1]
    group = lax.axis_index("cols")
    odd = group % 2
    digit = half_digit(phases, odd)
    width = recv_ref.shape[1]
    points = own_ref.shape[0] // nblock
    half = width // 2
    height = half + 8
    wide[...] = recv_ref[...].astype(F32)
    if lead_ref:
        lead_ref[2][...] = leading(*lead_ref[:2]).astype(F32)
    out = jnp.zeros((width, 2 * width), F32)
    for b in range(nblock):
        at = slice(b * points, (b + 1) * points)
        start = b * points * rounds
        theirs = wide[pl.ds(start + 1 - odd, points, stride=rounds), :].astype(BF16)
        if lead_ref:
            panel = lead_ref[2][pl.ds(start, points, stride=rounds), :].astype(BF16)
        else:
            panel = jnp.where(odd == 1, theirs, first_ref[at, :])
        block = lax.dot_general(
            panel, jnp.concatenate([theirs, own_ref[at, :]], axis=1), (((0,), (0,)), ((), ())), preferred_element_type=F32
        )
        left = block[:, :width] * tall(factor_ref[4 * b], width)
        right = block[:, width:] * tall(factor_ref[4 * b + 1], width)
        out = out + jnp.concatenate([left, right], axis=1)
    packed = pack(out[:, :width])
    cross[:width, :] = out[:, :width]
    cross[width:, :] = out[:, width:]
    for ref, place in ((same_ref, digit), (other_ref, 1 - digit), (again_ref, 1 - digit), (fourth_ref, digit)):
        theirs = cross[pl.ds(pl.multiple_of(place * half, half), half), :]
        ref[:half, :] = jnp.where(group == 1, packed[:half, :], theirs)
        ref[half:height, :] = packed[half:, :]
        ref[height:, :] = cross[pl.ds(pl.multiple_of(width + place * half, half), half), :]


def spread_kernel(rounds, even_ref, odd_ref, out_ref):
    width = even_ref.shape[1]
    rows = lax.broadcasted_iota(jnp.int32, even_ref.shape, 0) % rounds
    lead = leading(even_ref, odd_ref).astype(F32)
    for r in range(rounds):
        moved = lead if r == 0 else pltpu.roll(lead, r, 0)
        out_ref[:, r * width : (r + 1) * width] = jnp.where(rows == r, moved, 0.0).astype(BF16)


def factor_kernel(sums_ref, cross_ref, *pieces):
    width = sums_ref.shape[1]
    half = width // 2
    height = half + 8
    group = lax.axis_index("cols")
    long = pieces[0].shape[0]
    cross_ref[:height, :] = sums_ref[:height, :]
    cross_ref[height:, :] = jnp.zeros((cross_ref.shape[0] - height, width), F32)

    def put(row, value):
        pieces[row // long][row % long : row % long + 8, :] = value

    for row in range(2 * width, len(pieces) * long, 8):
        put(row, jnp.zeros((8, width), F32))

    @pl.when(group == 1)
    def _():
        gram = unpack(sums_ref[:height, :])
        rows = [gram[8 * i : 8 * i + 8, :] for i in range(width // 8)]
        for i, row in enumerate(rows):
            put(width + 8 * i, row)
        for i, row in enumerate(lower_inverse(rows, width)):
            put(8 * i, row)

    @pl.when(group != 1)
    def _():
        for row in range(0, 2 * width, 8):
            at = row - width
            put(row, sums_ref[at : at + 8, :] if 0 <= at < half else jnp.zeros((8, width), F32))


def finish_kernel(
    rounds, nblock, phases, root, chunks, factor_ref, z_ref, lead_ref, same_ref, gathered_ref, across_ref, kept_0, kept_1,
    kept_2, swapped_0, swapped_1, swapped_2,
    coef_ref, out_ref, mine, theirs, coef, held, sems,
):
    group = lax.axis_index("cols")
    odd = group % 2 == 1
    width = z_ref.shape[1]
    half = width // 2
    height = half + 8
    own_digit, pair_digit = half_digit(phases, group % 2), half_digit(phases, 1 - group % 2)
    swapped = jnp.concatenate([swapped_0[...], swapped_1[...], swapped_2[...]], axis=0)
    kept = jnp.concatenate([kept_0[...], kept_1[...], kept_2[...]], axis=0)[:width, :]
    gram = swapped[width : 2 * width, :]
    start = gathered_ref.shape[0] - half
    pieces = ((same_ref[height:, :], gram[:half, :], 0), (gathered_ref[start:, :], across_ref[:half, :], 1))
    for own_rows, pair_rows, other in pieces:
        mine[pl.ds(pl.multiple_of((own_digit ^ other) * half, half), half), :] = own_rows
        theirs[pl.ds(pl.multiple_of((pair_digit ^ other) * half, half), half), :] = pair_rows
    own_block = mine[...]
    pair_block = jnp.where(group == 0, gram, theirs[...])
    cross = jnp.concatenate([jnp.where(odd, own_block, pair_block), jnp.where(odd, pair_block, own_block)], axis=1)
    inverse = jnp.where(odd, kept, swapped[:width, :])
    across = inverse.T
    raw = product(inverse, cross)
    for r in range(rounds):
        coef[pl.ds(r, width, stride=rounds), :] = raw[:, r * width : (r + 1) * width] * (1.0 / root)
    copies = [pltpu.make_async_copy(coef, coef_ref, sems.at[chunks])]
    copies[0].start()
    weights = product(across, raw)
    stacked = []
    for r in range(rounds):
        weight = weights[:, r * width : (r + 1) * width]
        if r == 0:
            weight = jnp.where(group == 0, -root * across, weight)
        upper = weight.astype(BF16)
        stacked.append(jnp.concatenate([upper, (weight - upper.astype(F32)).astype(BF16)], axis=1))
    weight = jnp.concatenate(stacked, axis=0)
    span = z_ref.shape[0] // chunks
    for c in range(chunks):
        block = c * nblock // chunks
        at = slice(c * span, (c + 1) * span)
        acc = jnp.dot(lead_ref[at, :], weight, preferred_element_type=F32)
        acc = (acc[:, :width] + acc[:, width:]) * tall(factor_ref[4 * block + 2], span)
        factor = tall(factor_ref[4 * block + 3], span)
        held[at, :] = (z_ref[at, :].astype(F32) * factor - acc).astype(BF16)
        copies.append(pltpu.make_async_copy(held.at[at, :], out_ref.at[at, :], sems.at[c]))
        copies[-1].start()
    for copy in copies:
        copy.wait()


def shards(snapshots, scales):
    points, _, rounds, width = snapshots.shape
    nblock = scales.shape[0]
    n_rows, n_cols = lax.axis_size("rows"), lax.axis_size("cols")
    root = math.sqrt(points * n_rows)
    long = points * rounds
    z = snapshots.reshape(long, width)
    group = lax.axis_index("cols")
    recv = partner(z, "cols", n_cols, 1)
    even = among_pairs(z, n_cols, group, 0)
    leads = (even, recv) if n_cols == 2 else (even, partner(even, "cols", n_cols, 1))
    phases = radices(n_rows)
    payload = width + 8
    params = pltpu.CompilerParams(vmem_limit_bytes=48 << 20)
    first, own, factors = pl.pallas_call(
        functools.partial(split_kernel, rounds, nblock),
        out_shape=[jax.ShapeDtypeStruct((points, width), BF16)] * 2 + [jax.ShapeDtypeStruct((4 * nblock, 8, width), F32)],
        in_specs=[pl.BlockSpec(memory_space=pltpu.HBM)] * 2,
        out_specs=[VMEM] * 3,
        scratch_shapes=[
            pltpu.VMEM(scales.shape, F32),
            pltpu.VMEM((long, width), BF16),
            pltpu.VMEM((long, width), F32),
            pltpu.SemaphoreType.DMA((nblock + 1,)),
        ],
        compiler_params=params,
        name="split",
    )(*[pltpu.with_memory_space_constraint(x, pltpu.HBM) for x in (scales, z)])
    extra = () if n_cols == 2 else leads
    sent = pl.pallas_call(
        functools.partial(products_kernel, rounds, nblock, phases),
        out_shape=[jax.ShapeDtypeStruct((payload, width), F32)] * 4,
        in_specs=[VMEM] * (4 + len(extra)),
        out_specs=[VMEM] * 4,
        scratch_shapes=[pltpu.VMEM((long, width), F32), pltpu.VMEM((2 * width, width), F32)]
        + [pltpu.VMEM((long, width), F32)] * (len(extra) // 2),
        compiler_params=params,
        name="products",
    )(factors, first, own, recv, *extra)
    sums = sent[0]
    for step, (_, base) in enumerate(phases):
        source = (sent[0], sent[1], sent[3], sent[2]) if step == 0 else [sums] * base
        others = [
            hop(source[b], n_rows, n_cols, lambda parity: b * order(phases, parity)[step][0]) for b in (range(base - 1, 0, -1) if step == 0 else range(1, base))
        ]
        if step == len(phases) - 1:
            lead = pl.pallas_call(
                functools.partial(spread_kernel, rounds),
                out_shape=jax.ShapeDtypeStruct((long, rounds * width), BF16),
                in_specs=[VMEM, VMEM],
                out_specs=VMEM,
                compiler_params=params,
                name="spread",
            )(*leads)
            *others, lead = lax.optimization_barrier((*others, lead))
        for other in others:
            sums = sums + other
    beside = lambda parity: order(phases, parity)[0][0]
    long_piece = 2 * width // 3 // 8 * 8 + 8
    gathered = hop(sums[payload - long_piece - 16 :], n_rows, n_cols, beside)
    block, *factored = pl.pallas_call(
        factor_kernel,
        out_shape=[jax.ShapeDtypeStruct((long_piece + pad, width), F32) for pad in (8, 0, 0, 0)],
        in_specs=[VMEM],
        out_specs=[VMEM] * 4,
        compiler_params=params,
        cost_estimate=pl.CostEstimate(flops=1 << 30, bytes_accessed=1 << 23, transcendentals=0),
        name="factor",
    )(sums)
    if n_cols > 2:
        joined = jnp.concatenate(factored, axis=0)
        joined = jnp.concatenate([among_pairs(joined[:width], n_cols, group, 1), joined[width:]], axis=0)
        factored = [joined[i * long_piece : (i + 1) * long_piece] for i in range(3)]
    swapped = [partner(x, "cols", n_cols, 1) for x in factored]
    crossed = hop(block, n_rows, n_cols, beside, 1)
    chunks = 2 * nblock
    coef, updated = pl.pallas_call(
        functools.partial(finish_kernel, rounds, nblock, phases, root, chunks),
        out_shape=[
            jax.ShapeDtypeStruct((width * rounds, width), F32),
            jax.ShapeDtypeStruct((long, width), BF16),
        ],
        in_specs=[VMEM] * 12,
        out_specs=[pl.BlockSpec(memory_space=pl.ANY)] * 2,
        scratch_shapes=[
            pltpu.VMEM((width, width), F32),
            pltpu.VMEM((width, width), F32),
            pltpu.VMEM((width * rounds, width), F32),
            pltpu.VMEM((long, width), BF16),
            pltpu.SemaphoreType.DMA((chunks + 1,)),
        ],
        compiler_params=params,
        name="finish",
    )(factors, z, lead, sums, gathered, crossed, *factored, *swapped)
    return coef.reshape(width, 1, rounds, width), updated.reshape(snapshots.shape)


def solution(mesh):
    return jax.shard_map(
        shards,
        mesh=mesh,
        in_specs=(P("rows", "cols", None, None), P("rows", None, None)),
        out_specs=(P(None, "cols", None, None), P("rows", "cols", None, None)),
        check_vma=False,
    )
```

```python
import functools
import math

import jax
import jax.numpy as jnp
from jax import lax
from jax.experimental import pallas as pl
from jax.experimental.pallas import tpu as pltpu
from jax.sharding import PartitionSpec as P

F32 = jnp.float32
BF16 = jnp.bfloat16
VMEM = pl.BlockSpec(memory_space=pltpu.VMEM)


def partner(x, axis, count, offset):
    return lax.ppermute(x, axis, [(i, i ^ offset) for i in range(count)])


def radices(count):
    found = []
    stride = 1
    while stride < count:
        radix = 4 if (count // stride) % 4 == 0 else 2
        found.append((stride, radix))
        stride *= radix
    return found


def order(phases, parity):
    if parity == 0 and len({radix for _, radix in phases}) == 1:
        return phases[::-1]
    return phases


def hop(x, n_rows, n_cols, offset, turn=0):
    pairs = []
    for row in range(n_rows):
        for col in range(n_cols):
            pairs.append((row * n_cols + col, (row ^ offset(col % 2)) * n_cols + (col ^ turn)))
    return lax.ppermute(x, ("rows", "cols"), pairs)


def half_digit(phases, parity):
    even, odd = [(lax.axis_index("rows") // order(phases, p)[0][0]) % 2 for p in range(2)]
    return jnp.where(parity == 0, even, odd)


def among_pairs(x, count, mine, root):
    stride = 2
    while stride < count:
        x = jnp.where(((mine ^ root) & stride) != 0, partner(x, "cols", count, stride), x)
        stride *= 2
    return x


def lanes(x, p):
    return jnp.broadcast_to(x[:, p : p + 1], x.shape)


def sublanes(x, j):
    return jnp.broadcast_to(x[j : j + 1, :], x.shape)


def thirds(x):
    high = x.astype(BF16)
    rest = x - high.astype(F32)
    middle = rest.astype(BF16)
    return high, middle, (rest - middle.astype(F32)).astype(BF16)


def product(left, right):
    return product_of_thirds(thirds(left), thirds(right))


def product_of_thirds(left, right):
    columns = right[0].shape[1]
    wide = jnp.concatenate(right[:2], axis=1)
    both = jnp.dot(
        jnp.concatenate(left[:2], axis=1), jnp.concatenate([wide, wide], axis=0), preferred_element_type=F32
    )
    small = jnp.dot(
        jnp.concatenate([left[0], left[2]], axis=1),
        jnp.concatenate([right[2], right[0]], axis=0),
        preferred_element_type=F32,
    )
    return (both[:, :columns] + both[:, columns:]) + small


def lower_inverse(rows, width):
    n = len(rows)
    rid = lax.broadcasted_iota(jnp.int32, (8, width), 0)
    cid = lax.broadcasted_iota(jnp.int32, (8, width), 1)
    done = []
    for k in range(n):
        base = 8 * k
        held = rows[k]
        columns = [lanes(held, base + j) for j in range(8)]
        inside = (cid >= base) & (cid < base + 8)
        eye = jnp.where(cid - base == rid, 1.0, 0.0).astype(F32)
        full = jnp.where(inside, eye, held)
        forward = full
        scale = jnp.zeros((8, width), F32)
        inverses = []
        for j in range(0, 8, 2):
            left, right = columns[j], columns[j + 1]
            a, b, c = sublanes(left, j), sublanes(right, j), sublanes(right, j + 1)
            det = a * c - b * b
            inverse, inverse_a = 1.0 / det, 1.0 / a
            pair = (rid == j) | (rid == j + 1)
            left, right = jnp.where(pair, 0.0, left), jnp.where(pair, 0.0, right)
            first, second = (left * c - right * b) * inverse, (right * a - left * b) * inverse
            for m in range(j + 2, 8):
                columns[m] = columns[m] - (first * sublanes(columns[m], j) + second * sublanes(columns[m], j + 1))
            full = full - (first * sublanes(full, j) + second * sublanes(full, j + 1))
            below = rid > j + 1
            first = jnp.where(below, first, jnp.where(rid == j + 1, b * inverse_a, 0.0))
            second = jnp.where(below, second, 0.0)
            forward = forward - (first * sublanes(forward, j) + second * sublanes(forward, j + 1))
            scale = jnp.where(rid == j, lax.rsqrt(a), jnp.where(rid == j + 1, lax.rsqrt(det * inverse_a), scale))
            inverses.append((a * inverse, b * inverse, c * inverse))
        done.append(jnp.where(cid <= rid + base, forward * scale, 0.0))
        if k + 1 == n:
            break
        spread = []
        for j, (a, b, c) in enumerate(inverses):
            above, under = sublanes(full, 2 * j), sublanes(full, 2 * j + 1)
            spread += [above * c - under * b, under * a - above * b]
        terms = [lanes(rows[k + 1], base + j) * spread[j] for j in range(8)]
        while len(terms) > 1:
            terms = [terms[q] + terms[q + 1] for q in range(0, len(terms), 2)]
        rows[k + 1] = jnp.where(inside, 0.0, rows[k + 1]) - terms[0]
        if k + 2 == n:
            continue
        solved = jnp.zeros((8, width), F32)
        for j in range(8):
            solved = jnp.where(rid == j, spread[j], solved)
        far = jnp.concatenate(rows[k + 2 :], axis=0)
        column = lax.broadcasted_iota(jnp.int32, far.shape, 1)
        within = (column >= base) & (column < base + 8)
        placed = []
        for third in thirds(solved):
            blocks = [jnp.zeros((base, width), F32)] if base else []
            blocks += [third.astype(F32), jnp.zeros((width - base - 8, width), F32)]
            placed.append(jnp.concatenate(blocks, axis=0).astype(BF16))
        update = product_of_thirds(thirds(jnp.where(within, far, 0.0)), placed)
        far = jnp.where(within, 0.0, far) - update
        for i in range(k + 2, n):
            rows[i] = far[8 * (i - k - 2) : 8 * (i - k - 1)]
    return done


def pack(gram):
    width = gram.shape[0]
    half = width // 2
    row = lax.broadcasted_iota(jnp.int32, (half, width), 0)
    col = lax.broadcasted_iota(jnp.int32, (half, width), 1)
    turned = pltpu.roll(gram[half:, :], half, 1)
    both = jnp.where((col < half) & (row < col), turned, gram[:half, :])
    diagonal = jnp.sum(jnp.where(row + half == col, gram[half:, :], 0.0), axis=0, keepdims=True)
    return jnp.concatenate([both, jnp.broadcast_to(diagonal, (8, width))], axis=0)


def unpack(packed):
    width = packed.shape[1]
    half = width // 2
    row = lax.broadcasted_iota(jnp.int32, (width, width), 0)
    col = lax.broadcasted_iota(jnp.int32, (width, width), 1)
    both = packed[:half, :]
    square = jnp.concatenate([both, pltpu.roll(both, half, 1)], axis=0)
    direct = ((row < half) & ((col >= half) | (col <= row))) | ((row >= half) & (col >= half) & (col > row))
    gram = jnp.where(direct, square, square.T)
    return jnp.where((row == col) & (row >= half), jnp.broadcast_to(packed[half : half + 1, :], gram.shape), gram)


def leading(even_ref, odd_ref):
    return jnp.where(lax.axis_index("cols") % 2 == 0, even_ref[...], odd_ref[...])


def tall(tile, rows):
    return jnp.broadcast_to(tile[None], (rows // 8, *tile.shape)).reshape(rows, tile.shape[1])


def split_kernel(rounds, nblock, scale_hbm, z_hbm, first_ref, own_ref, factor_ref, scale_ref, z_ref, wide, sems):
    group = lax.axis_index("cols")
    odd = group % 2
    width = z_ref.shape[1]
    span = z_ref.shape[0] // nblock
    points = span // rounds
    scale_copy = pltpu.make_async_copy(scale_hbm, scale_ref, sems.at[nblock])
    scale_copy.start()
    copies = []
    for b in range(nblock):
        at = slice(b * span, (b + 1) * span)
        copies.append(pltpu.make_async_copy(z_hbm.at[at, :], z_ref.at[at, :], sems.at[b]))
        copies[b].start()
    scale_copy.wait()
    row = lax.broadcasted_iota(jnp.int32, (8, width), 0)
    for b in range(nblock):
        lead = jnp.broadcast_to(scale_ref[b, 0:1, 0:1], (8, width))
        mine = scale_ref[b, pl.ds(group, 1), :]
        theirs = scale_ref[b, pl.ds(group + 1 - 2 * odd, 1), :]
        mine, theirs = [[jnp.broadcast_to(x[:, r : r + 1], (8, width)) for r in range(2)] for x in (mine, theirs)]
        factor_ref[4 * b] = lead * jnp.where(odd == 1, theirs[0], theirs[1])
        factor_ref[4 * b + 1] = lead * jnp.where(odd == 1, mine[0], mine[1])
        factor_ref[4 * b + 2] = lead
        factor_ref[4 * b + 3] = jnp.where(row % rounds == 0, jnp.where(group == 0, 0.0, mine[0]), mine[1])
    for b in range(nblock):
        copies[b].wait()
        at = slice(b * span, (b + 1) * span)
        wide[at, :] = z_ref[at, :].astype(F32)
        first = wide[pl.ds(b * span, points, stride=rounds), :].astype(BF16)
        last = wide[pl.ds(b * span + 1, points, stride=rounds), :].astype(BF16)
        first_ref[b * points : (b + 1) * points, :] = first
        own_ref[b * points : (b + 1) * points, :] = jnp.where(odd == 1, first, last)


def products_kernel(rounds, nblock, phases, factor_ref, first_ref, own_ref, recv_ref, *rest):
    lead_ref = () if len(rest) == 6 else (*rest[:2], rest[-1])
    same_ref, other_ref, again_ref, fourth_ref, wide, cross = rest if len(rest) == 6 else rest[2:-1]
    group = lax.axis_index("cols")
    odd = group % 2
    digit = half_digit(phases, odd)
    width = recv_ref.shape[1]
    points = own_ref.shape[0] // nblock
    half = width // 2
    height = half + 8
    wide[...] = recv_ref[...].astype(F32)
    if lead_ref:
        lead_ref[2][...] = leading(*lead_ref[:2]).astype(F32)
    out = jnp.zeros((width, 2 * width), F32)
    for b in range(nblock):
        at = slice(b * points, (b + 1) * points)
        start = b * points * rounds
        theirs = wide[pl.ds(start + 1 - odd, points, stride=rounds), :].astype(BF16)
        if lead_ref:
            panel = lead_ref[2][pl.ds(start, points, stride=rounds), :].astype(BF16)
        else:
            panel = jnp.where(odd == 1, theirs, first_ref[at, :])
        block = lax.dot_general(
            panel, jnp.concatenate([theirs, own_ref[at, :]], axis=1), (((0,), (0,)), ((), ())), preferred_element_type=F32
        )
        left = block[:, :width] * tall(factor_ref[4 * b], width)
        right = block[:, width:] * tall(factor_ref[4 * b + 1], width)
        out = out + jnp.concatenate([left, right], axis=1)
    packed = pack(out[:, :width])
    cross[:width, :] = out[:, :width]
    cross[width:, :] = out[:, width:]
    for ref, place in ((same_ref, digit), (other_ref, 1 - digit), (again_ref, 1 - digit), (fourth_ref, digit)):
        theirs = cross[pl.ds(pl.multiple_of(place * half, half), half), :]
        ref[:half, :] = jnp.where(group == 1, packed[:half, :], theirs)
        ref[half:height, :] = packed[half:, :]
        ref[height:, :] = cross[pl.ds(pl.multiple_of(width + place * half, half), half), :]


def spread_kernel(rounds, even_ref, odd_ref, out_ref):
    width = even_ref.shape[1]
    rows = lax.broadcasted_iota(jnp.int32, even_ref.shape, 0) % rounds
    lead = leading(even_ref, odd_ref).astype(F32)
    for r in range(rounds):
        moved = lead if r == 0 else pltpu.roll(lead, r, 0)
        out_ref[:, r * width : (r + 1) * width] = jnp.where(rows == r, moved, 0.0).astype(BF16)


def factor_kernel(sums_ref, cross_ref, *pieces):
    width = sums_ref.shape[1]
    half = width // 2
    height = half + 8
    group = lax.axis_index("cols")
    long = pieces[0].shape[0]
    cross_ref[:height, :] = sums_ref[:height, :]
    cross_ref[height:, :] = jnp.zeros((cross_ref.shape[0] - height, width), F32)

    def put(row, value):
        pieces[row // long][row % long : row % long + 8, :] = value

    for row in range(2 * width, len(pieces) * long, 8):
        put(row, jnp.zeros((8, width), F32))

    @pl.when(group == 1)
    def _():
        gram = unpack(sums_ref[:height, :])
        rows = [gram[8 * i : 8 * i + 8, :] for i in range(width // 8)]
        for i, row in enumerate(rows):
            put(width + 8 * i, row)
        for i, row in enumerate(lower_inverse(rows, width)):
            put(8 * i, row)

    @pl.when(group != 1)
    def _():
        for row in range(0, 2 * width, 8):
            at = row - width
            put(row, sums_ref[at : at + 8, :] if 0 <= at < half else jnp.zeros((8, width), F32))


def finish_kernel(
    rounds, nblock, phases, root, chunks, factor_ref, z_ref, lead_ref, same_ref, gathered_ref, across_ref, kept_0, kept_1,
    kept_2, swapped_0, swapped_1, swapped_2,
    coef_ref, out_ref, mine, theirs, coef, held, sems,
):
    group = lax.axis_index("cols")
    odd = group % 2 == 1
    width = z_ref.shape[1]
    half = width // 2
    height = half + 8
    own_digit, pair_digit = half_digit(phases, group % 2), half_digit(phases, 1 - group % 2)
    swapped = jnp.concatenate([swapped_0[...], swapped_1[...], swapped_2[...]], axis=0)
    kept = jnp.concatenate([kept_0[...], kept_1[...], kept_2[...]], axis=0)[:width, :]
    gram = swapped[width : 2 * width, :]
    start = gathered_ref.shape[0] - half
    pieces = ((same_ref[height:, :], gram[:half, :], 0), (gathered_ref[start:, :], across_ref[:half, :], 1))
    for own_rows, pair_rows, other in pieces:
        mine[pl.ds(pl.multiple_of((own_digit ^ other) * half, half), half), :] = own_rows
        theirs[pl.ds(pl.multiple_of((pair_digit ^ other) * half, half), half), :] = pair_rows
    own_block = mine[...]
    pair_block = jnp.where(group == 0, gram, theirs[...])
    cross = jnp.concatenate([jnp.where(odd, own_block, pair_block), jnp.where(odd, pair_block, own_block)], axis=1)
    inverse = jnp.where(odd, kept, swapped[:width, :])
    across = inverse.T
    raw = product(inverse, cross)
    for r in range(rounds):
        coef[pl.ds(r, width, stride=rounds), :] = raw[:, r * width : (r + 1) * width] * (1.0 / root)
    copies = [pltpu.make_async_copy(coef, coef_ref, sems.at[chunks])]
    copies[0].start()
    weights = product(across, raw)
    stacked = []
    for r in range(rounds):
        weight = weights[:, r * width : (r + 1) * width]
        if r == 0:
            weight = jnp.where(group == 0, -root * across, weight)
        upper = weight.astype(BF16)
        stacked.append(jnp.concatenate([upper, (weight - upper.astype(F32)).astype(BF16)], axis=1))
    weight = jnp.concatenate(stacked, axis=0)
    span = z_ref.shape[0] // chunks
    for c in range(chunks):
        block = c * nblock // chunks
        at = slice(c * span, (c + 1) * span)
        acc = jnp.dot(lead_ref[at, :], weight, preferred_element_type=F32)
        acc = (acc[:, :width] + acc[:, width:]) * tall(factor_ref[4 * block + 2], span)
        factor = tall(factor_ref[4 * block + 3], span)
        held[at, :] = (z_ref[at, :].astype(F32) * factor - acc).astype(BF16)
        copies.append(pltpu.make_async_copy(held.at[at, :], out_ref.at[at, :], sems.at[c]))
        copies[-1].start()
    for copy in copies:
        copy.wait()


def shards(snapshots, scales):
    points, _, rounds, width = snapshots.shape
    nblock = scales.shape[0]
    n_rows, n_cols = lax.axis_size("rows"), lax.axis_size("cols")
    root = math.sqrt(points * n_rows)
    long = points * rounds
    z = snapshots.reshape(long, width)
    group = lax.axis_index("cols")
    recv = partner(z, "cols", n_cols, 1)
    even = among_pairs(z, n_cols, group, 0)
    leads = (even, recv) if n_cols == 2 else (even, partner(even, "cols", n_cols, 1))
    phases = radices(n_rows)
    payload = width + 8
    params = pltpu.CompilerParams(vmem_limit_bytes=48 << 20)
    first, own, factors = pl.pallas_call(
        functools.partial(split_kernel, rounds, nblock),
        out_shape=[jax.ShapeDtypeStruct((points, width), BF16)] * 2 + [jax.ShapeDtypeStruct((4 * nblock, 8, width), F32)],
        in_specs=[pl.BlockSpec(memory_space=pltpu.HBM)] * 2,
        out_specs=[VMEM] * 3,
        scratch_shapes=[
            pltpu.VMEM(scales.shape, F32),
            pltpu.VMEM((long, width), BF16),
            pltpu.VMEM((long, width), F32),
            pltpu.SemaphoreType.DMA((nblock + 1,)),
        ],
        compiler_params=params,
        name="split",
    )(*[pltpu.with_memory_space_constraint(x, pltpu.HBM) for x in (scales, z)])
    extra = () if n_cols == 2 else leads
    sent = pl.pallas_call(
        functools.partial(products_kernel, rounds, nblock, phases),
        out_shape=[jax.ShapeDtypeStruct((payload, width), F32)] * 4,
        in_specs=[VMEM] * (4 + len(extra)),
        out_specs=[VMEM] * 4,
        scratch_shapes=[pltpu.VMEM((long, width), F32), pltpu.VMEM((2 * width, width), F32)]
        + [pltpu.VMEM((long, width), F32)] * (len(extra) // 2),
        compiler_params=params,
        name="products",
    )(factors, first, own, recv, *extra)
    sums = sent[0]
    for step, (_, base) in enumerate(phases):
        source = (sent[0], sent[1], sent[3], sent[2]) if step == 0 else [sums] * base
        others = [
            hop(source[b], n_rows, n_cols, lambda parity: b * order(phases, parity)[step][0]) for b in (range(base - 1, 0, -1) if step == 0 else range(1, base))
        ]
        if step == len(phases) - 1:
            lead = pl.pallas_call(
                functools.partial(spread_kernel, rounds),
                out_shape=jax.ShapeDtypeStruct((long, rounds * width), BF16),
                in_specs=[VMEM, VMEM],
                out_specs=VMEM,
                compiler_params=params,
                name="spread",
            )(*leads)
            *others, lead = lax.optimization_barrier((*others, lead))
        for other in others:
            sums = sums + other
    beside = lambda parity: order(phases, parity)[0][0]
    long_piece = 2 * width // 3 // 8 * 8 + 8
    gathered = hop(sums[payload - long_piece - 16 :], n_rows, n_cols, beside)
    block, *factored = pl.pallas_call(
        factor_kernel,
        out_shape=[jax.ShapeDtypeStruct((long_piece + pad, width), F32) for pad in (8, 0, 0, 0)],
        in_specs=[VMEM],
        out_specs=[VMEM] * 4,
        compiler_params=params,
        cost_estimate=pl.CostEstimate(flops=1 << 30, bytes_accessed=1 << 23, transcendentals=0),
        name="factor",
    )(sums)
    if n_cols > 2:
        joined = jnp.concatenate(factored, axis=0)
        joined = jnp.concatenate([among_pairs(joined[:width], n_cols, group, 1), joined[width:]], axis=0)
        factored = [joined[i * long_piece : (i + 1) * long_piece] for i in range(3)]
    swapped = [partner(x, "cols", n_cols, 1) for x in factored]
    crossed = hop(block, n_rows, n_cols, lambda parity: 0 if parity == 1 and n_cols == 2 else beside(parity), 1)
    chunks = 2 * nblock
    coef, updated = pl.pallas_call(
        functools.partial(finish_kernel, rounds, nblock, phases, root, chunks),
        out_shape=[
            jax.ShapeDtypeStruct((width * rounds, width), F32),
            jax.ShapeDtypeStruct((long, width), BF16),
        ],
        in_specs=[VMEM] * 12,
        out_specs=[pl.BlockSpec(memory_space=pl.ANY)] * 2,
        scratch_shapes=[
            pltpu.VMEM((width, width), F32),
            pltpu.VMEM((width, width), F32),
            pltpu.VMEM((width * rounds, width), F32),
            pltpu.VMEM((long, width), BF16),
            pltpu.SemaphoreType.DMA((chunks + 1,)),
        ],
        compiler_params=params,
        name="finish",
    )(factors, z, lead, sums, gathered, crossed, *factored, *swapped)
    return coef.reshape(width, 1, rounds, width), updated.reshape(snapshots.shape)


def solution(mesh):
    return jax.shard_map(
        shards,
        mesh=mesh,
        in_specs=(P("rows", "cols", None, None), P("rows", None, None)),
        out_specs=(P(None, "cols", None, None), P("rows", "cols", None, None)),
        check_vma=False,
    )
```

```python
import functools
import math

import jax
import jax.numpy as jnp
from jax import lax
from jax.experimental import pallas as pl
from jax.experimental.pallas import tpu as pltpu
from jax.sharding import PartitionSpec as P

F32 = jnp.float32
BF16 = jnp.bfloat16
VMEM = pl.BlockSpec(memory_space=pltpu.VMEM)


def partner(x, axis, count, offset):
    return lax.ppermute(x, axis, [(i, i ^ offset) for i in range(count)])


def radices(count):
    found = []
    stride = 1
    while stride < count:
        radix = 4 if (count // stride) % 4 == 0 else 2
        found.append((stride, radix))
        stride *= radix
    return found


def order(phases, parity):
    if parity == 0 and len({radix for _, radix in phases}) == 1:
        return phases[::-1]
    return phases


def hop(x, n_rows, n_cols, offset, turn=0):
    pairs = []
    for row in range(n_rows):
        for col in range(n_cols):
            pairs.append((row * n_cols + col, (row ^ offset(col % 2)) * n_cols + (col ^ turn)))
    return lax.ppermute(x, ("rows", "cols"), pairs)


def half_digit(phases, parity):
    even, odd = [(lax.axis_index("rows") // order(phases, p)[0][0]) % 2 for p in range(2)]
    return jnp.where(parity == 0, even, odd)


def among_pairs(x, count, mine, root):
    stride = 2
    while stride < count:
        x = jnp.where(((mine ^ root) & stride) != 0, partner(x, "cols", count, stride), x)
        stride *= 2
    return x


def lanes(x, p):
    return jnp.broadcast_to(x[:, p : p + 1], x.shape)


def sublanes(x, j):
    return jnp.broadcast_to(x[j : j + 1, :], x.shape)


def thirds(x):
    high = x.astype(BF16)
    rest = x - high.astype(F32)
    middle = rest.astype(BF16)
    return high, middle, (rest - middle.astype(F32)).astype(BF16)


def product(left, right):
    return product_of_thirds(thirds(left), thirds(right))


def product_of_thirds(left, right):
    columns = right[0].shape[1]
    wide = jnp.concatenate(right[:2], axis=1)
    both = jnp.dot(
        jnp.concatenate(left[:2], axis=1), jnp.concatenate([wide, wide], axis=0), preferred_element_type=F32
    )
    small = jnp.dot(
        jnp.concatenate([left[0], left[2]], axis=1),
        jnp.concatenate([right[2], right[0]], axis=0),
        preferred_element_type=F32,
    )
    return (both[:, :columns] + both[:, columns:]) + small


def lower_inverse(rows, width):
    n = len(rows)
    rid = lax.broadcasted_iota(jnp.int32, (8, width), 0)
    cid = lax.broadcasted_iota(jnp.int32, (8, width), 1)
    done = []
    for k in range(n):
        base = 8 * k
        held = rows[k]
        columns = [lanes(held, base + j) for j in range(8)]
        inside = (cid >= base) & (cid < base + 8)
        eye = jnp.where(cid - base == rid, 1.0, 0.0).astype(F32)
        full = jnp.where(inside, eye, held)
        forward = full
        scale = jnp.zeros((8, width), F32)
        inverses = []
        for j in range(0, 8, 2):
            left, right = columns[j], columns[j + 1]
            a, b, c = sublanes(left, j), sublanes(right, j), sublanes(right, j + 1)
            det = a * c - b * b
            inverse, inverse_a = 1.0 / det, 1.0 / a
            pair = (rid == j) | (rid == j + 1)
            left, right = jnp.where(pair, 0.0, left), jnp.where(pair, 0.0, right)
            first, second = (left * c - right * b) * inverse, (right * a - left * b) * inverse
            for m in range(j + 2, 8):
                columns[m] = columns[m] - (first * sublanes(columns[m], j) + second * sublanes(columns[m], j + 1))
            full = full - (first * sublanes(full, j) + second * sublanes(full, j + 1))
            below = rid > j + 1
            first = jnp.where(below, first, jnp.where(rid == j + 1, b * inverse_a, 0.0))
            second = jnp.where(below, second, 0.0)
            forward = forward - (first * sublanes(forward, j) + second * sublanes(forward, j + 1))
            scale = jnp.where(rid == j, lax.rsqrt(a), jnp.where(rid == j + 1, lax.rsqrt(det * inverse_a), scale))
            inverses.append((a * inverse, b * inverse, c * inverse))
        done.append(jnp.where(cid <= rid + base, forward * scale, 0.0))
        if k + 1 == n:
            break
        spread = []
        for j, (a, b, c) in enumerate(inverses):
            above, under = sublanes(full, 2 * j), sublanes(full, 2 * j + 1)
            spread += [above * c - under * b, under * a - above * b]
        terms = [lanes(rows[k + 1], base + j) * spread[j] for j in range(8)]
        while len(terms) > 1:
            terms = [terms[q] + terms[q + 1] for q in range(0, len(terms), 2)]
        rows[k + 1] = jnp.where(inside, 0.0, rows[k + 1]) - terms[0]
        if k + 2 == n:
            continue
        solved = jnp.zeros((8, width), F32)
        for j in range(8):
            solved = jnp.where(rid == j, spread[j], solved)
        far = jnp.concatenate(rows[k + 2 :], axis=0)
        column = lax.broadcasted_iota(jnp.int32, far.shape, 1)
        within = (column >= base) & (column < base + 8)
        placed = []
        for third in thirds(solved):
            blocks = [jnp.zeros((base, width), F32)] if base else []
            blocks += [third.astype(F32), jnp.zeros((width - base - 8, width), F32)]
            placed.append(jnp.concatenate(blocks, axis=0).astype(BF16))
        update = product_of_thirds(thirds(jnp.where(within, far, 0.0)), placed)
        far = jnp.where(within, 0.0, far) - update
        for i in range(k + 2, n):
            rows[i] = far[8 * (i - k - 2) : 8 * (i - k - 1)]
    return done


def pack(gram):
    width = gram.shape[0]
    half = width // 2
    row = lax.broadcasted_iota(jnp.int32, (half, width), 0)
    col = lax.broadcasted_iota(jnp.int32, (half, width), 1)
    turned = pltpu.roll(gram[half:, :], half, 1)
    both = jnp.where((col < half) & (row < col), turned, gram[:half, :])
    diagonal = jnp.sum(jnp.where(row + half == col, gram[half:, :], 0.0), axis=0, keepdims=True)
    return jnp.concatenate([both, jnp.broadcast_to(diagonal, (8, width))], axis=0)


def unpack(packed):
    width = packed.shape[1]
    half = width // 2
    row = lax.broadcasted_iota(jnp.int32, (width, width), 0)
    col = lax.broadcasted_iota(jnp.int32, (width, width), 1)
    both = packed[:half, :]
    square = jnp.concatenate([both, pltpu.roll(both, half, 1)], axis=0)
    direct = ((row < half) & ((col >= half) | (col <= row))) | ((row >= half) & (col >= half) & (col > row))
    gram = jnp.where(direct, square, square.T)
    return jnp.where((row == col) & (row >= half), jnp.broadcast_to(packed[half : half + 1, :], gram.shape), gram)


def leading(even_ref, odd_ref):
    return jnp.where(lax.axis_index("cols") % 2 == 0, even_ref[...], odd_ref[...])


def tall(tile, rows):
    return jnp.broadcast_to(tile[None], (rows // 8, *tile.shape)).reshape(rows, tile.shape[1])


def split_kernel(rounds, nblock, scale_hbm, z_hbm, first_ref, own_ref, factor_ref, scale_ref, z_ref, wide, sems):
    group = lax.axis_index("cols")
    odd = group % 2
    width = z_ref.shape[1]
    span = z_ref.shape[0] // nblock
    points = span // rounds
    scale_copy = pltpu.make_async_copy(scale_hbm, scale_ref, sems.at[nblock])
    scale_copy.start()
    copies = []
    for b in range(nblock):
        at = slice(b * span, (b + 1) * span)
        copies.append(pltpu.make_async_copy(z_hbm.at[at, :], z_ref.at[at, :], sems.at[b]))
        copies[b].start()
    scale_copy.wait()
    row = lax.broadcasted_iota(jnp.int32, (8, width), 0)
    for b in range(nblock):
        lead = jnp.broadcast_to(scale_ref[b, 0:1, 0:1], (8, width))
        mine = scale_ref[b, pl.ds(group, 1), :]
        theirs = scale_ref[b, pl.ds(group + 1 - 2 * odd, 1), :]
        mine, theirs = [[jnp.broadcast_to(x[:, r : r + 1], (8, width)) for r in range(2)] for x in (mine, theirs)]
        factor_ref[4 * b] = lead * jnp.where(odd == 1, theirs[0], theirs[1])
        factor_ref[4 * b + 1] = lead * jnp.where(odd == 1, mine[0], mine[1])
        factor_ref[4 * b + 2] = lead
        factor_ref[4 * b + 3] = jnp.where(row % rounds == 0, jnp.where(group == 0, 0.0, mine[0]), mine[1])
    for b in range(nblock):
        copies[b].wait()
        at = slice(b * span, (b + 1) * span)
        wide[at, :] = z_ref[at, :].astype(F32)
        first = wide[pl.ds(b * span, points, stride=rounds), :].astype(BF16)
        last = wide[pl.ds(b * span + 1, points, stride=rounds), :].astype(BF16)
        first_ref[b * points : (b + 1) * points, :] = first
        own_ref[b * points : (b + 1) * points, :] = jnp.where(odd == 1, first, last)


def products_kernel(rounds, nblock, phases, factor_ref, first_ref, own_ref, recv_ref, *rest):
    lead_ref = () if len(rest) == 6 else (*rest[:2], rest[-1])
    same_ref, other_ref, again_ref, fourth_ref, wide, cross = rest if len(rest) == 6 else rest[2:-1]
    group = lax.axis_index("cols")
    odd = group % 2
    digit = half_digit(phases, odd)
    width = recv_ref.shape[1]
    points = own_ref.shape[0] // nblock
    half = width // 2
    height = half + 8
    wide[...] = recv_ref[...].astype(F32)
    if lead_ref:
        lead_ref[2][...] = leading(*lead_ref[:2]).astype(F32)
    out = jnp.zeros((width, 2 * width), F32)
    for b in range(nblock):
        at = slice(b * points, (b + 1) * points)
        start = b * points * rounds
        theirs = wide[pl.ds(start + 1 - odd, points, stride=rounds), :].astype(BF16)
        if lead_ref:
            panel = lead_ref[2][pl.ds(start, points, stride=rounds), :].astype(BF16)
        else:
            panel = jnp.where(odd == 1, theirs, first_ref[at, :])
        block = lax.dot_general(
            panel, jnp.concatenate([theirs, own_ref[at, :]], axis=1), (((0,), (0,)), ((), ())), preferred_element_type=F32
        )
        left = block[:, :width] * tall(factor_ref[4 * b], width)
        right = block[:, width:] * tall(factor_ref[4 * b + 1], width)
        out = out + jnp.concatenate([left, right], axis=1)
    packed = pack(out[:, :width])
    cross[:width, :] = out[:, :width]
    cross[width:, :] = out[:, width:]
    for ref, place in ((same_ref, digit), (other_ref, 1 - digit), (again_ref, 1 - digit), (fourth_ref, digit)):
        theirs = cross[pl.ds(pl.multiple_of(place * half, half), half), :]
        ref[:half, :] = jnp.where(group == 1, packed[:half, :], theirs)
        ref[half:height, :] = packed[half:, :]
        ref[height:, :] = cross[pl.ds(pl.multiple_of(width + place * half, half), half), :]


def spread_kernel(rounds, even_ref, odd_ref, out_ref):
    width = even_ref.shape[1]
    rows = lax.broadcasted_iota(jnp.int32, even_ref.shape, 0) % rounds
    lead = leading(even_ref, odd_ref).astype(F32)
    for r in range(rounds):
        moved = lead if r == 0 else pltpu.roll(lead, r, 0)
        out_ref[:, r * width : (r + 1) * width] = jnp.where(rows == r, moved, 0.0).astype(BF16)


def factor_kernel(sums_ref, cross_ref, *pieces):
    width = sums_ref.shape[1]
    half = width // 2
    height = half + 8
    group = lax.axis_index("cols")
    long = pieces[0].shape[0]
    cross_ref[:height, :] = sums_ref[:height, :]
    cross_ref[height:, :] = jnp.zeros((cross_ref.shape[0] - height, width), F32)

    def put(row, value):
        pieces[row // long][row % long : row % long + 8, :] = value

    for row in range(2 * width, len(pieces) * long, 8):
        put(row, jnp.zeros((8, width), F32))

    @pl.when(group == 1)
    def _():
        gram = unpack(sums_ref[:height, :])
        rows = [gram[8 * i : 8 * i + 8, :] for i in range(width // 8)]
        for i, row in enumerate(rows):
            put(width + 8 * i, row)
        for i, row in enumerate(lower_inverse(rows, width)):
            put(8 * i, row)

    @pl.when(group != 1)
    def _():
        for row in range(0, 2 * width, 8):
            at = row - width
            put(row, sums_ref[at : at + 8, :] if 0 <= at < half else jnp.zeros((8, width), F32))


def finish_kernel(
    rounds, nblock, phases, root, chunks, factor_ref, z_ref, lead_ref, same_ref, gathered_ref, across_ref, kept_0, kept_1,
    kept_2, swapped_0, swapped_1, swapped_2,
    coef_ref, out_ref, mine, theirs, coef, held, sems,
):
    group = lax.axis_index("cols")
    odd = group % 2 == 1
    width = z_ref.shape[1]
    half = width // 2
    height = half + 8
    own_digit, pair_digit = half_digit(phases, group % 2), half_digit(phases, 1 - group % 2)
    swapped = jnp.concatenate([swapped_0[...], swapped_1[...], swapped_2[...]], axis=0)
    kept = jnp.concatenate([kept_0[...], kept_1[...], kept_2[...]], axis=0)[:width, :]
    gram = swapped[width : 2 * width, :]
    start = gathered_ref.shape[0] - half
    pieces = ((same_ref[height:, :], gram[:half, :], 0), (gathered_ref[start:, :], across_ref[:half, :], 1))
    for own_rows, pair_rows, other in pieces:
        mine[pl.ds(pl.multiple_of((own_digit ^ other) * half, half), half), :] = own_rows
        theirs[pl.ds(pl.multiple_of((pair_digit ^ other) * half, half), half), :] = pair_rows
    own_block = mine[...]
    pair_block = jnp.where(group == 0, gram, theirs[...])
    cross = jnp.concatenate([jnp.where(odd, own_block, pair_block), jnp.where(odd, pair_block, own_block)], axis=1)
    inverse = jnp.where(odd, kept, swapped[:width, :])
    across = inverse.T
    raw = product(inverse, cross)
    for r in range(rounds):
        coef[pl.ds(r, width, stride=rounds), :] = raw[:, r * width : (r + 1) * width] * (1.0 / root)
    copies = [pltpu.make_async_copy(coef, coef_ref, sems.at[chunks])]
    copies[0].start()
    weights = product(across, raw)
    stacked = []
    for r in range(rounds):
        weight = weights[:, r * width : (r + 1) * width]
        if r == 0:
            weight = jnp.where(group == 0, -root * across, weight)
        upper = weight.astype(BF16)
        stacked.append(jnp.concatenate([upper, (weight - upper.astype(F32)).astype(BF16)], axis=1))
    weight = jnp.concatenate(stacked, axis=0)
    span = z_ref.shape[0] // chunks
    for c in range(chunks):
        block = c * nblock // chunks
        at = slice(c * span, (c + 1) * span)
        acc = jnp.dot(lead_ref[at, :], weight, preferred_element_type=F32)
        acc = (acc[:, :width] + acc[:, width:]) * tall(factor_ref[4 * block + 2], span)
        factor = tall(factor_ref[4 * block + 3], span)
        held[at, :] = (z_ref[at, :].astype(F32) * factor - acc).astype(BF16)
        copies.append(pltpu.make_async_copy(held.at[at, :], out_ref.at[at, :], sems.at[c]))
        copies[-1].start()
    for copy in copies:
        copy.wait()


def shards(snapshots, scales):
    points, _, rounds, width = snapshots.shape
    nblock = scales.shape[0]
    n_rows, n_cols = lax.axis_size("rows"), lax.axis_size("cols")
    root = math.sqrt(points * n_rows)
    long = points * rounds
    z = snapshots.reshape(long, width)
    group = lax.axis_index("cols")
    recv = partner(z, "cols", n_cols, 1)
    even = among_pairs(z, n_cols, group, 0)
    leads = (even, recv) if n_cols == 2 else (even, partner(even, "cols", n_cols, 1))
    phases = radices(n_rows)
    payload = width + 8
    params = pltpu.CompilerParams(vmem_limit_bytes=48 << 20)
    first, own, factors = pl.pallas_call(
        functools.partial(split_kernel, rounds, nblock),
        out_shape=[jax.ShapeDtypeStruct((points, width), BF16)] * 2 + [jax.ShapeDtypeStruct((4 * nblock, 8, width), F32)],
        in_specs=[pl.BlockSpec(memory_space=pltpu.HBM)] * 2,
        out_specs=[VMEM] * 3,
        scratch_shapes=[
            pltpu.VMEM(scales.shape, F32),
            pltpu.VMEM((long, width), BF16),
            pltpu.VMEM((long, width), F32),
            pltpu.SemaphoreType.DMA((nblock + 1,)),
        ],
        compiler_params=params,
        name="split",
    )(*[pltpu.with_memory_space_constraint(x, pltpu.HBM) for x in (scales, z)])
    extra = () if n_cols == 2 else leads
    sent = pl.pallas_call(
        functools.partial(products_kernel, rounds, nblock, phases),
        out_shape=[jax.ShapeDtypeStruct((payload, width), F32)] * 4,
        in_specs=[VMEM] * (4 + len(extra)),
        out_specs=[VMEM] * 4,
        scratch_shapes=[pltpu.VMEM((long, width), F32), pltpu.VMEM((2 * width, width), F32)]
        + [pltpu.VMEM((long, width), F32)] * (len(extra) // 2),
        compiler_params=params,
        name="products",
    )(factors, first, own, recv, *extra)
    sums = sent[0]
    for step, (_, base) in enumerate(phases):
        source = (sent[0], sent[1], sent[3], sent[2]) if step == 0 else [sums] * base
        others = [
            hop(source[b], n_rows, n_cols, lambda parity: b * order(phases, parity)[step][0]) for b in (range(base - 1, 0, -1) if step == 0 else range(1, base))
        ]
        if step == len(phases) - 1:
            lead = pl.pallas_call(
                functools.partial(spread_kernel, rounds),
                out_shape=jax.ShapeDtypeStruct((long, rounds * width), BF16),
                in_specs=[VMEM, VMEM],
                out_specs=VMEM,
                compiler_params=params,
                name="spread",
            )(*leads)
            *others, lead = lax.optimization_barrier((*others, lead))
        for other in others:
            sums = sums + other
    beside = lambda parity: order(phases, parity)[0][0]
    long_piece = 2 * width // 3 // 8 * 8 + 8
    gathered = hop(sums[payload - long_piece - 16 :], n_rows, n_cols, beside)
    block, *factored = pl.pallas_call(
        factor_kernel,
        out_shape=[jax.ShapeDtypeStruct((long_piece + pad, width), F32) for pad in (8, 0, 0, 0)],
        in_specs=[VMEM],
        out_specs=[VMEM] * 4,
        compiler_params=params,
        cost_estimate=pl.CostEstimate(flops=1 << 30, bytes_accessed=1 << 23, transcendentals=0),
        name="factor",
    )(sums)
    if n_cols > 2:
        joined = jnp.concatenate(factored, axis=0)
        joined = jnp.concatenate([among_pairs(joined[:width], n_cols, group, 1), joined[width:]], axis=0)
        factored = [joined[i * long_piece : (i + 1) * long_piece] for i in range(3)]
    swapped = [partner(x, "cols", n_cols, 1) for x in factored]
    crossed = hop(block, n_rows, n_cols, lambda parity: 0 if parity == 1 and n_cols == 2 else beside(parity), 1)
    chunks = 4 * nblock
    coef, updated = pl.pallas_call(
        functools.partial(finish_kernel, rounds, nblock, phases, root, chunks),
        out_shape=[
            jax.ShapeDtypeStruct((width * rounds, width), F32),
            jax.ShapeDtypeStruct((long, width), BF16),
        ],
        in_specs=[VMEM] * 12,
        out_specs=[pl.BlockSpec(memory_space=pl.ANY)] * 2,
        scratch_shapes=[
            pltpu.VMEM((width, width), F32),
            pltpu.VMEM((width, width), F32),
            pltpu.VMEM((width * rounds, width), F32),
            pltpu.VMEM((long, width), BF16),
            pltpu.SemaphoreType.DMA((chunks + 1,)),
        ],
        compiler_params=params,
        name="finish",
    )(factors, z, lead, sums, gathered, crossed, *factored, *swapped)
    return coef.reshape(width, 1, rounds, width), updated.reshape(snapshots.shape)


def solution(mesh):
    return jax.shard_map(
        shards,
        mesh=mesh,
        in_specs=(P("rows", "cols", None, None), P("rows", None, None)),
        out_specs=(P(None, "cols", None, None), P("rows", "cols", None, None)),
        check_vma=False,
    )
```

```python
import functools
import math

import jax
import jax.numpy as jnp
from jax import lax
from jax.experimental import pallas as pl
from jax.experimental.pallas import tpu as pltpu
from jax.sharding import PartitionSpec as P

F32 = jnp.float32
BF16 = jnp.bfloat16
VMEM = pl.BlockSpec(memory_space=pltpu.VMEM)


def partner(x, axis, count, offset):
    return lax.ppermute(x, axis, [(i, i ^ offset) for i in range(count)])


def radices(count):
    found = []
    stride = 1
    while stride < count:
        radix = 4 if (count // stride) % 4 == 0 else 2
        found.append((stride, radix))
        stride *= radix
    return found


def order(phases, parity):
    if parity == 1 and len({radix for _, radix in phases}) == 1:
        return phases[::-1]
    return phases


def hop(x, n_rows, n_cols, offset, turn=0):
    pairs = []
    for row in range(n_rows):
        for col in range(n_cols):
            pairs.append((row * n_cols + col, (row ^ offset(col % 2)) * n_cols + (col ^ turn)))
    return lax.ppermute(x, ("rows", "cols"), pairs)


def half_digit(phases, parity):
    even, odd = [(lax.axis_index("rows") // order(phases, p)[0][0]) % 2 for p in range(2)]
    return jnp.where(parity == 0, even, odd)


def among_pairs(x, count, mine, root):
    stride = 2
    while stride < count:
        x = jnp.where(((mine ^ root) & stride) != 0, partner(x, "cols", count, stride), x)
        stride *= 2
    return x


def lanes(x, p):
    return jnp.broadcast_to(x[:, p : p + 1], x.shape)


def sublanes(x, j):
    return jnp.broadcast_to(x[j : j + 1, :], x.shape)


def thirds(x):
    high = x.astype(BF16)
    rest = x - high.astype(F32)
    middle = rest.astype(BF16)
    return high, middle, (rest - middle.astype(F32)).astype(BF16)


def product(left, right):
    return product_of_thirds(thirds(left), thirds(right))


def product_of_thirds(left, right):
    columns = right[0].shape[1]
    wide = jnp.concatenate(right[:2], axis=1)
    both = jnp.dot(
        jnp.concatenate(left[:2], axis=1), jnp.concatenate([wide, wide], axis=0), preferred_element_type=F32
    )
    small = jnp.dot(
        jnp.concatenate([left[0], left[2]], axis=1),
        jnp.concatenate([right[2], right[0]], axis=0),
        preferred_element_type=F32,
    )
    return (both[:, :columns] + both[:, columns:]) + small


def lower_inverse(rows, width):
    n = len(rows)
    rid = lax.broadcasted_iota(jnp.int32, (8, width), 0)
    cid = lax.broadcasted_iota(jnp.int32, (8, width), 1)
    done = []
    for k in range(n):
        base = 8 * k
        held = rows[k]
        columns = [lanes(held, base + j) for j in range(8)]
        inside = (cid >= base) & (cid < base + 8)
        eye = jnp.where(cid - base == rid, 1.0, 0.0).astype(F32)
        full = jnp.where(inside, eye, held)
        forward = full
        scale = jnp.zeros((8, width), F32)
        inverses = []
        for j in range(0, 8, 2):
            left, right = columns[j], columns[j + 1]
            a, b, c = sublanes(left, j), sublanes(right, j), sublanes(right, j + 1)
            det = a * c - b * b
            inverse, inverse_a = 1.0 / det, 1.0 / a
            pair = (rid == j) | (rid == j + 1)
            left, right = jnp.where(pair, 0.0, left), jnp.where(pair, 0.0, right)
            first, second = (left * c - right * b) * inverse, (right * a - left * b) * inverse
            for m in range(j + 2, 8):
                columns[m] = columns[m] - (first * sublanes(columns[m], j) + second * sublanes(columns[m], j + 1))
            full = full - (first * sublanes(full, j) + second * sublanes(full, j + 1))
            below = rid > j + 1
            first = jnp.where(below, first, jnp.where(rid == j + 1, b * inverse_a, 0.0))
            second = jnp.where(below, second, 0.0)
            forward = forward - (first * sublanes(forward, j) + second * sublanes(forward, j + 1))
            scale = jnp.where(rid == j, lax.rsqrt(a), jnp.where(rid == j + 1, lax.rsqrt(det * inverse_a), scale))
            inverses.append((a * inverse, b * inverse, c * inverse))
        done.append(jnp.where(cid <= rid + base, forward * scale, 0.0))
        if k + 1 == n:
            break
        spread = []
        for j, (a, b, c) in enumerate(inverses):
            above, under = sublanes(full, 2 * j), sublanes(full, 2 * j + 1)
            spread += [above * c - under * b, under * a - above * b]
        terms = [lanes(rows[k + 1], base + j) * spread[j] for j in range(8)]
        while len(terms) > 1:
            terms = [terms[q] + terms[q + 1] for q in range(0, len(terms), 2)]
        rows[k + 1] = jnp.where(inside, 0.0, rows[k + 1]) - terms[0]
        if k + 2 == n:
            continue
        solved = jnp.zeros((8, width), F32)
        for j in range(8):
            solved = jnp.where(rid == j, spread[j], solved)
        far = jnp.concatenate(rows[k + 2 :], axis=0)
        column = lax.broadcasted_iota(jnp.int32, far.shape, 1)
        within = (column >= base) & (column < base + 8)
        placed = []
        for third in thirds(solved):
            blocks = [jnp.zeros((base, width), F32)] if base else []
            blocks += [third.astype(F32), jnp.zeros((width - base - 8, width), F32)]
            placed.append(jnp.concatenate(blocks, axis=0).astype(BF16))
        update = product_of_thirds(thirds(jnp.where(within, far, 0.0)), placed)
        far = jnp.where(within, 0.0, far) - update
        for i in range(k + 2, n):
            rows[i] = far[8 * (i - k - 2) : 8 * (i - k - 1)]
    return done


def pack(gram):
    width = gram.shape[0]
    half = width // 2
    row = lax.broadcasted_iota(jnp.int32, (half, width), 0)
    col = lax.broadcasted_iota(jnp.int32, (half, width), 1)
    turned = pltpu.roll(gram[half:, :], half, 1)
    both = jnp.where((col < half) & (row < col), turned, gram[:half, :])
    diagonal = jnp.sum(jnp.where(row + half == col, gram[half:, :], 0.0), axis=0, keepdims=True)
    return jnp.concatenate([both, jnp.broadcast_to(diagonal, (8, width))], axis=0)


def unpack(packed):
    width = packed.shape[1]
    half = width // 2
    row = lax.broadcasted_iota(jnp.int32, (width, width), 0)
    col = lax.broadcasted_iota(jnp.int32, (width, width), 1)
    both = packed[:half, :]
    square = jnp.concatenate([both, pltpu.roll(both, half, 1)], axis=0)
    direct = ((row < half) & ((col >= half) | (col <= row))) | ((row >= half) & (col >= half) & (col > row))
    gram = jnp.where(direct, square, square.T)
    return jnp.where((row == col) & (row >= half), jnp.broadcast_to(packed[half : half + 1, :], gram.shape), gram)


def leading(even_ref, odd_ref):
    return jnp.where(lax.axis_index("cols") % 2 == 0, even_ref[...], odd_ref[...])


def tall(tile, rows):
    return jnp.broadcast_to(tile[None], (rows // 8, *tile.shape)).reshape(rows, tile.shape[1])


def split_kernel(rounds, nblock, scale_hbm, z_hbm, first_ref, own_ref, factor_ref, scale_ref, z_ref, wide, sems):
    group = lax.axis_index("cols")
    odd = group % 2
    width = z_ref.shape[1]
    span = z_ref.shape[0] // nblock
    points = span // rounds
    scale_copy = pltpu.make_async_copy(scale_hbm, scale_ref, sems.at[nblock])
    scale_copy.start()
    copies = []
    for b in range(nblock):
        at = slice(b * span, (b + 1) * span)
        copies.append(pltpu.make_async_copy(z_hbm.at[at, :], z_ref.at[at, :], sems.at[b]))
        copies[b].start()
    scale_copy.wait()
    row = lax.broadcasted_iota(jnp.int32, (8, width), 0)
    for b in range(nblock):
        lead = jnp.broadcast_to(scale_ref[b, 0:1, 0:1], (8, width))
        mine = scale_ref[b, pl.ds(group, 1), :]
        theirs = scale_ref[b, pl.ds(group + 1 - 2 * odd, 1), :]
        mine, theirs = [[jnp.broadcast_to(x[:, r : r + 1], (8, width)) for r in range(2)] for x in (mine, theirs)]
        factor_ref[4 * b] = lead * jnp.where(odd == 1, theirs[0], theirs[1])
        factor_ref[4 * b + 1] = lead * jnp.where(odd == 1, mine[0], mine[1])
        factor_ref[4 * b + 2] = lead
        factor_ref[4 * b + 3] = jnp.where(row % rounds == 0, jnp.where(group == 0, 0.0, mine[0]), mine[1])
    for b in range(nblock):
        copies[b].wait()
        at = slice(b * span, (b + 1) * span)
        wide[at, :] = z_ref[at, :].astype(F32)
        first = wide[pl.ds(b * span, points, stride=rounds), :].astype(BF16)
        last = wide[pl.ds(b * span + 1, points, stride=rounds), :].astype(BF16)
        first_ref[b * points : (b + 1) * points, :] = first
        own_ref[b * points : (b + 1) * points, :] = jnp.where(odd == 1, first, last)


def products_kernel(rounds, nblock, phases, factor_ref, first_ref, own_ref, recv_ref, *rest):
    lead_ref = () if len(rest) == 6 else (*rest[:2], rest[-1])
    same_ref, other_ref, again_ref, fourth_ref, wide, cross = rest if len(rest) == 6 else rest[2:-1]
    group = lax.axis_index("cols")
    odd = group % 2
    digit = half_digit(phases, odd)
    width = recv_ref.shape[1]
    points = own_ref.shape[0] // nblock
    half = width // 2
    height = half + 8
    wide[...] = recv_ref[...].astype(F32)
    if lead_ref:
        lead_ref[2][...] = leading(*lead_ref[:2]).astype(F32)
    out = jnp.zeros((width, 2 * width), F32)
    for b in range(nblock):
        at = slice(b * points, (b + 1) * points)
        start = b * points * rounds
        theirs = wide[pl.ds(start + 1 - odd, points, stride=rounds), :].astype(BF16)
        if lead_ref:
            panel = lead_ref[2][pl.ds(start, points, stride=rounds), :].astype(BF16)
        else:
            panel = jnp.where(odd == 1, theirs, first_ref[at, :])
        block = lax.dot_general(
            panel, jnp.concatenate([theirs, own_ref[at, :]], axis=1), (((0,), (0,)), ((), ())), preferred_element_type=F32
        )
        left = block[:, :width] * tall(factor_ref[4 * b], width)
        right = block[:, width:] * tall(factor_ref[4 * b + 1], width)
        out = out + jnp.concatenate([left, right], axis=1)
    packed = pack(out[:, :width])
    cross[:width, :] = out[:, :width]
    cross[width:, :] = out[:, width:]
    for ref, place in ((same_ref, digit), (other_ref, 1 - digit), (again_ref, 1 - digit), (fourth_ref, digit)):
        theirs = cross[pl.ds(pl.multiple_of(place * half, half), half), :]
        ref[:half, :] = jnp.where(group == 1, packed[:half, :], theirs)
        ref[half:height, :] = packed[half:, :]
        ref[height:, :] = cross[pl.ds(pl.multiple_of(width + place * half, half), half), :]


def spread_kernel(rounds, even_ref, odd_ref, out_ref):
    width = even_ref.shape[1]
    rows = lax.broadcasted_iota(jnp.int32, even_ref.shape, 0) % rounds
    lead = leading(even_ref, odd_ref).astype(F32)
    for r in range(rounds):
        moved = lead if r == 0 else pltpu.roll(lead, r, 0)
        out_ref[:, r * width : (r + 1) * width] = jnp.where(rows == r, moved, 0.0).astype(BF16)


def factor_kernel(sums_ref, cross_ref, *pieces):
    width = sums_ref.shape[1]
    half = width // 2
    height = half + 8
    group = lax.axis_index("cols")
    long = pieces[0].shape[0]
    cross_ref[:height, :] = sums_ref[:height, :]
    cross_ref[height:, :] = jnp.zeros((cross_ref.shape[0] - height, width), F32)

    def put(row, value):
        pieces[row // long][row % long : row % long + 8, :] = value

    for row in range(2 * width, len(pieces) * long, 8):
        put(row, jnp.zeros((8, width), F32))

    @pl.when(group == 1)
    def _():
        gram = unpack(sums_ref[:height, :])
        rows = [gram[8 * i : 8 * i + 8, :] for i in range(width // 8)]
        for i, row in enumerate(rows):
            put(width + 8 * i, row)
        for i, row in enumerate(lower_inverse(rows, width)):
            put(8 * i, row)

    @pl.when(group != 1)
    def _():
        for row in range(0, 2 * width, 8):
            at = row - width
            put(row, sums_ref[at : at + 8, :] if 0 <= at < half else jnp.zeros((8, width), F32))


def finish_kernel(
    rounds, nblock, phases, root, chunks, factor_ref, z_ref, lead_ref, same_ref, gathered_ref, across_ref, kept_0, kept_1,
    kept_2, swapped_0, swapped_1, swapped_2,
    coef_ref, out_ref, mine, theirs, coef, held, sems,
):
    group = lax.axis_index("cols")
    odd = group % 2 == 1
    width = z_ref.shape[1]
    half = width // 2
    height = half + 8
    own_digit, pair_digit = half_digit(phases, group % 2), half_digit(phases, 1 - group % 2)
    swapped = jnp.concatenate([swapped_0[...], swapped_1[...], swapped_2[...]], axis=0)
    kept = jnp.concatenate([kept_0[...], kept_1[...], kept_2[...]], axis=0)[:width, :]
    gram = swapped[width : 2 * width, :]
    start = gathered_ref.shape[0] - half
    pieces = ((same_ref[height:, :], gram[:half, :], 0), (gathered_ref[start:, :], across_ref[:half, :], 1))
    for own_rows, pair_rows, other in pieces:
        mine[pl.ds(pl.multiple_of((own_digit ^ other) * half, half), half), :] = own_rows
        theirs[pl.ds(pl.multiple_of((pair_digit ^ other) * half, half), half), :] = pair_rows
    own_block = mine[...]
    pair_block = jnp.where(group == 0, gram, theirs[...])
    cross = jnp.concatenate([jnp.where(odd, own_block, pair_block), jnp.where(odd, pair_block, own_block)], axis=1)
    inverse = jnp.where(odd, kept, swapped[:width, :])
    across = inverse.T
    raw = product(inverse, cross)
    for r in range(rounds):
        coef[pl.ds(r, width, stride=rounds), :] = raw[:, r * width : (r + 1) * width] * (1.0 / root)
    copies = [pltpu.make_async_copy(coef, coef_ref, sems.at[chunks])]
    copies[0].start()
    weights = product(across, raw)
    stacked = []
    for r in range(rounds):
        weight = weights[:, r * width : (r + 1) * width]
        if r == 0:
            weight = jnp.where(group == 0, -root * across, weight)
        upper = weight.astype(BF16)
        stacked.append(jnp.concatenate([upper, (weight - upper.astype(F32)).astype(BF16)], axis=1))
    weight = jnp.concatenate(stacked, axis=0)
    span = z_ref.shape[0] // chunks
    for c in range(chunks):
        block = c * nblock // chunks
        at = slice(c * span, (c + 1) * span)
        acc = jnp.dot(lead_ref[at, :], weight, preferred_element_type=F32)
        acc = (acc[:, :width] + acc[:, width:]) * tall(factor_ref[4 * block + 2], span)
        factor = tall(factor_ref[4 * block + 3], span)
        held[at, :] = (z_ref[at, :].astype(F32) * factor - acc).astype(BF16)
        copies.append(pltpu.make_async_copy(held.at[at, :], out_ref.at[at, :], sems.at[c]))
        copies[-1].start()
    for copy in copies:
        copy.wait()


def shards(snapshots, scales):
    points, _, rounds, width = snapshots.shape
    nblock = scales.shape[0]
    n_rows, n_cols = lax.axis_size("rows"), lax.axis_size("cols")
    root = math.sqrt(points * n_rows)
    long = points * rounds
    z = snapshots.reshape(long, width)
    group = lax.axis_index("cols")
    recv = partner(z, "cols", n_cols, 1)
    even = among_pairs(z, n_cols, group, 0)
    leads = (even, recv) if n_cols == 2 else (even, partner(even, "cols", n_cols, 1))
    phases = radices(n_rows)
    payload = width + 8
    params = pltpu.CompilerParams(vmem_limit_bytes=48 << 20)
    first, own, factors = pl.pallas_call(
        functools.partial(split_kernel, rounds, nblock),
        out_shape=[jax.ShapeDtypeStruct((points, width), BF16)] * 2 + [jax.ShapeDtypeStruct((4 * nblock, 8, width), F32)],
        in_specs=[pl.BlockSpec(memory_space=pltpu.HBM)] * 2,
        out_specs=[VMEM] * 3,
        scratch_shapes=[
            pltpu.VMEM(scales.shape, F32),
            pltpu.VMEM((long, width), BF16),
            pltpu.VMEM((long, width), F32),
            pltpu.SemaphoreType.DMA((nblock + 1,)),
        ],
        compiler_params=params,
        name="split",
    )(*[pltpu.with_memory_space_constraint(x, pltpu.HBM) for x in (scales, z)])
    extra = () if n_cols == 2 else leads
    sent = pl.pallas_call(
        functools.partial(products_kernel, rounds, nblock, phases),
        out_shape=[jax.ShapeDtypeStruct((payload, width), F32)] * 4,
        in_specs=[VMEM] * (4 + len(extra)),
        out_specs=[VMEM] * 4,
        scratch_shapes=[pltpu.VMEM((long, width), F32), pltpu.VMEM((2 * width, width), F32)]
        + [pltpu.VMEM((long, width), F32)] * (len(extra) // 2),
        compiler_params=params,
        name="products",
    )(factors, first, own, recv, *extra)
    sums = sent[0]
    for step, (_, base) in enumerate(phases):
        source = (sent[0], sent[1], sent[3], sent[2]) if step == 0 else [sums] * base
        others = [
            hop(source[b], n_rows, n_cols, lambda parity: b * order(phases, parity)[step][0]) for b in (range(base - 1, 0, -1) if step == 0 else range(1, base))
        ]
        if step == len(phases) - 1:
            lead = pl.pallas_call(
                functools.partial(spread_kernel, rounds),
                out_shape=jax.ShapeDtypeStruct((long, rounds * width), BF16),
                in_specs=[VMEM, VMEM],
                out_specs=VMEM,
                compiler_params=params,
                name="spread",
            )(*leads)
            *others, lead = lax.optimization_barrier((*others, lead))
        for other in others:
            sums = sums + other
    beside = lambda parity: order(phases, parity)[0][0]
    long_piece = 2 * width // 3 // 8 * 8 + 8
    gathered = hop(sums[payload - long_piece - 16 :], n_rows, n_cols, beside)
    block, *factored = pl.pallas_call(
        factor_kernel,
        out_shape=[jax.ShapeDtypeStruct((long_piece + pad, width), F32) for pad in (8, 0, 0, 0)],
        in_specs=[VMEM],
        out_specs=[VMEM] * 4,
        compiler_params=params,
        cost_estimate=pl.CostEstimate(flops=1 << 30, bytes_accessed=1 << 23, transcendentals=0),
        name="factor",
    )(sums)
    if n_cols > 2:
        joined = jnp.concatenate(factored, axis=0)
        joined = jnp.concatenate([among_pairs(joined[:width], n_cols, group, 1), joined[width:]], axis=0)
        factored = [joined[i * long_piece : (i + 1) * long_piece] for i in range(3)]
    swapped = [partner(x, "cols", n_cols, 1) for x in factored]
    crossed = hop(block, n_rows, n_cols, lambda parity: 0 if parity == 1 and n_cols == 2 else beside(parity), 1)
    chunks = 2 * nblock
    coef, updated = pl.pallas_call(
        functools.partial(finish_kernel, rounds, nblock, phases, root, chunks),
        out_shape=[
            jax.ShapeDtypeStruct((width * rounds, width), F32),
            jax.ShapeDtypeStruct((long, width), BF16),
        ],
        in_specs=[VMEM] * 12,
        out_specs=[pl.BlockSpec(memory_space=pl.ANY)] * 2,
        scratch_shapes=[
            pltpu.VMEM((width, width), F32),
            pltpu.VMEM((width, width), F32),
            pltpu.VMEM((width * rounds, width), F32),
            pltpu.VMEM((long, width), BF16),
            pltpu.SemaphoreType.DMA((chunks + 1,)),
        ],
        compiler_params=params,
        name="finish",
    )(factors, z, lead, sums, gathered, crossed, *factored, *swapped)
    return coef.reshape(width, 1, rounds, width), updated.reshape(snapshots.shape)


def solution(mesh):
    return jax.shard_map(
        shards,
        mesh=mesh,
        in_specs=(P("rows", "cols", None, None), P("rows", None, None)),
        out_specs=(P(None, "cols", None, None), P("rows", "cols", None, None)),
        check_vma=False,
    )
```
